128 devices in a mesh: row: 8 (over z, core), col: 16 (over y, x).
Axes of the slice: x: 4, y: 4, z: 4, core: 2. Of those that a mesh axis runs over, the one named last changes fastest.
Arguments:
- hidden: bfloat16 [1408, 16384], P('col', 'row'), may hold values from -18 to 18
- gain_in: bfloat16 [1408], replicated, may hold values from 0.5 to 1.5
- w_query: bfloat16 [1408, 1408], P('col'), may hold values from -0.3125 to 0.3125
- w_pair: bfloat16 [2, 1408, 1408], P(None, 'col'), may hold values from -0.15625 to 0.15625
- kv_cache: bfloat16 [2, 1408, 16384], P(None, 'col', 'row'), may hold values from -103 to 103
- recompute_rows: int32 [8, 200], P('row'), may hold values from 0 to 2047, as said below
- segment_ids: int32 [16384], P('row'), may hold values from -1 to 1, as said below
- w_out: bfloat16 [1408, 1408], P('col'), may hold values from -0.3125 to 0.3125
- gain_merge: bfloat16 [1408], replicated, may hold values from 0.5 to 1.5
- w_merge: bfloat16 [4, 1408, 1408], P(None, 'col'), may hold values from -0.078125 to 0.078125
- requests: int32 [8, 16, 85], P('row'), may hold values from -1 to 511, as said below
Outputs:
- delivered: bfloat16 [8, 16, 85, 1408], P('row', 'col')
The draws below stay inside these ranges and needn't reach their ends.
Inputs may be any that keep to these rules, and one draw needn't show every extreme that they name: `segment_ids`: ids do not fall along the tokens except to -1 for the padding at the end; every image covers a multiple of 4 tokens and starts at a multiple of 4. `recompute_rows`: the 200 offsets of one index of row are distinct. `requests`: for each index of row, the lists of all owners together name each of its 512 merged tokens exactly once; unused slots hold -1 and follow the used ones.
All inputs are finite; a program needn't handle non-finite values.
Results may differ from the reference program's by a relative error of at most 0.025.
The reference program's roundings to bfloat16 on the way (of `normed`, `queries`, `fresh_pairs`, `keys_values`, `weights_exp`, `attended` and `merger_in`) count: a program that leaves them out, or rounds other values in their place, can miss the bound.
Values may be sent and summed in bfloat16 or wider, within the bound.
A program may use at most 128 MiB of HBM per device.

```python
import jax
import jax.numpy as jnp
from jax import lax

HEADS = 16
HD = 88
D = 1408
TOK_DEV = 2048
TOKENS = 16384
MERGED_DEV = 512
RECOMP_DEV = 200
REQ = 85
N_ROW = 8
N_COL = 16


def draw_hidden(key, part):
    feature = jnp.arange(D, dtype=jnp.float32) / D
    feature_scale = 0.3 * 10.0 ** feature
    drawn = jnp.clip(jax.random.normal(jax.random.fold_in(key, 21), (D, TOKENS), jnp.float32), -6.0, 6.0)
    return (drawn * feature_scale[:, None]).astype(jnp.bfloat16)


def draw_kv_cache(key, part):
    array_shape = (2, D, TOKENS)
    drawn = jnp.clip(jax.random.normal(jax.random.fold_in(key, 31), array_shape, jnp.float32), -6.0, 6.0)
    return drawn.astype(jnp.bfloat16)


def draw_segment_ids(key, part):
    quads = TOKENS // 4
    first_quads = jax.random.randint(jax.random.fold_in(key, 13), (), 9 * quads // 16, 3 * quads // 4 + 1)
    second_quads = jax.random.randint(jax.random.fold_in(key, 16), (), quads // 8, 7 * quads // 32 + 1)
    first_end = 4 * first_quads
    second_end = first_end + 4 * second_quads
    position = jnp.arange(TOKENS, dtype=jnp.int32)
    image_ids = jnp.where(position < first_end, 0, jnp.where(position < second_end, 1, -1))
    return image_ids.astype(jnp.int32)


def recompute_block(block_key):
    return jax.random.permutation(block_key, TOK_DEV)[:RECOMP_DEV].astype(jnp.int32)


def draw_recompute_rows(key, part):
    key_list = jax.random.split(jax.random.fold_in(key, 14), N_ROW)
    return jax.vmap(recompute_block)(key_list).astype(jnp.int32)


def request_block(block_key):
    shuffled = jax.random.permutation(block_key, MERGED_DEV).astype(jnp.int32)
    busiest = jax.random.randint(jax.random.fold_in(block_key, 1), (), 0, N_COL)
    owners = jnp.arange(N_COL, dtype=jnp.int32)
    other_rank = jnp.where(owners < busiest, owners, owners - 1)
    remaining = MERGED_DEV - REQ
    share_base = remaining // (N_COL - 1)
    share_extra = remaining % (N_COL - 1)
    counts = jnp.where(owners == busiest, REQ, share_base + (other_rank < share_extra).astype(jnp.int32))
    starts = jnp.where(owners == busiest, 0, REQ + other_rank * share_base + jnp.minimum(other_rank, share_extra))
    slot_index = jnp.arange(REQ, dtype=jnp.int32)
    position = jnp.clip(starts[:, None] + slot_index[None, :], 0, MERGED_DEV - 1)
    picked = shuffled[position]
    return jnp.where(slot_index[None, :] < counts[:, None], picked, -1).astype(jnp.int32)


def draw_requests(key, part):
    key_list = jax.random.split(jax.random.fold_in(key, 15), N_ROW)
    return jax.vmap(request_block)(key_list).astype(jnp.int32)


def shard_levels(own_key, dims, pieces, least, high):
    factor_of, own = 1.0, jax.random.fold_in(own_key, 6)
    for dim, parts in pieces:
        steps = jnp.exp(jax.random.uniform(jax.random.fold_in(own, dim), (parts,), jnp.float32, least / len(pieces), high / len(pieces)))
        factor_of = factor_of * jnp.repeat(steps, dims[dim] // parts).reshape([-1 if axis == dim else 1 for axis in range(len(dims))])
    return factor_of


def gaussian(key, shape, scale, most, shards=(), kind=jnp.bfloat16):
    values = scale * jax.random.normal(key, shape, jnp.float32)
    if shards:
        values = values * shard_levels(key, shape, shards, -0.22, 0.18)
    return jnp.clip(values, -most, most).astype(kind)


def setup_inputs(seed: int = 0) -> dict:
    splits = jax.random.split(jax.random.key(seed), 12)
    return {
        "hidden": draw_hidden(jax.random.fold_in(splits[11], 71), 0),
        "gain_in": jnp.clip(1.0 + 0.1 * jax.random.normal(splits[1], (D,), jnp.float32), 0.5, 1.5).astype(jnp.bfloat16),
        "w_query": gaussian(splits[2], (D, D), (D // 4) ** -0.5, 0.3125, ((0, 16),)),
        "w_pair": gaussian(splits[3], (2, D, D), D ** -0.5, 0.15625, ((1, 16),)),
        "kv_cache": draw_kv_cache(jax.random.fold_in(splits[11], 71), 0),
        "recompute_rows": draw_recompute_rows(jax.random.fold_in(splits[11], 71), 0),
        "segment_ids": draw_segment_ids(jax.random.fold_in(splits[11], 71), 0),
        "w_out": gaussian(splits[7], (D, D), (4 * HD) ** -0.5, 0.3125, ((0, 16),)),
        "gain_merge": jnp.clip(1.0 + 0.1 * jax.random.normal(splits[8], (D,), jnp.float32), 0.5, 1.5).astype(jnp.bfloat16),
        "w_merge": gaussian(splits[9], (4, D, D), (4 * D) ** -0.5, 0.078125, ((1, 16),)),
        "requests": draw_requests(jax.random.fold_in(splits[11], 71), 0),
    }


EPSILON = 1e-06
MASKED = -1e+30

def layer_norm(inputs, gain_vector):
    model_width = inputs.shape[-1]
    row_mean = lax.optimization_barrier(jnp.sum(inputs, axis=-1, keepdims=True)) / model_width
    row_square = lax.optimization_barrier(jnp.sum(inputs * inputs, axis=-1, keepdims=True)) / model_width
    return (inputs - row_mean) * lax.rsqrt(row_square - row_mean * row_mean + EPSILON) * gain_vector

def reference(hidden, gain_in, w_query, w_pair, kv_cache, recompute_rows, segment_ids, w_out, gain_merge, w_merge, requests):
    token_major = hidden.T.astype(jnp.float32)
    normed = layer_norm(token_major, gain_in.astype(jnp.float32)).astype(jnp.bfloat16)
    queries = jnp.dot(normed, w_query.T, preferred_element_type=jnp.float32).astype(jnp.bfloat16)
    block_base = (jnp.arange(N_ROW, dtype=jnp.int32) * TOK_DEV)[:, None]
    picked_rows = (recompute_rows + block_base).reshape(-1).astype(jnp.int32)
    fresh_pairs = jnp.dot(normed[picked_rows], w_pair.reshape(2 * D, D).T, preferred_element_type=jnp.float32)
    fresh_pairs = fresh_pairs.astype(jnp.bfloat16).reshape(-1, 2, D).transpose(1, 2, 0)
    keys_values = kv_cache.at[:, :, picked_rows].set(fresh_pairs)
    score_scale = HD ** (-0.5)
    query_heads = queries.reshape(TOKENS, HEADS, HD).transpose(1, 0, 2)
    key_heads = keys_values[0].T.reshape(TOKENS, HEADS, HD).transpose(1, 0, 2)
    value_heads = keys_values[1].T.reshape(TOKENS, HEADS, HD).transpose(1, 0, 2)
    segment_blocks = segment_ids.reshape(N_ROW, TOK_DEV)

    def head_attention(operands):
        query_head, key_head, value_head = operands

        def query_block(paired):
            query_rows, segment_rows = paired
            scores = jnp.dot(query_rows, key_head.T, preferred_element_type=jnp.float32) * score_scale
            allowed = segment_rows[:, None] == segment_ids[None, :]
            row_max = lax.optimization_barrier(jnp.max(jnp.where(allowed, scores, MASKED), axis=1, keepdims=True))
            weights_exp = jnp.where(allowed, jnp.exp(scores - row_max), 0.0)
            row_total = lax.optimization_barrier(jnp.sum(weights_exp, axis=1, keepdims=True))
            mixed = jnp.dot(weights_exp.astype(jnp.bfloat16), value_head, preferred_element_type=jnp.float32)
            return (mixed / row_total).astype(jnp.bfloat16)
        return lax.map(query_block, (query_head.reshape(N_ROW, TOK_DEV, HD), segment_blocks))
    attended = lax.map(head_attention, (query_heads, key_heads, value_heads))
    attended = attended.reshape(HEADS, TOKENS, HD).transpose(1, 0, 2).reshape(TOKENS, D)
    updated = token_major + jnp.dot(attended, w_out, preferred_element_type=jnp.float32)
    merger_in = layer_norm(updated, gain_merge.astype(jnp.float32)).astype(jnp.bfloat16)
    grouped = merger_in.reshape(TOKENS // 4, 4 * D)
    merged = jnp.dot(grouped, w_merge.reshape(4 * D, D), preferred_element_type=jnp.float32)
    merged_base = (jnp.arange(N_ROW, dtype=jnp.int32) * MERGED_DEV)[:, None, None]
    is_valid = requests >= 0
    safe_index = jnp.where(is_valid, requests + merged_base, 0).astype(jnp.int32)
    picked = merged[safe_index]
    delivered = jnp.where(is_valid[..., None], picked, 0.0).astype(jnp.bfloat16)
    return delivered
```

```python
import jax
import jax.numpy as jnp
from jax import lax
from jax.sharding import PartitionSpec as P

HD = 88


EPSILON = 1e-06
MASKED = -1e30
KEY_BLOCK = 1024


def on_device(
    hidden,
    gain_in,
    w_query,
    w_pair,
    kv_cache,
    recompute_rows,
    segment_ids,
    w_out,
    gain_merge,
    w_merge,
    requests,
):
    local_width, tok_rows = hidden.shape
    model_width = w_query.shape[1]
    n_col = model_width // local_width
    heads_here = local_width // HD
    score_scale = HD ** (-0.5)
    col_index = lax.axis_index("col")
    full_rows = lax.all_gather(hidden, "col", axis=0, tiled=True)
    out_weight = lax.all_gather(w_out, "col", axis=0, tiled=True)
    full_float = full_rows.astype(jnp.float32)
    in_mean = jnp.sum(full_float, axis=0, keepdims=True) / model_width
    in_square = jnp.sum(full_float * full_float, axis=0, keepdims=True) / model_width
    normed = (
        (full_float - in_mean)
        * lax.rsqrt(in_square - in_mean * in_mean + EPSILON)
        * gain_in.astype(jnp.float32)[:, None]
    ).astype(jnp.bfloat16)
    queries = jnp.dot(w_query, normed, preferred_element_type=jnp.float32).astype(jnp.bfloat16)
    picked_rows = recompute_rows[0]
    normed_picked = jnp.take(normed, picked_rows, axis=1)
    fresh_pairs = jnp.dot(
        w_pair.reshape(2 * local_width, model_width),
        normed_picked,
        preferred_element_type=jnp.float32,
    )
    fresh_pairs = fresh_pairs.astype(jnp.bfloat16).reshape(2, local_width, -1)
    keys_values = kv_cache.at[:, :, picked_rows].set(fresh_pairs)
    query_heads = queries.reshape(heads_here, HD, tok_rows)

    pair_local = jnp.concatenate(
        [keys_values.reshape(2 * local_width, tok_rows), segment_ids.astype(jnp.bfloat16)[None, :]],
        axis=0,
    )
    pair_all = lax.all_gather(pair_local, "row", axis=1, tiled=True)
    pair_rows = pair_all[: 2 * local_width].reshape(2, local_width, -1)
    segment_line = pair_all[2 * local_width].astype(jnp.int32)

    def take_block(carried, pair_block, segment_block):
        running_max, running_sum, weighted = carried
        key_block = pair_block[0].reshape(heads_here, HD, -1)
        value_block = pair_block[1].reshape(heads_here, HD, -1)
        scores = (
            jnp.einsum("hdq,hdk->hqk", query_heads, key_block, preferred_element_type=jnp.float32)
            * score_scale
        )
        allowed = (segment_ids[:, None] == segment_block[None, :])[None, :, :]
        new_max = jnp.maximum(running_max, jnp.max(jnp.where(allowed, scores, MASKED), axis=2))
        weights_exp = jnp.where(allowed, jnp.exp(scores - new_max[:, :, None]), 0.0)
        factor = jnp.exp(running_max - new_max)
        running_sum = running_sum * factor + jnp.sum(weights_exp, axis=2)
        product = jnp.einsum(
            "hqk,hdk->hdq",
            weights_exp.astype(jnp.bfloat16),
            value_block,
            preferred_element_type=jnp.float32,
        )
        weighted = weighted * factor[:, None, :] + product
        return (new_max, running_sum, weighted)

    starting = (
        jnp.full((heads_here, tok_rows), MASKED, jnp.float32),
        jnp.zeros((heads_here, tok_rows), jnp.float32),
        jnp.zeros((heads_here, HD, tok_rows), jnp.float32),
    )
    piece_rows = pair_rows.shape[2]
    whole_blocks = piece_rows // KEY_BLOCK

    def loop_body(block_index, loop_state):
        pair_block = lax.dynamic_slice_in_dim(pair_rows, block_index * KEY_BLOCK, KEY_BLOCK, 2)
        segment_block = lax.dynamic_slice_in_dim(
            segment_line, block_index * KEY_BLOCK, KEY_BLOCK, 0
        )
        return take_block(loop_state, pair_block, segment_block)

    running_max, running_sum, weighted = lax.fori_loop(0, whole_blocks, loop_body, starting)
    attended = (
        (weighted / running_sum[:, None, :]).astype(jnp.bfloat16).reshape(local_width, tok_rows)
    )
    chunk = tok_rows // n_col
    attended_chunk = lax.all_to_all(attended, "col", 1, 0, tiled=True)
    x_chunk = lax.dynamic_slice_in_dim(full_float, col_index * chunk, chunk, 1)
    projected = lax.dot_general(
        out_weight, attended_chunk, (((0,), (0,)), ((), ())), preferred_element_type=jnp.float32
    )
    updated = x_chunk + projected
    row_mean = jnp.sum(updated, axis=0, keepdims=True) / model_width
    row_square = jnp.sum(updated * updated, axis=0, keepdims=True) / model_width
    merger_chunk = (
        (updated - row_mean)
        * lax.rsqrt(row_square - row_mean * row_mean + EPSILON)
        * gain_merge.astype(jnp.float32)[:, None]
    ).astype(jnp.bfloat16)
    merger_in = lax.all_to_all(merger_chunk, "col", 0, 1, tiled=True)
    merged_rows = tok_rows // 4
    grouped = merger_in.reshape(local_width, merged_rows, 4)
    merged = jnp.einsum("cgi,icd->gd", grouped, w_merge, preferred_element_type=jnp.float32)
    merged_sum = lax.psum(merged.astype(jnp.bfloat16), "col")
    wanted_rows = lax.dynamic_index_in_dim(requests[0], col_index, 0, keepdims=False)
    is_valid = wanted_rows >= 0
    safe_index = jnp.where(is_valid, wanted_rows, 0)
    picked = jnp.where(is_valid[:, None], merged_sum[safe_index], jnp.zeros((), jnp.bfloat16))
    return picked.reshape(1, 1, picked.shape[0], model_width)


def solution(mesh):
    placed = (
        P("col", "row"),
        P(),
        P("col", None),
        P(None, "col", None),
        P(None, "col", "row"),
        P("row", None),
        P("row"),
        P("col", None),
        P(),
        P(None, "col", None),
        P("row", None, None),
    )
    return jax.shard_map(
        on_device,
        mesh=mesh,
        in_specs=placed,
        out_specs=P("row", "col", None, None),
        check_vma=False,
    )
```

```python
import jax
import jax.numpy as jnp
from jax import lax
from jax.sharding import PartitionSpec as P

HD = 88


EPSILON = 1e-06
MASKED = -1e30
KEY_BLOCK = 1024


def on_device(
    hidden,
    gain_in,
    w_query,
    w_pair,
    kv_cache,
    recompute_rows,
    segment_ids,
    w_out,
    gain_merge,
    w_merge,
    requests,
):
    local_width, tok_rows = hidden.shape
    model_width = w_query.shape[1]
    n_col = model_width // local_width
    heads_here = local_width // HD
    score_scale = HD ** (-0.5)
    col_index = lax.axis_index("col")
    full_rows = lax.all_gather(hidden, "col", axis=0, tiled=True)
    out_weight = lax.all_gather(w_out, "col", axis=0, tiled=True)
    full_float = full_rows.astype(jnp.float32)
    in_mean = jnp.sum(full_float, axis=0, keepdims=True) / model_width
    in_square = jnp.sum(full_float * full_float, axis=0, keepdims=True) / model_width
    normed = (
        (full_float - in_mean)
        * lax.rsqrt(in_square - in_mean * in_mean + EPSILON)
        * gain_in.astype(jnp.float32)[:, None]
    ).astype(jnp.bfloat16)
    queries = jnp.dot(w_query, normed, preferred_element_type=jnp.float32).astype(jnp.bfloat16)
    picked_rows = recompute_rows[0]
    normed_picked = jnp.take(normed, picked_rows, axis=1)
    fresh_pairs = jnp.dot(
        w_pair.reshape(2 * local_width, model_width),
        normed_picked,
        preferred_element_type=jnp.float32,
    )
    fresh_pairs = fresh_pairs.astype(jnp.bfloat16).reshape(2, local_width, -1)
    keys_values = kv_cache.at[:, :, picked_rows].set(fresh_pairs)
    query_heads = queries.reshape(heads_here, HD, tok_rows)

    pair_local = jnp.concatenate(
        [keys_values.reshape(2 * local_width, tok_rows), segment_ids.astype(jnp.bfloat16)[None, :]],
        axis=0,
    )
    pair_all = lax.all_gather(pair_local, "row", axis=1, tiled=True)
    pair_rows = pair_all[: 2 * local_width].reshape(2, local_width, -1)
    segment_line = pair_all[2 * local_width].astype(jnp.int32)

    def take_block(carried, pair_block, segment_block):
        running_max, running_sum, weighted = carried
        key_block = pair_block[0].reshape(heads_here, HD, -1)
        value_block = pair_block[1].reshape(heads_here, HD, -1)
        scores = (
            jnp.einsum("hdq,hdk->hqk", query_heads, key_block, preferred_element_type=jnp.float32)
            * score_scale
        )
        allowed = (segment_ids[:, None] == segment_block[None, :])[None, :, :]
        new_max = jnp.maximum(running_max, jnp.max(jnp.where(allowed, scores, MASKED), axis=2))
        weights_exp = jnp.where(allowed, jnp.exp(scores - new_max[:, :, None]), 0.0)
        factor = jnp.exp(running_max - new_max)
        running_sum = running_sum * factor + jnp.sum(weights_exp, axis=2)
        product = jnp.einsum(
            "hqk,hdk->hdq",
            weights_exp.astype(jnp.bfloat16),
            value_block,
            preferred_element_type=jnp.float32,
        )
        weighted = weighted * factor[:, None, :] + product
        return (new_max, running_sum, weighted)

    starting = (
        jnp.full((heads_here, tok_rows), MASKED, jnp.float32),
        jnp.zeros((heads_here, tok_rows), jnp.float32),
        jnp.zeros((heads_here, HD, tok_rows), jnp.float32),
    )
    piece_rows = pair_rows.shape[2]
    whole_blocks = piece_rows // KEY_BLOCK

    def loop_body(block_index, loop_state):
        pair_block = lax.dynamic_slice_in_dim(pair_rows, block_index * KEY_BLOCK, KEY_BLOCK, 2)
        segment_block = lax.dynamic_slice_in_dim(
            segment_line, block_index * KEY_BLOCK, KEY_BLOCK, 0
        )
        return take_block(loop_state, pair_block, segment_block)

    running_max, running_sum, weighted = lax.fori_loop(0, whole_blocks, loop_body, starting)
    attended = (
        (weighted / running_sum[:, None, :]).astype(jnp.bfloat16).reshape(local_width, tok_rows)
    )
    chunk = tok_rows // n_col
    attended_chunk = lax.all_to_all(attended, "col", 1, 0, tiled=True)
    x_chunk = lax.dynamic_slice_in_dim(full_float, col_index * chunk, chunk, 1)
    projected = lax.dot_general(
        out_weight, attended_chunk, (((0,), (0,)), ((), ())), preferred_element_type=jnp.float32
    )
    updated = x_chunk + projected
    row_mean = jnp.sum(updated, axis=0, keepdims=True) / model_width
    row_square = jnp.sum(updated * updated, axis=0, keepdims=True) / model_width
    merger_chunk = (
        (updated - row_mean)
        * lax.rsqrt(row_square - row_mean * row_mean + EPSILON)
        * gain_merge.astype(jnp.float32)[:, None]
    ).astype(jnp.bfloat16)
    merge_weight, _ = lax.optimization_barrier((w_merge, pair_all))
    merge_full = lax.all_gather(merge_weight, "col", axis=1, tiled=True)
    grouped = merger_chunk.reshape(model_width, chunk // 4, 4)
    merged_here = jnp.einsum("fgi,ifd->gd", grouped, merge_full, preferred_element_type=jnp.float32)
    merged_all = lax.all_gather(merged_here.astype(jnp.bfloat16), "col", axis=0, tiled=True)
    wanted_rows = lax.dynamic_index_in_dim(requests[0], col_index, 0, keepdims=False)
    is_valid = wanted_rows >= 0
    safe_index = jnp.where(is_valid, wanted_rows, 0)
    picked = jnp.where(is_valid[:, None], merged_all[safe_index], jnp.zeros((), jnp.bfloat16))
    return picked.reshape(1, 1, picked.shape[0], model_width)


def solution(mesh):
    placed = (
        P("col", "row"),
        P(),
        P("col", None),
        P(None, "col", None),
        P(None, "col", "row"),
        P("row", None),
        P("row"),
        P("col", None),
        P(),
        P(None, "col", None),
        P("row", None, None),
    )
    return jax.shard_map(
        on_device,
        mesh=mesh,
        in_specs=placed,
        out_specs=P("row", "col", None, None),
        check_vma=False,
    )
```

```python
import jax
import jax.numpy as jnp
from jax import lax
import functools
from jax.experimental import pallas as pl
from jax.experimental.pallas import tpu as pltpu
from jax.sharding import PartitionSpec as P

HD = 88


EPSILON = 1e-06
MASKED = -1e30
PADW = 96
Q_BLOCK = 512
K_BLOCK = 1024


def _attn_kernel(kb_map, flags, q_ref, qs_ref, k_ref, v_ref, o_ref, m_ref, l_ref, acc_ref, *, scale, n_steps):
    qb = pl.program_id(0)
    j = pl.program_id(1)
    flag = flags[qb, j]

    @pl.when(j == 0)
    def _():
        m_ref[...] = jnp.full(m_ref.shape, MASKED, jnp.float32)
        l_ref[...] = jnp.zeros(l_ref.shape, jnp.float32)
        acc_ref[...] = jnp.zeros(acc_ref.shape, jnp.float32)

    def step(masked):
        q = q_ref[...]
        k = k_ref[...]
        s = jnp.dot(q, k, preferred_element_type=jnp.float32) * scale
        if masked:
            key_seg = k[HD:HD + 1, :].astype(jnp.float32)
            s = jnp.where(qs_ref[...] == key_seg, s, MASKED)
        m_prev = m_ref[...]
        m_new = jnp.maximum(m_prev, jnp.max(s, axis=1, keepdims=True))
        p = jnp.exp(s - m_new)
        alpha = jnp.exp(m_prev - m_new)
        l_ref[...] = alpha * l_ref[...] + jnp.sum(p, axis=1, keepdims=True)
        pv = lax.dot_general(
            p.astype(jnp.bfloat16), v_ref[...], (((1,), (1,)), ((), ())),
            preferred_element_type=jnp.float32,
        )
        acc_ref[...] = alpha * acc_ref[...] + pv
        m_ref[...] = m_new

    @pl.when(flag == 1)
    def _():
        step(True)

    @pl.when(flag == 2)
    def _():
        step(False)

    @pl.when(j == n_steps - 1)
    def _():
        o_ref[...] = (acc_ref[...] / l_ref[...]).astype(o_ref.dtype)


def block_tables(q_seg, k_seg, q_start):
    n_q = q_seg.shape[0] // Q_BLOCK
    n_k = k_seg.shape[0] // K_BLOCK
    values = jnp.arange(-1, 2, dtype=jnp.int32)
    q_has = jnp.any(q_seg.reshape(n_q, Q_BLOCK, 1) == values, axis=1).astype(jnp.float32)
    k_has = jnp.any(k_seg.reshape(n_k, K_BLOCK, 1) == values, axis=1).astype(jnp.float32)
    shared = jnp.dot(q_has, k_has.T) > 0
    single = (jnp.sum(q_has, axis=1)[:, None] == 1) & (jnp.sum(k_has, axis=1)[None, :] == 1)
    diag = (q_start + jnp.arange(n_q, dtype=jnp.int32) * Q_BLOCK) // K_BLOCK
    order = (diag[:, None] + jnp.arange(n_k, dtype=jnp.int32)[None, :]) % n_k
    need = jnp.take_along_axis(shared, order, axis=1)
    full = jnp.take_along_axis(single, order, axis=1)
    rank = jnp.cumsum(need.astype(jnp.int32), axis=1) - 1
    count = jnp.sum(need.astype(jnp.int32), axis=1)
    pos = jnp.where(need, rank, n_k + jnp.arange(n_k)[None, :])
    perm = jnp.argsort(pos, axis=1)
    kb_sorted = jnp.take_along_axis(order, perm, axis=1)
    full_sorted = jnp.take_along_axis(full, perm, axis=1)
    step = jnp.arange(n_k, dtype=jnp.int32)[None, :]
    live = step < count[:, None]
    last = jnp.take_along_axis(kb_sorted, (count - 1)[:, None], axis=1)
    kb_map = jnp.where(live, kb_sorted, last).astype(jnp.int32)
    flags = jnp.where(live, jnp.where(full_sorted, 2, 1), 0).astype(jnp.int32)
    return kb_map, flags


def attention(q_t, q_seg_f, kv, kb_map, flags, scale, interpret=False):
    n_tok = q_t.shape[0]
    n_keys = kv.shape[2]
    n_q = n_tok // Q_BLOCK
    n_k = n_keys // K_BLOCK
    kernel = functools.partial(_attn_kernel, scale=scale, n_steps=n_k)
    grid_spec = pltpu.PrefetchScalarGridSpec(
        num_scalar_prefetch=2,
        grid=(n_q, n_k),
        in_specs=[
            pl.BlockSpec((Q_BLOCK, PADW), lambda i, j, km, fl: (i, 0)),
            pl.BlockSpec((Q_BLOCK, 1), lambda i, j, km, fl: (i, 0)),
            pl.BlockSpec((None, PADW, K_BLOCK), lambda i, j, km, fl: (0, 0, km[i, j])),
            pl.BlockSpec((None, PADW, K_BLOCK), lambda i, j, km, fl: (1, 0, km[i, j])),
        ],
        out_specs=pl.BlockSpec((Q_BLOCK, PADW), lambda i, j, km, fl: (i, 0)),
        scratch_shapes=[
            pltpu.VMEM((Q_BLOCK, 1), jnp.float32),
            pltpu.VMEM((Q_BLOCK, 1), jnp.float32),
            pltpu.VMEM((Q_BLOCK, PADW), jnp.float32),
        ],
    )
    return pl.pallas_call(
        kernel,
        grid_spec=grid_spec,
        out_shape=jax.ShapeDtypeStruct((n_tok, PADW), jnp.bfloat16),
        compiler_params=pltpu.CompilerParams(dimension_semantics=("arbitrary", "arbitrary")),
        interpret=interpret,
    )(kb_map, flags, q_t, q_seg_f, kv, kv)


def on_device(
    hidden,
    gain_in,
    w_query,
    w_pair,
    kv_cache,
    recompute_rows,
    segment_ids,
    w_out,
    gain_merge,
    w_merge,
    requests,
):
    local_width, tok_rows = hidden.shape
    model_width = w_query.shape[1]
    n_col = model_width // local_width
    heads_here = local_width // HD
    score_scale = HD ** (-0.5)
    col_index = lax.axis_index("col")
    full_rows = lax.all_gather(hidden, "col", axis=0, tiled=True)
    out_weight = lax.all_gather(w_out, "col", axis=0, tiled=True)
    full_float = full_rows.astype(jnp.float32)
    in_mean = jnp.sum(full_float, axis=0, keepdims=True) / model_width
    in_square = jnp.sum(full_float * full_float, axis=0, keepdims=True) / model_width
    normed = (
        (full_float - in_mean)
        * lax.rsqrt(in_square - in_mean * in_mean + EPSILON)
        * gain_in.astype(jnp.float32)[:, None]
    ).astype(jnp.bfloat16)
    query_rows = lax.dot_general(
        normed, w_query, (((0,), (1,)), ((), ())), preferred_element_type=jnp.float32
    ).astype(jnp.bfloat16)
    query_rows = jnp.pad(query_rows, ((0, 0), (0, PADW - HD)))
    picked_rows = recompute_rows[0]
    normed_picked = jnp.take(normed, picked_rows, axis=1)
    fresh_pairs = jnp.dot(
        w_pair.reshape(2 * local_width, model_width),
        normed_picked,
        preferred_element_type=jnp.float32,
    )
    fresh_pairs = fresh_pairs.astype(jnp.bfloat16).reshape(2, local_width, -1)
    keys_values = kv_cache.at[:, :, picked_rows].set(fresh_pairs)

    pair_local = jnp.pad(keys_values, ((0, 0), (0, PADW - HD), (0, 0)))
    pair_local = pair_local.at[0, HD].set(segment_ids.astype(jnp.bfloat16))
    pair_all = lax.all_gather(pair_local, "row", axis=2, tiled=True)
    segment_line = pair_all[0, HD].astype(jnp.int32)
    kb_map, flags = block_tables(segment_ids, segment_line, lax.axis_index("row") * tok_rows)
    attended_rows = attention(
        query_rows, segment_ids.astype(jnp.float32)[:, None], pair_all, kb_map, flags, score_scale
    )
    attended = attended_rows[:, :HD].T
    chunk = tok_rows // n_col
    attended_chunk = lax.all_to_all(attended, "col", 1, 0, tiled=True)
    x_chunk = lax.dynamic_slice_in_dim(full_float, col_index * chunk, chunk, 1)
    projected = lax.dot_general(
        out_weight, attended_chunk, (((0,), (0,)), ((), ())), preferred_element_type=jnp.float32
    )
    updated = x_chunk + projected
    row_mean = jnp.sum(updated, axis=0, keepdims=True) / model_width
    row_square = jnp.sum(updated * updated, axis=0, keepdims=True) / model_width
    merger_chunk = (
        (updated - row_mean)
        * lax.rsqrt(row_square - row_mean * row_mean + EPSILON)
        * gain_merge.astype(jnp.float32)[:, None]
    ).astype(jnp.bfloat16)
    merge_weight, _ = lax.optimization_barrier((w_merge, pair_all))
    merge_full = lax.all_gather(merge_weight, "col", axis=1, tiled=True)
    grouped = merger_chunk.reshape(model_width, chunk // 4, 4)
    merged_here = jnp.einsum("fgi,ifd->gd", grouped, merge_full, preferred_element_type=jnp.float32)
    merged_all = lax.all_gather(merged_here.astype(jnp.bfloat16), "col", axis=0, tiled=True)
    wanted_rows = lax.dynamic_index_in_dim(requests[0], col_index, 0, keepdims=False)
    is_valid = wanted_rows >= 0
    safe_index = jnp.where(is_valid, wanted_rows, 0)
    picked = jnp.where(is_valid[:, None], merged_all[safe_index], jnp.zeros((), jnp.bfloat16))
    return picked.reshape(1, 1, picked.shape[0], model_width)


def solution(mesh):
    placed = (
        P("col", "row"),
        P(),
        P("col", None),
        P(None, "col", None),
        P(None, "col", "row"),
        P("row", None),
        P("row"),
        P("col", None),
        P(),
        P(None, "col", None),
        P("row", None, None),
    )
    return jax.shard_map(
        on_device,
        mesh=mesh,
        in_specs=placed,
        out_specs=P("row", "col", None, None),
        check_vma=False,
    )
```

```python
import jax
import jax.numpy as jnp
from jax import lax
import functools
from jax.experimental import pallas as pl
from jax.experimental.pallas import tpu as pltpu
from jax.sharding import PartitionSpec as P

HD = 88


EPSILON = 1e-06
MASKED = -1e30
PADW = 96
Q_BLOCK = 512
K_BLOCK = 1024


def _attn_kernel(kb_map, flags, q_ref, qs_ref, k_ref, v_ref, o_ref, m_ref, l_ref, acc_ref, *, scale, n_steps):
    qb = pl.program_id(0)
    j = pl.program_id(1)
    flag = flags[qb, j]

    @pl.when(j == 0)
    def _():
        m_ref[...] = jnp.full(m_ref.shape, MASKED, jnp.float32)
        l_ref[...] = jnp.zeros(l_ref.shape, jnp.float32)
        acc_ref[...] = jnp.zeros(acc_ref.shape, jnp.float32)

    def step(masked):
        q = q_ref[...]
        k = k_ref[...]
        s = jnp.dot(q, k, preferred_element_type=jnp.float32) * scale
        if masked:
            key_seg = k[HD:HD + 1, :].astype(jnp.float32)
            s = jnp.where(qs_ref[...] == key_seg, s, MASKED)
        m_prev = m_ref[...]
        m_new = jnp.maximum(m_prev, jnp.max(s, axis=1, keepdims=True))
        p = jnp.exp(s - m_new)
        alpha = jnp.exp(m_prev - m_new)
        l_ref[...] = alpha * l_ref[...] + jnp.sum(p, axis=1, keepdims=True)
        pv = lax.dot_general(
            p.astype(jnp.bfloat16), v_ref[...], (((1,), (1,)), ((), ())),
            preferred_element_type=jnp.float32,
        )
        acc_ref[...] = alpha * acc_ref[...] + pv
        m_ref[...] = m_new

    @pl.when(flag == 1)
    def _():
        step(True)

    @pl.when(flag == 2)
    def _():
        step(False)

    @pl.when(j == n_steps - 1)
    def _():
        o_ref[...] = (acc_ref[...] / l_ref[...]).astype(o_ref.dtype)


def block_tables(q_seg, k_seg, q_start):
    n_q = q_seg.shape[0] // Q_BLOCK
    n_k = k_seg.shape[0] // K_BLOCK
    values = jnp.arange(-1, 2, dtype=jnp.int32)
    q_has = jnp.any(q_seg.reshape(n_q, Q_BLOCK, 1) == values, axis=1).astype(jnp.float32)
    k_has = jnp.any(k_seg.reshape(n_k, K_BLOCK, 1) == values, axis=1).astype(jnp.float32)
    shared = jnp.dot(q_has, k_has.T) > 0
    single = (jnp.sum(q_has, axis=1)[:, None] == 1) & (jnp.sum(k_has, axis=1)[None, :] == 1)
    diag = (q_start + jnp.arange(n_q, dtype=jnp.int32) * Q_BLOCK) // K_BLOCK
    order = (diag[:, None] + jnp.arange(n_k, dtype=jnp.int32)[None, :]) % n_k
    need = jnp.take_along_axis(shared, order, axis=1)
    full = jnp.take_along_axis(single, order, axis=1)
    rank = jnp.cumsum(need.astype(jnp.int32), axis=1) - 1
    count = jnp.sum(need.astype(jnp.int32), axis=1)
    pos = jnp.where(need, rank, n_k + jnp.arange(n_k)[None, :])
    perm = jnp.argsort(pos, axis=1)
    kb_sorted = jnp.take_along_axis(order, perm, axis=1)
    full_sorted = jnp.take_along_axis(full, perm, axis=1)
    step = jnp.arange(n_k, dtype=jnp.int32)[None, :]
    live = step < count[:, None]
    last = jnp.take_along_axis(kb_sorted, (count - 1)[:, None], axis=1)
    kb_map = jnp.where(live, kb_sorted, last).astype(jnp.int32)
    flags = jnp.where(live, jnp.where(full_sorted, 2, 1), 0).astype(jnp.int32)
    return kb_map, flags


def attention(q_t, q_seg_f, kv, kb_map, flags, scale, interpret=False):
    n_tok = q_t.shape[0]
    n_keys = kv.shape[2]
    n_q = n_tok // Q_BLOCK
    n_k = n_keys // K_BLOCK
    kernel = functools.partial(_attn_kernel, scale=scale, n_steps=n_k)
    grid_spec = pltpu.PrefetchScalarGridSpec(
        num_scalar_prefetch=2,
        grid=(n_q, n_k),
        in_specs=[
            pl.BlockSpec((Q_BLOCK, PADW), lambda i, j, km, fl: (i, 0)),
            pl.BlockSpec((Q_BLOCK, 1), lambda i, j, km, fl: (i, 0)),
            pl.BlockSpec((None, PADW, K_BLOCK), lambda i, j, km, fl: (0, 0, km[i, j])),
            pl.BlockSpec((None, PADW, K_BLOCK), lambda i, j, km, fl: (1, 0, km[i, j])),
        ],
        out_specs=pl.BlockSpec((Q_BLOCK, PADW), lambda i, j, km, fl: (i, 0)),
        scratch_shapes=[
            pltpu.VMEM((Q_BLOCK, 1), jnp.float32),
            pltpu.VMEM((Q_BLOCK, 1), jnp.float32),
            pltpu.VMEM((Q_BLOCK, PADW), jnp.float32),
        ],
    )
    return pl.pallas_call(
        kernel,
        grid_spec=grid_spec,
        out_shape=jax.ShapeDtypeStruct((n_tok, PADW), jnp.bfloat16),
        compiler_params=pltpu.CompilerParams(dimension_semantics=("arbitrary", "arbitrary")),
        interpret=interpret,
    )(kb_map, flags, q_t, q_seg_f, kv, kv)


def on_device(
    hidden,
    gain_in,
    w_query,
    w_pair,
    kv_cache,
    recompute_rows,
    segment_ids,
    w_out,
    gain_merge,
    w_merge,
    requests,
):
    local_width, tok_rows = hidden.shape
    model_width = w_query.shape[1]
    n_col = model_width // local_width
    heads_here = local_width // HD
    score_scale = HD ** (-0.5)
    col_index = lax.axis_index("col")
    full_rows = lax.all_gather(hidden, "col", axis=0, tiled=True)
    out_weight = lax.all_gather(w_out, "col", axis=0, tiled=True)
    full_float = full_rows.astype(jnp.float32)
    in_mean = jnp.sum(full_float, axis=0, keepdims=True) / model_width
    in_square = jnp.sum(full_float * full_float, axis=0, keepdims=True) / model_width
    normed = (
        (full_float - in_mean)
        * lax.rsqrt(in_square - in_mean * in_mean + EPSILON)
        * gain_in.astype(jnp.float32)[:, None]
    ).astype(jnp.bfloat16)
    query_rows = lax.dot_general(
        normed, w_query, (((0,), (1,)), ((), ())), preferred_element_type=jnp.float32
    ).astype(jnp.bfloat16)
    query_rows = jnp.pad(query_rows, ((0, 0), (0, PADW - HD)))
    picked_rows = recompute_rows[0]
    hidden_picked = jnp.take(hidden, picked_rows, axis=1)
    picked_copies = jnp.broadcast_to(hidden_picked[None], (n_col,) + hidden_picked.shape)
    picked_full = lax.all_to_all(picked_copies, "col", 0, 0, tiled=True)
    picked_float = picked_full.reshape(model_width, -1).astype(jnp.float32)
    picked_mean = jnp.sum(picked_float, axis=0, keepdims=True) / model_width
    picked_square = jnp.sum(picked_float * picked_float, axis=0, keepdims=True) / model_width
    normed_picked = (
        (picked_float - picked_mean)
        * lax.rsqrt(picked_square - picked_mean * picked_mean + EPSILON)
        * gain_in.astype(jnp.float32)[:, None]
    ).astype(jnp.bfloat16)
    fresh_pairs = jnp.dot(
        w_pair.reshape(2 * local_width, model_width),
        normed_picked,
        preferred_element_type=jnp.float32,
    )
    fresh_pairs = fresh_pairs.astype(jnp.bfloat16).reshape(2, local_width, -1)
    keys_values = kv_cache.at[:, :, picked_rows].set(fresh_pairs)

    pair_local = jnp.pad(keys_values, ((0, 0), (0, PADW - HD), (0, 0)))
    pair_local = pair_local.at[0, HD].set(segment_ids.astype(jnp.bfloat16))
    pair_local, _ = lax.optimization_barrier((pair_local, full_rows))
    pair_all = lax.all_gather(pair_local, "row", axis=2, tiled=True)
    segment_line = pair_all[0, HD].astype(jnp.int32)
    kb_map, flags = block_tables(segment_ids, segment_line, lax.axis_index("row") * tok_rows)
    attended_rows = attention(
        query_rows, segment_ids.astype(jnp.float32)[:, None], pair_all, kb_map, flags, score_scale
    )
    attended = attended_rows[:, :HD].T
    chunk = tok_rows // n_col
    attended_chunk = lax.all_to_all(attended, "col", 1, 0, tiled=True)
    x_chunk = lax.dynamic_slice_in_dim(full_float, col_index * chunk, chunk, 1)
    projected = lax.dot_general(
        out_weight, attended_chunk, (((0,), (0,)), ((), ())), preferred_element_type=jnp.float32
    )
    updated = x_chunk + projected
    row_mean = jnp.sum(updated, axis=0, keepdims=True) / model_width
    row_square = jnp.sum(updated * updated, axis=0, keepdims=True) / model_width
    merger_chunk = (
        (updated - row_mean)
        * lax.rsqrt(row_square - row_mean * row_mean + EPSILON)
        * gain_merge.astype(jnp.float32)[:, None]
    ).astype(jnp.bfloat16)
    merge_weight, _ = lax.optimization_barrier((w_merge, pair_all))
    merge_full = lax.all_gather(merge_weight, "col", axis=1, tiled=True)
    grouped = merger_chunk.reshape(model_width, chunk // 4, 4)
    merged_here = jnp.einsum("fgi,ifd->gd", grouped, merge_full, preferred_element_type=jnp.float32)
    merged_all = lax.all_gather(merged_here.astype(jnp.bfloat16), "col", axis=0, tiled=True)
    wanted_rows = lax.dynamic_index_in_dim(requests[0], col_index, 0, keepdims=False)
    is_valid = wanted_rows >= 0
    safe_index = jnp.where(is_valid, wanted_rows, 0)
    picked = jnp.where(is_valid[:, None], merged_all[safe_index], jnp.zeros((), jnp.bfloat16))
    return picked.reshape(1, 1, picked.shape[0], model_width)


def solution(mesh):
    placed = (
        P("col", "row"),
        P(),
        P("col", None),
        P(None, "col", None),
        P(None, "col", "row"),
        P("row", None),
        P("row"),
        P("col", None),
        P(),
        P(None, "col", None),
        P("row", None, None),
    )
    return jax.shard_map(
        on_device,
        mesh=mesh,
        in_specs=placed,
        out_specs=P("row", "col", None, None),
        check_vma=False,
    )
```

```python
import jax
import jax.numpy as jnp
from jax import lax
import functools
from jax.experimental import pallas as pl
from jax.experimental.pallas import tpu as pltpu
from jax.sharding import PartitionSpec as P

HD = 88


EPSILON = 1e-06
MASKED = -1e30
PADW = 96
Q_BLOCK = 512
K_BLOCK = 1024


def _attn_kernel(kb_map, flags, q_ref, qs_ref, k_ref, v_ref, o_ref, m_ref, l_ref, acc_ref, *, scale, n_steps):
    qb = pl.program_id(0)
    j = pl.program_id(1)
    flag = flags[qb, j]

    @pl.when(j == 0)
    def _():
        m_ref[...] = jnp.full(m_ref.shape, MASKED, jnp.float32)
        l_ref[...] = jnp.zeros(l_ref.shape, jnp.float32)
        acc_ref[...] = jnp.zeros(acc_ref.shape, jnp.float32)

    def step(masked):
        q = q_ref[...]
        k = k_ref[...]
        s = jnp.dot(q, k, preferred_element_type=jnp.float32) * scale
        if masked:
            key_seg = k[HD:HD + 1, :].astype(jnp.float32)
            s = jnp.where(qs_ref[...] == key_seg, s, MASKED)
        m_prev = m_ref[...]
        m_new = jnp.maximum(m_prev, jnp.max(s, axis=1, keepdims=True))
        p = jnp.exp(s - m_new)
        alpha = jnp.exp(m_prev - m_new)
        l_ref[...] = alpha * l_ref[...] + jnp.sum(p, axis=1, keepdims=True)
        pv = lax.dot_general(
            p.astype(jnp.bfloat16), v_ref[...], (((1,), (1,)), ((), ())),
            preferred_element_type=jnp.float32,
        )
        acc_ref[...] = alpha * acc_ref[...] + pv
        m_ref[...] = m_new

    @pl.when(flag == 1)
    def _():
        step(True)

    @pl.when(flag == 2)
    def _():
        step(False)

    @pl.when(j == n_steps - 1)
    def _():
        o_ref[...] = (acc_ref[...] / l_ref[...]).astype(o_ref.dtype)


def block_tables(q_seg, k_seg, q_start):
    n_q = q_seg.shape[0] // Q_BLOCK
    n_k = k_seg.shape[0] // K_BLOCK
    values = jnp.arange(-1, 2, dtype=jnp.int32)
    q_has = jnp.any(q_seg.reshape(n_q, Q_BLOCK, 1) == values, axis=1).astype(jnp.float32)
    k_has = jnp.any(k_seg.reshape(n_k, K_BLOCK, 1) == values, axis=1).astype(jnp.float32)
    shared = jnp.dot(q_has, k_has.T) > 0
    single = (jnp.sum(q_has, axis=1)[:, None] == 1) & (jnp.sum(k_has, axis=1)[None, :] == 1)
    diag = (q_start + jnp.arange(n_q, dtype=jnp.int32) * Q_BLOCK) // K_BLOCK
    order = (diag[:, None] + jnp.arange(n_k, dtype=jnp.int32)[None, :]) % n_k
    need = jnp.take_along_axis(shared, order, axis=1)
    full = jnp.take_along_axis(single, order, axis=1)
    rank = jnp.cumsum(need.astype(jnp.int32), axis=1) - 1
    count = jnp.sum(need.astype(jnp.int32), axis=1)
    pos = jnp.where(need, rank, n_k + jnp.arange(n_k)[None, :])
    perm = jnp.argsort(pos, axis=1)
    kb_sorted = jnp.take_along_axis(order, perm, axis=1)
    full_sorted = jnp.take_along_axis(full, perm, axis=1)
    step = jnp.arange(n_k, dtype=jnp.int32)[None, :]
    live = step < count[:, None]
    last = jnp.take_along_axis(kb_sorted, (count - 1)[:, None], axis=1)
    kb_map = jnp.where(live, kb_sorted, last).astype(jnp.int32)
    flags = jnp.where(live, jnp.where(full_sorted, 2, 1), 0).astype(jnp.int32)
    return kb_map, flags


def attention(q_t, q_seg_f, kv, kb_map, flags, scale, interpret=False):
    n_tok = q_t.shape[0]
    n_keys = kv.shape[2]
    n_q = n_tok // Q_BLOCK
    n_k = n_keys // K_BLOCK
    kernel = functools.partial(_attn_kernel, scale=scale, n_steps=n_k)
    grid_spec = pltpu.PrefetchScalarGridSpec(
        num_scalar_prefetch=2,
        grid=(n_q, n_k),
        in_specs=[
            pl.BlockSpec((Q_BLOCK, PADW), lambda i, j, km, fl: (i, 0)),
            pl.BlockSpec((Q_BLOCK, 1), lambda i, j, km, fl: (i, 0)),
            pl.BlockSpec((None, PADW, K_BLOCK), lambda i, j, km, fl: (0, 0, km[i, j])),
            pl.BlockSpec((None, PADW, K_BLOCK), lambda i, j, km, fl: (1, 0, km[i, j])),
        ],
        out_specs=pl.BlockSpec((Q_BLOCK, PADW), lambda i, j, km, fl: (i, 0)),
        scratch_shapes=[
            pltpu.VMEM((Q_BLOCK, 1), jnp.float32),
            pltpu.VMEM((Q_BLOCK, 1), jnp.float32),
            pltpu.VMEM((Q_BLOCK, PADW), jnp.float32),
        ],
    )
    return pl.pallas_call(
        kernel,
        grid_spec=grid_spec,
        out_shape=jax.ShapeDtypeStruct((n_tok, PADW), jnp.bfloat16),
        compiler_params=pltpu.CompilerParams(dimension_semantics=("arbitrary", "arbitrary")),
        interpret=interpret,
    )(kb_map, flags, q_t, q_seg_f, kv, kv)


def on_device(
    hidden,
    gain_in,
    w_query,
    w_pair,
    kv_cache,
    recompute_rows,
    segment_ids,
    w_out,
    gain_merge,
    w_merge,
    requests,
):
    local_width, tok_rows = hidden.shape
    model_width = w_query.shape[1]
    n_col = model_width // local_width
    heads_here = local_width // HD
    score_scale = HD ** (-0.5)
    col_index = lax.axis_index("col")
    full_rows = lax.all_gather(hidden, "col", axis=0, tiled=True)
    full_float = full_rows.astype(jnp.float32)
    in_mean = jnp.sum(full_float, axis=0, keepdims=True) / model_width
    in_square = jnp.sum(full_float * full_float, axis=0, keepdims=True) / model_width
    normed = (
        (full_float - in_mean)
        * lax.rsqrt(in_square - in_mean * in_mean + EPSILON)
        * gain_in.astype(jnp.float32)[:, None]
    ).astype(jnp.bfloat16)
    query_rows = lax.dot_general(
        normed, w_query, (((0,), (1,)), ((), ())), preferred_element_type=jnp.float32
    ).astype(jnp.bfloat16)
    query_rows = jnp.pad(query_rows, ((0, 0), (0, PADW - HD)))
    picked_rows = recompute_rows[0]
    hidden_picked = jnp.take(hidden, picked_rows, axis=1)
    picked_copies = jnp.broadcast_to(hidden_picked[None], (n_col,) + hidden_picked.shape)
    picked_full = lax.all_to_all(picked_copies, "col", 0, 0, tiled=True)
    picked_float = picked_full.reshape(model_width, -1).astype(jnp.float32)
    picked_mean = jnp.sum(picked_float, axis=0, keepdims=True) / model_width
    picked_square = jnp.sum(picked_float * picked_float, axis=0, keepdims=True) / model_width
    normed_picked = (
        (picked_float - picked_mean)
        * lax.rsqrt(picked_square - picked_mean * picked_mean + EPSILON)
        * gain_in.astype(jnp.float32)[:, None]
    ).astype(jnp.bfloat16)
    fresh_pairs = jnp.dot(
        w_pair.reshape(2 * local_width, model_width),
        normed_picked,
        preferred_element_type=jnp.float32,
    )
    fresh_pairs = fresh_pairs.astype(jnp.bfloat16).reshape(2, local_width, -1)
    keys_values = kv_cache.at[:, :, picked_rows].set(fresh_pairs)

    pair_local = jnp.pad(keys_values, ((0, 0), (0, PADW - HD), (0, 0)))
    pair_local = pair_local.at[0, HD].set(segment_ids.astype(jnp.bfloat16))
    pair_local, _ = lax.optimization_barrier((pair_local, full_rows))
    pair_all = lax.all_gather(pair_local, "row", axis=2, tiled=True)
    segment_line = pair_all[0, HD].astype(jnp.int32)
    weight_stack = jnp.concatenate([w_out[None], w_merge], axis=0)
    weight_stack, _ = lax.optimization_barrier((weight_stack, pair_all))
    weights_full = lax.all_gather(weight_stack, "col", axis=1, tiled=True)
    out_weight = weights_full[0]
    merge_full = weights_full[1:]
    kb_map, flags = block_tables(segment_ids, segment_line, lax.axis_index("row") * tok_rows)
    attended_rows = attention(
        query_rows, segment_ids.astype(jnp.float32)[:, None], pair_all, kb_map, flags, score_scale
    )
    attended = attended_rows[:, :HD].T
    chunk = tok_rows // n_col
    attended_chunk = lax.all_to_all(attended, "col", 1, 0, tiled=True)
    x_chunk = lax.dynamic_slice_in_dim(full_float, col_index * chunk, chunk, 1)
    projected = lax.dot_general(
        out_weight, attended_chunk, (((0,), (0,)), ((), ())), preferred_element_type=jnp.float32
    )
    updated = x_chunk + projected
    row_mean = jnp.sum(updated, axis=0, keepdims=True) / model_width
    row_square = jnp.sum(updated * updated, axis=0, keepdims=True) / model_width
    merger_chunk = (
        (updated - row_mean)
        * lax.rsqrt(row_square - row_mean * row_mean + EPSILON)
        * gain_merge.astype(jnp.float32)[:, None]
    ).astype(jnp.bfloat16)
    grouped = merger_chunk.reshape(model_width, chunk // 4, 4)
    merged_here = jnp.einsum("fgi,ifd->gd", grouped, merge_full, preferred_element_type=jnp.float32)
    merged_all = lax.all_gather(merged_here.astype(jnp.bfloat16), "col", axis=0, tiled=True)
    wanted_rows = lax.dynamic_index_in_dim(requests[0], col_index, 0, keepdims=False)
    is_valid = wanted_rows >= 0
    safe_index = jnp.where(is_valid, wanted_rows, 0)
    picked = jnp.where(is_valid[:, None], merged_all[safe_index], jnp.zeros((), jnp.bfloat16))
    return picked.reshape(1, 1, picked.shape[0], model_width)


def solution(mesh):
    placed = (
        P("col", "row"),
        P(),
        P("col", None),
        P(None, "col", None),
        P(None, "col", "row"),
        P("row", None),
        P("row"),
        P("col", None),
        P(),
        P(None, "col", None),
        P("row", None, None),
    )
    return jax.shard_map(
        on_device,
        mesh=mesh,
        in_specs=placed,
        out_specs=P("row", "col", None, None),
        check_vma=False,
    )
```

```python
import jax
import jax.numpy as jnp
from jax import lax
import functools
from jax.experimental import pallas as pl
from jax.experimental.pallas import tpu as pltpu
from jax.sharding import PartitionSpec as P

HD = 88


EPSILON = 1e-06
MASKED = -1e30
PADW = 96
Q_BLOCK = 512
K_BLOCK = 1024


def _attn_kernel(kb_map, flags, q_ref, qs_ref, k_ref, v_ref, o_ref, m_ref, l_ref, acc_ref, *, scale, n_steps):
    qb = pl.program_id(0)
    j = pl.program_id(1)
    flag = flags[qb, j]

    @pl.when(j == 0)
    def _():
        m_ref[...] = jnp.full(m_ref.shape, MASKED, jnp.float32)
        l_ref[...] = jnp.zeros(l_ref.shape, jnp.float32)
        acc_ref[...] = jnp.zeros(acc_ref.shape, jnp.float32)

    def step(masked):
        q = q_ref[...]
        k = k_ref[...]
        s = jnp.dot(q, k, preferred_element_type=jnp.float32) * scale
        if masked:
            key_seg = k[HD:HD + 1, :].astype(jnp.float32)
            s = jnp.where(qs_ref[...] == key_seg, s, MASKED)
        m_prev = m_ref[...]
        m_new = jnp.maximum(m_prev, jnp.max(s, axis=1, keepdims=True))
        p = jnp.exp(s - m_new)
        alpha = jnp.exp(m_prev - m_new)
        l_ref[...] = alpha * l_ref[...] + jnp.sum(p, axis=1, keepdims=True)
        pv = lax.dot_general(
            p.astype(jnp.bfloat16), v_ref[...], (((1,), (1,)), ((), ())),
            preferred_element_type=jnp.float32,
        )
        acc_ref[...] = alpha * acc_ref[...] + pv
        m_ref[...] = m_new

    @pl.when(flag == 1)
    def _():
        step(True)

    @pl.when(flag == 2)
    def _():
        step(False)

    @pl.when(j == n_steps - 1)
    def _():
        o_ref[...] = (acc_ref[...] / l_ref[...]).astype(o_ref.dtype)


def _row_gather_kernel(x_ref, o_ref, send_sems, recv_sems, local_sem, *, n_row):
    me = lax.axis_index("row")
    col = lax.axis_index("col")
    barrier = pltpu.get_barrier_semaphore()
    for k in range(1, n_row):
        peer = lax.rem(me + k, n_row)
        pl.semaphore_signal(barrier, inc=1, device_id=(peer, col), device_id_type=pl.DeviceIdType.MESH)
    pl.semaphore_wait(barrier, n_row - 1)
    local = pltpu.make_async_copy(x_ref, o_ref.at[me], local_sem)
    local.start()
    copies = []
    for k in range(1, n_row):
        peer = lax.rem(me + k, n_row)
        copy = pltpu.make_async_remote_copy(
            src_ref=x_ref,
            dst_ref=o_ref.at[me],
            send_sem=send_sems.at[k],
            recv_sem=recv_sems.at[k],
            device_id=(peer, col),
            device_id_type=pl.DeviceIdType.MESH,
        )
        copy.start()
        copies.append(copy)
    local.wait()
    for copy in copies:
        copy.wait()


def row_gather(x, n_row):
    return pl.pallas_call(
        functools.partial(_row_gather_kernel, n_row=n_row),
        out_shape=jax.ShapeDtypeStruct((n_row,) + x.shape, x.dtype),
        in_specs=[pl.BlockSpec(memory_space=pl.ANY)],
        out_specs=pl.BlockSpec(memory_space=pl.ANY),
        scratch_shapes=[
            pltpu.SemaphoreType.DMA((n_row,)),
            pltpu.SemaphoreType.DMA((n_row,)),
            pltpu.SemaphoreType.DMA,
        ],
        compiler_params=pltpu.CompilerParams(collective_id=0, has_side_effects=True),
    )(x)


def block_tables(q_seg, k_seg, q_start):
    n_q = q_seg.shape[0] // Q_BLOCK
    n_k = k_seg.shape[0] // K_BLOCK
    values = jnp.arange(-1, 2, dtype=jnp.int32)
    q_has = jnp.any(q_seg.reshape(n_q, Q_BLOCK, 1) == values, axis=1).astype(jnp.float32)
    k_has = jnp.any(k_seg.reshape(n_k, K_BLOCK, 1) == values, axis=1).astype(jnp.float32)
    shared = jnp.dot(q_has, k_has.T) > 0
    single = (jnp.sum(q_has, axis=1)[:, None] == 1) & (jnp.sum(k_has, axis=1)[None, :] == 1)
    diag = (q_start + jnp.arange(n_q, dtype=jnp.int32) * Q_BLOCK) // K_BLOCK
    order = (diag[:, None] + jnp.arange(n_k, dtype=jnp.int32)[None, :]) % n_k
    need = jnp.take_along_axis(shared, order, axis=1)
    full = jnp.take_along_axis(single, order, axis=1)
    rank = jnp.cumsum(need.astype(jnp.int32), axis=1) - 1
    count = jnp.sum(need.astype(jnp.int32), axis=1)
    pos = jnp.where(need, rank, n_k + jnp.arange(n_k)[None, :])
    perm = jnp.argsort(pos, axis=1)
    kb_sorted = jnp.take_along_axis(order, perm, axis=1)
    full_sorted = jnp.take_along_axis(full, perm, axis=1)
    step = jnp.arange(n_k, dtype=jnp.int32)[None, :]
    live = step < count[:, None]
    last = jnp.take_along_axis(kb_sorted, (count - 1)[:, None], axis=1)
    kb_map = jnp.where(live, kb_sorted, last).astype(jnp.int32)
    flags = jnp.where(live, jnp.where(full_sorted, 2, 1), 0).astype(jnp.int32)
    return kb_map, flags


def attention(q_t, q_seg_f, kv, kb_map, flags, scale, interpret=False):
    n_tok = q_t.shape[0]
    per_peer = kv.shape[3] // K_BLOCK
    n_keys = kv.shape[0] * kv.shape[3]
    n_q = n_tok // Q_BLOCK
    n_k = n_keys // K_BLOCK
    kernel = functools.partial(_attn_kernel, scale=scale, n_steps=n_k)
    grid_spec = pltpu.PrefetchScalarGridSpec(
        num_scalar_prefetch=2,
        grid=(n_q, n_k),
        in_specs=[
            pl.BlockSpec((Q_BLOCK, PADW), lambda i, j, km, fl: (i, 0)),
            pl.BlockSpec((Q_BLOCK, 1), lambda i, j, km, fl: (i, 0)),
            pl.BlockSpec((None, None, PADW, K_BLOCK), lambda i, j, km, fl: (km[i, j] // per_peer, 0, 0, km[i, j] % per_peer)),
            pl.BlockSpec((None, None, PADW, K_BLOCK), lambda i, j, km, fl: (km[i, j] // per_peer, 1, 0, km[i, j] % per_peer)),
        ],
        out_specs=pl.BlockSpec((Q_BLOCK, PADW), lambda i, j, km, fl: (i, 0)),
        scratch_shapes=[
            pltpu.VMEM((Q_BLOCK, 1), jnp.float32),
            pltpu.VMEM((Q_BLOCK, 1), jnp.float32),
            pltpu.VMEM((Q_BLOCK, PADW), jnp.float32),
        ],
    )
    return pl.pallas_call(
        kernel,
        grid_spec=grid_spec,
        out_shape=jax.ShapeDtypeStruct((n_tok, PADW), jnp.bfloat16),
        compiler_params=pltpu.CompilerParams(dimension_semantics=("arbitrary", "arbitrary")),
        interpret=interpret,
    )(kb_map, flags, q_t, q_seg_f, kv, kv)


def on_device(
    n_row,
    hidden,
    gain_in,
    w_query,
    w_pair,
    kv_cache,
    recompute_rows,
    segment_ids,
    w_out,
    gain_merge,
    w_merge,
    requests,
):
    local_width, tok_rows = hidden.shape
    model_width = w_query.shape[1]
    n_col = model_width // local_width
    heads_here = local_width // HD
    score_scale = HD ** (-0.5)
    col_index = lax.axis_index("col")
    gathered_rows = lax.all_gather(hidden, "col", axis=0, tiled=True)
    picked_rows = recompute_rows[0]
    hidden_picked = jnp.take(hidden, picked_rows, axis=1)
    picked_copies = jnp.broadcast_to(hidden_picked[None], (n_col,) + hidden_picked.shape)
    picked_full = lax.all_to_all(picked_copies, "col", 0, 0, tiled=True)
    picked_float = picked_full.reshape(model_width, -1).astype(jnp.float32)
    picked_mean = jnp.sum(picked_float, axis=0, keepdims=True) / model_width
    picked_square = jnp.sum(picked_float * picked_float, axis=0, keepdims=True) / model_width
    normed_picked = (
        (picked_float - picked_mean)
        * lax.rsqrt(picked_square - picked_mean * picked_mean + EPSILON)
        * gain_in.astype(jnp.float32)[:, None]
    ).astype(jnp.bfloat16)
    fresh_pairs = jnp.dot(
        w_pair.reshape(2 * local_width, model_width),
        normed_picked,
        preferred_element_type=jnp.float32,
    )
    fresh_pairs = fresh_pairs.astype(jnp.bfloat16).reshape(2, local_width, -1)
    keys_values = kv_cache.at[:, :, picked_rows].set(fresh_pairs)

    pair_local = jnp.pad(keys_values, ((0, 0), (0, PADW - HD), (0, 0)))
    pair_local = pair_local.at[0, HD].set(segment_ids.astype(jnp.bfloat16))
    pair_all = row_gather(pair_local, n_row)
    full_rows, pair_all = lax.optimization_barrier((gathered_rows, pair_all))
    full_float = full_rows.astype(jnp.float32)
    in_mean = jnp.sum(full_float, axis=0, keepdims=True) / model_width
    in_square = jnp.sum(full_float * full_float, axis=0, keepdims=True) / model_width
    normed = (
        (full_float - in_mean)
        * lax.rsqrt(in_square - in_mean * in_mean + EPSILON)
        * gain_in.astype(jnp.float32)[:, None]
    ).astype(jnp.bfloat16)
    query_rows = lax.dot_general(
        normed, w_query, (((0,), (1,)), ((), ())), preferred_element_type=jnp.float32
    ).astype(jnp.bfloat16)
    query_rows = jnp.pad(query_rows, ((0, 0), (0, PADW - HD)))
    segment_line = pair_all[:, 0, HD].reshape(-1).astype(jnp.int32)
    weight_stack = jnp.concatenate([w_out[None], w_merge], axis=0)
    weight_stack, _ = lax.optimization_barrier((weight_stack, full_rows))
    weights_full = lax.all_gather(weight_stack, "col", axis=1, tiled=True)
    out_weight = weights_full[0]
    merge_full = weights_full[1:]
    kb_map, flags = block_tables(segment_ids, segment_line, lax.axis_index("row") * tok_rows)
    attended_rows = attention(
        query_rows, segment_ids.astype(jnp.float32)[:, None], pair_all, kb_map, flags, score_scale
    )
    attended = attended_rows[:, :HD].T
    chunk = tok_rows // n_col
    attended_chunk = lax.all_to_all(attended, "col", 1, 0, tiled=True)
    x_chunk = lax.dynamic_slice_in_dim(full_float, col_index * chunk, chunk, 1)
    projected = lax.dot_general(
        out_weight, attended_chunk, (((0,), (0,)), ((), ())), preferred_element_type=jnp.float32
    )
    updated = x_chunk + projected
    row_mean = jnp.sum(updated, axis=0, keepdims=True) / model_width
    row_square = jnp.sum(updated * updated, axis=0, keepdims=True) / model_width
    merger_chunk = (
        (updated - row_mean)
        * lax.rsqrt(row_square - row_mean * row_mean + EPSILON)
        * gain_merge.astype(jnp.float32)[:, None]
    ).astype(jnp.bfloat16)
    grouped = merger_chunk.reshape(model_width, chunk // 4, 4)
    merged_here = jnp.einsum("fgi,ifd->gd", grouped, merge_full, preferred_element_type=jnp.float32)
    merged_all = lax.all_gather(merged_here.astype(jnp.bfloat16), "col", axis=0, tiled=True)
    wanted_rows = lax.dynamic_index_in_dim(requests[0], col_index, 0, keepdims=False)
    is_valid = wanted_rows >= 0
    safe_index = jnp.where(is_valid, wanted_rows, 0)
    picked = jnp.where(is_valid[:, None], merged_all[safe_index], jnp.zeros((), jnp.bfloat16))
    return picked.reshape(1, 1, picked.shape[0], model_width)


def solution(mesh):
    placed = (
        P("col", "row"),
        P(),
        P("col", None),
        P(None, "col", None),
        P(None, "col", "row"),
        P("row", None),
        P("row"),
        P("col", None),
        P(),
        P(None, "col", None),
        P("row", None, None),
    )
    return jax.shard_map(
        functools.partial(on_device, mesh.shape["row"]),
        mesh=mesh,
        in_specs=placed,
        out_specs=P("row", "col", None, None),
        check_vma=False,
    )
```

```python
import jax
import jax.numpy as jnp
from jax import lax
import functools
from jax.experimental import pallas as pl
from jax.experimental.pallas import tpu as pltpu
from jax.sharding import PartitionSpec as P

HD = 88


EPSILON = 1e-06
MASKED = -1e30
PADW = 96
Q_BLOCK = 512
K_BLOCK = 1024


def _attn_kernel(kb_map, flags, q_ref, qs_ref, k_ref, v_ref, o_ref, m_ref, l_ref, acc_ref, *, scale, n_steps):
    qb = pl.program_id(0)
    j = pl.program_id(1)
    flag = flags[qb, j]

    @pl.when(j == 0)
    def _():
        m_ref[...] = jnp.full(m_ref.shape, MASKED, jnp.float32)
        l_ref[...] = jnp.zeros(l_ref.shape, jnp.float32)
        acc_ref[...] = jnp.zeros(acc_ref.shape, jnp.float32)

    def step(masked):
        q = q_ref[...]
        k = k_ref[...]
        s = jnp.dot(q, k, preferred_element_type=jnp.float32) * scale
        if masked:
            key_seg = k[HD:HD + 1, :].astype(jnp.float32)
            s = jnp.where(qs_ref[...] == key_seg, s, MASKED)
        m_prev = m_ref[...]
        m_new = jnp.maximum(m_prev, jnp.max(s, axis=1, keepdims=True))
        p = jnp.exp(s - m_new)
        alpha = jnp.exp(m_prev - m_new)
        l_ref[...] = alpha * l_ref[...] + jnp.sum(p, axis=1, keepdims=True)
        pv = lax.dot_general(
            p.astype(jnp.bfloat16), v_ref[...], (((1,), (1,)), ((), ())),
            preferred_element_type=jnp.float32,
        )
        acc_ref[...] = alpha * acc_ref[...] + pv
        m_ref[...] = m_new

    @pl.when(flag == 1)
    def _():
        step(True)

    @pl.when(flag == 2)
    def _():
        step(False)

    @pl.when(j == n_steps - 1)
    def _():
        o_ref[...] = (acc_ref[...] / l_ref[...]).astype(o_ref.dtype)


def _row_gather_kernel(x_ref, o_ref, send_far, recv_far, send_pair, recv_pair, send_fwd, recv_fwd, local_sem, *, n_row):
    mesh_ids = pl.DeviceIdType.MESH
    n_chip = n_row // 2
    me = lax.axis_index("row")
    col = lax.axis_index("col")
    chip = me // 2
    core = me % 2
    sibling = chip * 2 + 1 - core
    far = [lax.rem(chip + k, n_chip) * 2 + core for k in range(1, n_chip)]
    barrier = pltpu.get_barrier_semaphore()
    for peer in far + [sibling]:
        pl.semaphore_signal(barrier, inc=1, device_id=(peer, col), device_id_type=mesh_ids)
    pl.semaphore_wait(barrier, n_chip)
    local = pltpu.make_async_copy(x_ref, o_ref.at[me], local_sem)
    local.start()
    pair = pltpu.make_async_remote_copy(
        src_ref=x_ref, dst_ref=o_ref.at[me], send_sem=send_pair, recv_sem=recv_pair,
        device_id=(sibling, col), device_id_type=mesh_ids,
    )
    pair.start()
    outgoing = []
    for k in range(1, n_chip):
        copy = pltpu.make_async_remote_copy(
            src_ref=x_ref, dst_ref=o_ref.at[me], send_sem=send_far.at[k], recv_sem=recv_far.at[k],
            device_id=(far[k - 1], col), device_id_type=mesh_ids,
        )
        copy.start()
        outgoing.append(copy)
    forwards = []
    for k in range(1, n_chip):
        outgoing[k - 1].wait_recv()
        source = lax.rem(chip + n_chip - k, n_chip) * 2 + core
        forward = pltpu.make_async_remote_copy(
            src_ref=o_ref.at[source], dst_ref=o_ref.at[source], send_sem=send_fwd.at[k],
            recv_sem=recv_fwd.at[k], device_id=(sibling, col), device_id_type=mesh_ids,
        )
        forward.start()
        forwards.append(forward)
    local.wait()
    pair.wait()
    for copy in outgoing:
        copy.wait_send()
    for forward in forwards:
        forward.wait()


def row_gather(x, n_row):
    n_chip = n_row // 2
    return pl.pallas_call(
        functools.partial(_row_gather_kernel, n_row=n_row),
        out_shape=jax.ShapeDtypeStruct((n_row,) + x.shape, x.dtype),
        in_specs=[pl.BlockSpec(memory_space=pl.ANY)],
        out_specs=pl.BlockSpec(memory_space=pl.ANY),
        scratch_shapes=[
            pltpu.SemaphoreType.DMA((n_chip,)),
            pltpu.SemaphoreType.DMA((n_chip,)),
            pltpu.SemaphoreType.DMA,
            pltpu.SemaphoreType.DMA,
            pltpu.SemaphoreType.DMA((n_chip,)),
            pltpu.SemaphoreType.DMA((n_chip,)),
            pltpu.SemaphoreType.DMA,
        ],
        compiler_params=pltpu.CompilerParams(collective_id=0, has_side_effects=True),
    )(x)


def block_tables(q_seg, k_seg, q_start):
    n_q = q_seg.shape[0] // Q_BLOCK
    n_k = k_seg.shape[0] // K_BLOCK
    values = jnp.arange(-1, 2, dtype=jnp.int32)
    q_has = jnp.any(q_seg.reshape(n_q, Q_BLOCK, 1) == values, axis=1).astype(jnp.float32)
    k_has = jnp.any(k_seg.reshape(n_k, K_BLOCK, 1) == values, axis=1).astype(jnp.float32)
    shared = jnp.dot(q_has, k_has.T) > 0
    single = (jnp.sum(q_has, axis=1)[:, None] == 1) & (jnp.sum(k_has, axis=1)[None, :] == 1)
    diag = (q_start + jnp.arange(n_q, dtype=jnp.int32) * Q_BLOCK) // K_BLOCK
    order = (diag[:, None] + jnp.arange(n_k, dtype=jnp.int32)[None, :]) % n_k
    need = jnp.take_along_axis(shared, order, axis=1)
    full = jnp.take_along_axis(single, order, axis=1)
    rank = jnp.cumsum(need.astype(jnp.int32), axis=1) - 1
    count = jnp.sum(need.astype(jnp.int32), axis=1)
    pos = jnp.where(need, rank, n_k + jnp.arange(n_k)[None, :])
    perm = jnp.argsort(pos, axis=1)
    kb_sorted = jnp.take_along_axis(order, perm, axis=1)
    full_sorted = jnp.take_along_axis(full, perm, axis=1)
    step = jnp.arange(n_k, dtype=jnp.int32)[None, :]
    live = step < count[:, None]
    last = jnp.take_along_axis(kb_sorted, (count - 1)[:, None], axis=1)
    kb_map = jnp.where(live, kb_sorted, last).astype(jnp.int32)
    flags = jnp.where(live, jnp.where(full_sorted, 2, 1), 0).astype(jnp.int32)
    return kb_map, flags


def attention(q_t, q_seg_f, kv, kb_map, flags, scale, interpret=False):
    n_tok = q_t.shape[0]
    per_peer = kv.shape[3] // K_BLOCK
    n_keys = kv.shape[0] * kv.shape[3]
    n_q = n_tok // Q_BLOCK
    n_k = n_keys // K_BLOCK
    kernel = functools.partial(_attn_kernel, scale=scale, n_steps=n_k)
    grid_spec = pltpu.PrefetchScalarGridSpec(
        num_scalar_prefetch=2,
        grid=(n_q, n_k),
        in_specs=[
            pl.BlockSpec((Q_BLOCK, PADW), lambda i, j, km, fl: (i, 0)),
            pl.BlockSpec((Q_BLOCK, 1), lambda i, j, km, fl: (i, 0)),
            pl.BlockSpec((None, None, PADW, K_BLOCK), lambda i, j, km, fl: (km[i, j] // per_peer, 0, 0, km[i, j] % per_peer)),
            pl.BlockSpec((None, None, PADW, K_BLOCK), lambda i, j, km, fl: (km[i, j] // per_peer, 1, 0, km[i, j] % per_peer)),
        ],
        out_specs=pl.BlockSpec((Q_BLOCK, PADW), lambda i, j, km, fl: (i, 0)),
        scratch_shapes=[
            pltpu.VMEM((Q_BLOCK, 1), jnp.float32),
            pltpu.VMEM((Q_BLOCK, 1), jnp.float32),
            pltpu.VMEM((Q_BLOCK, PADW), jnp.float32),
        ],
    )
    return pl.pallas_call(
        kernel,
        grid_spec=grid_spec,
        out_shape=jax.ShapeDtypeStruct((n_tok, PADW), jnp.bfloat16),
        compiler_params=pltpu.CompilerParams(dimension_semantics=("arbitrary", "arbitrary")),
        interpret=interpret,
    )(kb_map, flags, q_t, q_seg_f, kv, kv)


def on_device(
    n_row,
    hidden,
    gain_in,
    w_query,
    w_pair,
    kv_cache,
    recompute_rows,
    segment_ids,
    w_out,
    gain_merge,
    w_merge,
    requests,
):
    local_width, tok_rows = hidden.shape
    model_width = w_query.shape[1]
    n_col = model_width // local_width
    heads_here = local_width // HD
    score_scale = HD ** (-0.5)
    col_index = lax.axis_index("col")
    gathered_rows = lax.all_gather(hidden, "col", axis=0, tiled=True)
    picked_rows = recompute_rows[0]
    hidden_picked = jnp.take(hidden, picked_rows, axis=1)
    picked_copies = jnp.broadcast_to(hidden_picked[None], (n_col,) + hidden_picked.shape)
    picked_full = lax.all_to_all(picked_copies, "col", 0, 0, tiled=True)
    picked_float = picked_full.reshape(model_width, -1).astype(jnp.float32)
    picked_mean = jnp.sum(picked_float, axis=0, keepdims=True) / model_width
    picked_square = jnp.sum(picked_float * picked_float, axis=0, keepdims=True) / model_width
    normed_picked = (
        (picked_float - picked_mean)
        * lax.rsqrt(picked_square - picked_mean * picked_mean + EPSILON)
        * gain_in.astype(jnp.float32)[:, None]
    ).astype(jnp.bfloat16)
    fresh_pairs = jnp.dot(
        w_pair.reshape(2 * local_width, model_width),
        normed_picked,
        preferred_element_type=jnp.float32,
    )
    fresh_pairs = fresh_pairs.astype(jnp.bfloat16).reshape(2, local_width, -1)
    keys_values = kv_cache.at[:, :, picked_rows].set(fresh_pairs)

    pair_local = jnp.pad(keys_values, ((0, 0), (0, PADW - HD), (0, 0)))
    pair_local = pair_local.at[0, HD].set(segment_ids.astype(jnp.bfloat16))
    pair_all = row_gather(pair_local, n_row)
    full_rows, pair_all = lax.optimization_barrier((gathered_rows, pair_all))
    full_float = full_rows.astype(jnp.float32)
    in_mean = jnp.sum(full_float, axis=0, keepdims=True) / model_width
    in_square = jnp.sum(full_float * full_float, axis=0, keepdims=True) / model_width
    normed = (
        (full_float - in_mean)
        * lax.rsqrt(in_square - in_mean * in_mean + EPSILON)
        * gain_in.astype(jnp.float32)[:, None]
    ).astype(jnp.bfloat16)
    query_rows = lax.dot_general(
        normed, w_query, (((0,), (1,)), ((), ())), preferred_element_type=jnp.float32
    ).astype(jnp.bfloat16)
    query_rows = jnp.pad(query_rows, ((0, 0), (0, PADW - HD)))
    segment_line = pair_all[:, 0, HD].reshape(-1).astype(jnp.int32)
    weight_stack = jnp.concatenate([w_out[None], w_merge], axis=0)
    weight_stack, _ = lax.optimization_barrier((weight_stack, full_rows))
    weights_full = lax.all_gather(weight_stack, "col", axis=1, tiled=True)
    out_weight = weights_full[0]
    merge_full = weights_full[1:]
    kb_map, flags = block_tables(segment_ids, segment_line, lax.axis_index("row") * tok_rows)
    attended_rows = attention(
        query_rows, segment_ids.astype(jnp.float32)[:, None], pair_all, kb_map, flags, score_scale
    )
    attended = attended_rows[:, :HD].T
    chunk = tok_rows // n_col
    attended_chunk = lax.all_to_all(attended, "col", 1, 0, tiled=True)
    x_chunk = lax.dynamic_slice_in_dim(full_float, col_index * chunk, chunk, 1)
    projected = lax.dot_general(
        out_weight, attended_chunk, (((0,), (0,)), ((), ())), preferred_element_type=jnp.float32
    )
    updated = x_chunk + projected
    row_mean = jnp.sum(updated, axis=0, keepdims=True) / model_width
    row_square = jnp.sum(updated * updated, axis=0, keepdims=True) / model_width
    merger_chunk = (
        (updated - row_mean)
        * lax.rsqrt(row_square - row_mean * row_mean + EPSILON)
        * gain_merge.astype(jnp.float32)[:, None]
    ).astype(jnp.bfloat16)
    grouped = merger_chunk.reshape(model_width, chunk // 4, 4)
    merged_here = jnp.einsum("fgi,ifd->gd", grouped, merge_full, preferred_element_type=jnp.float32)
    merged_all = lax.all_gather(merged_here.astype(jnp.bfloat16), "col", axis=0, tiled=True)
    wanted_rows = lax.dynamic_index_in_dim(requests[0], col_index, 0, keepdims=False)
    is_valid = wanted_rows >= 0
    safe_index = jnp.where(is_valid, wanted_rows, 0)
    picked = jnp.where(is_valid[:, None], merged_all[safe_index], jnp.zeros((), jnp.bfloat16))
    return picked.reshape(1, 1, picked.shape[0], model_width)


def solution(mesh):
    placed = (
        P("col", "row"),
        P(),
        P("col", None),
        P(None, "col", None),
        P(None, "col", "row"),
        P("row", None),
        P("row"),
        P("col", None),
        P(),
        P(None, "col", None),
        P("row", None, None),
    )
    return jax.shard_map(
        functools.partial(on_device, mesh.shape["row"]),
        mesh=mesh,
        in_specs=placed,
        out_specs=P("row", "col", None, None),
        check_vma=False,
    )
```

```python
import jax
import jax.numpy as jnp
from jax import lax
import functools
from jax.experimental import pallas as pl
from jax.experimental.pallas import tpu as pltpu
from jax.sharding import PartitionSpec as P

HD = 88


EPSILON = 1e-06
MASKED = -1e30
PADW = 96
Q_BLOCK = 512
K_BLOCK = 1024


def _attn_kernel(kb_map, flags, q_ref, qs_ref, k_ref, v_ref, o_ref, m_ref, l_ref, acc_ref, *, scale, n_steps):
    qb = pl.program_id(0)
    j = pl.program_id(1)
    flag = flags[qb, j]

    @pl.when(j == 0)
    def _():
        m_ref[...] = jnp.full(m_ref.shape, MASKED, jnp.float32)
        l_ref[...] = jnp.zeros(l_ref.shape, jnp.float32)
        acc_ref[...] = jnp.zeros(acc_ref.shape, jnp.float32)

    def step(masked):
        q = q_ref[...]
        k = k_ref[...]
        s = jnp.dot(q, k, preferred_element_type=jnp.float32) * scale
        if masked:
            key_seg = k[HD:HD + 1, :].astype(jnp.float32)
            s = jnp.where(qs_ref[...] == key_seg, s, MASKED)
        m_prev = m_ref[...]
        m_new = jnp.maximum(m_prev, jnp.max(s, axis=1, keepdims=True))
        p = jnp.exp(s - m_new)
        alpha = jnp.exp(m_prev - m_new)
        l_ref[...] = alpha * l_ref[...] + jnp.sum(p, axis=1, keepdims=True)
        pv = lax.dot_general(
            p.astype(jnp.bfloat16), v_ref[...], (((1,), (1,)), ((), ())),
            preferred_element_type=jnp.float32,
        )
        acc_ref[...] = alpha * acc_ref[...] + pv
        m_ref[...] = m_new

    @pl.when(flag == 1)
    def _():
        step(True)

    @pl.when(flag == 2)
    def _():
        step(False)

    @pl.when(j == n_steps - 1)
    def _():
        o_ref[...] = (acc_ref[...] / l_ref[...]).astype(o_ref.dtype)


def _row_gather_kernel(x_ref, o_ref, send_far, recv_far, send_pair, recv_pair, send_fwd, recv_fwd, local_sem, *, n_row):
    mesh_ids = pl.DeviceIdType.MESH
    n_chip = n_row // 2
    me = lax.axis_index("row")
    col = lax.axis_index("col")
    chip = me // 2
    core = me % 2
    sibling = chip * 2 + 1 - core
    far = [lax.rem(chip + k, n_chip) * 2 + core for k in range(1, n_chip)]
    barrier = pltpu.get_barrier_semaphore()
    for peer in far + [sibling]:
        pl.semaphore_signal(barrier, inc=1, device_id=(peer, col), device_id_type=mesh_ids)
    pl.semaphore_wait(barrier, n_chip)
    local = pltpu.make_async_copy(x_ref, o_ref.at[me], local_sem)
    local.start()
    pair = pltpu.make_async_remote_copy(
        src_ref=x_ref, dst_ref=o_ref.at[me], send_sem=send_pair, recv_sem=recv_pair,
        device_id=(sibling, col), device_id_type=mesh_ids,
    )
    pair.start()
    outgoing = []
    for k in range(1, n_chip):
        copy = pltpu.make_async_remote_copy(
            src_ref=x_ref, dst_ref=o_ref.at[me], send_sem=send_far.at[k], recv_sem=recv_far.at[k],
            device_id=(far[k - 1], col), device_id_type=mesh_ids,
        )
        copy.start()
        outgoing.append(copy)
    forwards = []
    for k in range(1, n_chip):
        outgoing[k - 1].wait_recv()
        source = lax.rem(chip + n_chip - k, n_chip) * 2 + core
        forward = pltpu.make_async_remote_copy(
            src_ref=o_ref.at[source], dst_ref=o_ref.at[source], send_sem=send_fwd.at[k],
            recv_sem=recv_fwd.at[k], device_id=(sibling, col), device_id_type=mesh_ids,
        )
        forward.start()
        forwards.append(forward)
    local.wait()
    pair.wait()
    for copy in outgoing:
        copy.wait_send()
    for forward in forwards:
        forward.wait()


def row_gather(x, n_row):
    n_chip = n_row // 2
    return pl.pallas_call(
        functools.partial(_row_gather_kernel, n_row=n_row),
        out_shape=jax.ShapeDtypeStruct((n_row,) + x.shape, x.dtype),
        in_specs=[pl.BlockSpec(memory_space=pl.ANY)],
        out_specs=pl.BlockSpec(memory_space=pl.ANY),
        scratch_shapes=[
            pltpu.SemaphoreType.DMA((n_chip,)),
            pltpu.SemaphoreType.DMA((n_chip,)),
            pltpu.SemaphoreType.DMA,
            pltpu.SemaphoreType.DMA,
            pltpu.SemaphoreType.DMA((n_chip,)),
            pltpu.SemaphoreType.DMA((n_chip,)),
            pltpu.SemaphoreType.DMA,
        ],
        compiler_params=pltpu.CompilerParams(collective_id=0, has_side_effects=True),
    )(x)


def _col_gather_kernel(x_ref, o_ref, send_sems, recv_sems, local_sem, *, n_col):
    mesh_ids = pl.DeviceIdType.MESH
    me = lax.axis_index("col")
    row = lax.axis_index("row")
    barrier = pltpu.get_barrier_semaphore()
    for k in range(1, n_col):
        peer = lax.rem(me + k, n_col)
        pl.semaphore_signal(barrier, inc=1, device_id=(row, peer), device_id_type=mesh_ids)
    pl.semaphore_wait(barrier, n_col - 1)
    local = pltpu.make_async_copy(x_ref, o_ref.at[me], local_sem)
    local.start()
    copies = []
    for k in range(1, n_col):
        peer = lax.rem(me + k, n_col)
        copy = pltpu.make_async_remote_copy(
            src_ref=x_ref, dst_ref=o_ref.at[me], send_sem=send_sems.at[k], recv_sem=recv_sems.at[k],
            device_id=(row, peer), device_id_type=mesh_ids,
        )
        copy.start()
        copies.append(copy)
    local.wait()
    for copy in copies:
        copy.wait()


def col_gather(x, n_col):
    return pl.pallas_call(
        functools.partial(_col_gather_kernel, n_col=n_col),
        out_shape=jax.ShapeDtypeStruct((n_col,) + x.shape, x.dtype),
        in_specs=[pl.BlockSpec(memory_space=pl.ANY)],
        out_specs=pl.BlockSpec(memory_space=pl.ANY),
        scratch_shapes=[
            pltpu.SemaphoreType.DMA((n_col,)),
            pltpu.SemaphoreType.DMA((n_col,)),
            pltpu.SemaphoreType.DMA,
        ],
        compiler_params=pltpu.CompilerParams(collective_id=1, has_side_effects=True),
    )(x)


def block_tables(q_seg, k_seg, q_start):
    n_q = q_seg.shape[0] // Q_BLOCK
    n_k = k_seg.shape[0] // K_BLOCK
    values = jnp.arange(-1, 2, dtype=jnp.int32)
    q_has = jnp.any(q_seg.reshape(n_q, Q_BLOCK, 1) == values, axis=1).astype(jnp.float32)
    k_has = jnp.any(k_seg.reshape(n_k, K_BLOCK, 1) == values, axis=1).astype(jnp.float32)
    shared = jnp.dot(q_has, k_has.T) > 0
    single = (jnp.sum(q_has, axis=1)[:, None] == 1) & (jnp.sum(k_has, axis=1)[None, :] == 1)
    diag = (q_start + jnp.arange(n_q, dtype=jnp.int32) * Q_BLOCK) // K_BLOCK
    order = (diag[:, None] + jnp.arange(n_k, dtype=jnp.int32)[None, :]) % n_k
    need = jnp.take_along_axis(shared, order, axis=1)
    full = jnp.take_along_axis(single, order, axis=1)
    rank = jnp.cumsum(need.astype(jnp.int32), axis=1) - 1
    count = jnp.sum(need.astype(jnp.int32), axis=1)
    pos = jnp.where(need, rank, n_k + jnp.arange(n_k)[None, :])
    perm = jnp.argsort(pos, axis=1)
    kb_sorted = jnp.take_along_axis(order, perm, axis=1)
    full_sorted = jnp.take_along_axis(full, perm, axis=1)
    step = jnp.arange(n_k, dtype=jnp.int32)[None, :]
    live = step < count[:, None]
    last = jnp.take_along_axis(kb_sorted, (count - 1)[:, None], axis=1)
    kb_map = jnp.where(live, kb_sorted, last).astype(jnp.int32)
    flags = jnp.where(live, jnp.where(full_sorted, 2, 1), 0).astype(jnp.int32)
    return kb_map, flags


def attention(q_t, q_seg_f, kv, kb_map, flags, scale, interpret=False):
    n_tok = q_t.shape[0]
    per_peer = kv.shape[3] // K_BLOCK
    n_keys = kv.shape[0] * kv.shape[3]
    n_q = n_tok // Q_BLOCK
    n_k = n_keys // K_BLOCK
    kernel = functools.partial(_attn_kernel, scale=scale, n_steps=n_k)
    grid_spec = pltpu.PrefetchScalarGridSpec(
        num_scalar_prefetch=2,
        grid=(n_q, n_k),
        in_specs=[
            pl.BlockSpec((Q_BLOCK, PADW), lambda i, j, km, fl: (i, 0)),
            pl.BlockSpec((Q_BLOCK, 1), lambda i, j, km, fl: (i, 0)),
            pl.BlockSpec((None, None, PADW, K_BLOCK), lambda i, j, km, fl: (km[i, j] // per_peer, 0, 0, km[i, j] % per_peer)),
            pl.BlockSpec((None, None, PADW, K_BLOCK), lambda i, j, km, fl: (km[i, j] // per_peer, 1, 0, km[i, j] % per_peer)),
        ],
        out_specs=pl.BlockSpec((Q_BLOCK, PADW), lambda i, j, km, fl: (i, 0)),
        scratch_shapes=[
            pltpu.VMEM((Q_BLOCK, 1), jnp.float32),
            pltpu.VMEM((Q_BLOCK, 1), jnp.float32),
            pltpu.VMEM((Q_BLOCK, PADW), jnp.float32),
        ],
    )
    return pl.pallas_call(
        kernel,
        grid_spec=grid_spec,
        out_shape=jax.ShapeDtypeStruct((n_tok, PADW), jnp.bfloat16),
        compiler_params=pltpu.CompilerParams(dimension_semantics=("arbitrary", "arbitrary")),
        interpret=interpret,
    )(kb_map, flags, q_t, q_seg_f, kv, kv)


def on_device(
    n_row,
    hidden,
    gain_in,
    w_query,
    w_pair,
    kv_cache,
    recompute_rows,
    segment_ids,
    w_out,
    gain_merge,
    w_merge,
    requests,
):
    local_width, tok_rows = hidden.shape
    model_width = w_query.shape[1]
    n_col = model_width // local_width
    heads_here = local_width // HD
    score_scale = HD ** (-0.5)
    col_index = lax.axis_index("col")
    gathered_rows = lax.all_gather(hidden, "col", axis=0, tiled=True)
    picked_rows = recompute_rows[0]
    hidden_picked = jnp.take(hidden, picked_rows, axis=1)
    picked_copies = jnp.broadcast_to(hidden_picked[None], (n_col,) + hidden_picked.shape)
    picked_full = lax.all_to_all(picked_copies, "col", 0, 0, tiled=True)
    picked_float = picked_full.reshape(model_width, -1).astype(jnp.float32)
    picked_mean = jnp.sum(picked_float, axis=0, keepdims=True) / model_width
    picked_square = jnp.sum(picked_float * picked_float, axis=0, keepdims=True) / model_width
    normed_picked = (
        (picked_float - picked_mean)
        * lax.rsqrt(picked_square - picked_mean * picked_mean + EPSILON)
        * gain_in.astype(jnp.float32)[:, None]
    ).astype(jnp.bfloat16)
    fresh_pairs = jnp.dot(
        w_pair.reshape(2 * local_width, model_width),
        normed_picked,
        preferred_element_type=jnp.float32,
    )
    fresh_pairs = fresh_pairs.astype(jnp.bfloat16).reshape(2, local_width, -1)
    keys_values = kv_cache.at[:, :, picked_rows].set(fresh_pairs)

    pair_local = jnp.pad(keys_values, ((0, 0), (0, PADW - HD), (0, 0)))
    pair_local = pair_local.at[0, HD].set(segment_ids.astype(jnp.bfloat16))
    pair_all = row_gather(pair_local, n_row)
    full_rows, pair_all = lax.optimization_barrier((gathered_rows, pair_all))
    full_float = full_rows.astype(jnp.float32)
    in_mean = jnp.sum(full_float, axis=0, keepdims=True) / model_width
    in_square = jnp.sum(full_float * full_float, axis=0, keepdims=True) / model_width
    normed = (
        (full_float - in_mean)
        * lax.rsqrt(in_square - in_mean * in_mean + EPSILON)
        * gain_in.astype(jnp.float32)[:, None]
    ).astype(jnp.bfloat16)
    query_rows = lax.dot_general(
        normed, w_query, (((0,), (1,)), ((), ())), preferred_element_type=jnp.float32
    ).astype(jnp.bfloat16)
    query_rows = jnp.pad(query_rows, ((0, 0), (0, PADW - HD)))
    segment_line = pair_all[:, 0, HD].reshape(-1).astype(jnp.int32)
    weight_stack = jnp.concatenate([w_out[None], w_merge], axis=0)
    weight_stack, _ = lax.optimization_barrier((weight_stack, full_rows))
    weights_full = lax.all_gather(weight_stack, "col", axis=1, tiled=True)
    out_weight = weights_full[0]
    merge_full = weights_full[1:]
    kb_map, flags = block_tables(segment_ids, segment_line, lax.axis_index("row") * tok_rows)
    attended_rows = attention(
        query_rows, segment_ids.astype(jnp.float32)[:, None], pair_all, kb_map, flags, score_scale
    )
    attended = attended_rows[:, :HD].T
    chunk = tok_rows // n_col
    attended_chunk = lax.all_to_all(attended, "col", 1, 0, tiled=True)
    x_chunk = lax.dynamic_slice_in_dim(full_rows, col_index * chunk, chunk, 1).astype(jnp.float32)
    projected = lax.dot_general(
        out_weight, attended_chunk, (((0,), (0,)), ((), ())), preferred_element_type=jnp.float32
    )
    updated = x_chunk + projected
    row_mean = jnp.sum(updated, axis=0, keepdims=True) / model_width
    row_square = jnp.sum(updated * updated, axis=0, keepdims=True) / model_width
    merger_chunk = (
        (updated - row_mean)
        * lax.rsqrt(row_square - row_mean * row_mean + EPSILON)
        * gain_merge.astype(jnp.float32)[:, None]
    ).astype(jnp.bfloat16)
    grouped = merger_chunk.reshape(model_width, chunk // 4, 4)
    merged_here = jnp.einsum("fgi,ifd->gd", grouped, merge_full, preferred_element_type=jnp.float32)
    merged_all = col_gather(merged_here.astype(jnp.bfloat16), n_col).reshape(-1, model_width)
    wanted_rows = lax.dynamic_index_in_dim(requests[0], col_index, 0, keepdims=False)
    is_valid = wanted_rows >= 0
    safe_index = jnp.where(is_valid, wanted_rows, 0)
    picked = jnp.where(is_valid[:, None], merged_all[safe_index], jnp.zeros((), jnp.bfloat16))
    return picked.reshape(1, 1, picked.shape[0], model_width)


def solution(mesh):
    placed = (
        P("col", "row"),
        P(),
        P("col", None),
        P(None, "col", None),
        P(None, "col", "row"),
        P("row", None),
        P("row"),
        P("col", None),
        P(),
        P(None, "col", None),
        P("row", None, None),
    )
    return jax.shard_map(
        functools.partial(on_device, mesh.shape["row"]),
        mesh=mesh,
        in_specs=placed,
        out_specs=P("row", "col", None, None),
        check_vma=False,
    )
```

```python
import jax
import jax.numpy as jnp
from jax import lax
import functools
from jax.experimental import pallas as pl
from jax.experimental.pallas import tpu as pltpu
from jax.sharding import PartitionSpec as P

HD = 88


EPSILON = 1e-06
MASKED = -1e30
PADW = 96
Q_BLOCK = 1024
K_BLOCK = 2048


def _attn_kernel(kb_map, flags, q_ref, qs_ref, k_ref, v_ref, o_ref, m_ref, l_ref, acc_ref, *, scale, n_steps):
    qb = pl.program_id(0)
    j = pl.program_id(1)
    flag = flags[qb, j]

    @pl.when(j == 0)
    def _():
        m_ref[...] = jnp.full(m_ref.shape, MASKED, jnp.float32)
        l_ref[...] = jnp.zeros(l_ref.shape, jnp.float32)
        acc_ref[...] = jnp.zeros(acc_ref.shape, jnp.float32)

    def step(masked):
        q = q_ref[...]
        k = k_ref[...]
        s = jnp.dot(q, k, preferred_element_type=jnp.float32) * scale
        if masked:
            key_seg = k[HD:HD + 1, :].astype(jnp.float32)
            s = jnp.where(qs_ref[...] == key_seg, s, MASKED)
        m_prev = m_ref[...]
        m_new = jnp.maximum(m_prev, jnp.max(s, axis=1, keepdims=True))
        p = jnp.exp(s - m_new)
        alpha = jnp.exp(m_prev - m_new)
        l_ref[...] = alpha * l_ref[...] + jnp.sum(p, axis=1, keepdims=True)
        pv = lax.dot_general(
            p.astype(jnp.bfloat16), v_ref[...], (((1,), (1,)), ((), ())),
            preferred_element_type=jnp.float32,
        )
        acc_ref[...] = alpha * acc_ref[...] + pv
        m_ref[...] = m_new

    @pl.when(flag == 1)
    def _():
        step(True)

    @pl.when(flag == 2)
    def _():
        step(False)

    @pl.when(j == n_steps - 1)
    def _():
        o_ref[...] = (acc_ref[...] / l_ref[...]).astype(o_ref.dtype)


def _row_gather_kernel(x_ref, o_ref, send_far, recv_far, send_pair, recv_pair, send_fwd, recv_fwd, local_sem, *, n_row):
    mesh_ids = pl.DeviceIdType.MESH
    n_chip = n_row // 2
    me = lax.axis_index("row")
    col = lax.axis_index("col")
    chip = me // 2
    core = me % 2
    sibling = chip * 2 + 1 - core
    far = [lax.rem(chip + k, n_chip) * 2 + core for k in range(1, n_chip)]
    barrier = pltpu.get_barrier_semaphore()
    for peer in far + [sibling]:
        pl.semaphore_signal(barrier, inc=1, device_id=(peer, col), device_id_type=mesh_ids)
    pl.semaphore_wait(barrier, n_chip)
    local = pltpu.make_async_copy(x_ref, o_ref.at[me], local_sem)
    local.start()
    pair = pltpu.make_async_remote_copy(
        src_ref=x_ref, dst_ref=o_ref.at[me], send_sem=send_pair, recv_sem=recv_pair,
        device_id=(sibling, col), device_id_type=mesh_ids,
    )
    pair.start()
    outgoing = []
    for k in range(1, n_chip):
        copy = pltpu.make_async_remote_copy(
            src_ref=x_ref, dst_ref=o_ref.at[me], send_sem=send_far.at[k], recv_sem=recv_far.at[k],
            device_id=(far[k - 1], col), device_id_type=mesh_ids,
        )
        copy.start()
        outgoing.append(copy)
    forwards = []
    for k in range(1, n_chip):
        outgoing[k - 1].wait_recv()
        source = lax.rem(chip + n_chip - k, n_chip) * 2 + core
        forward = pltpu.make_async_remote_copy(
            src_ref=o_ref.at[source], dst_ref=o_ref.at[source], send_sem=send_fwd.at[k],
            recv_sem=recv_fwd.at[k], device_id=(sibling, col), device_id_type=mesh_ids,
        )
        forward.start()
        forwards.append(forward)
    local.wait()
    pair.wait()
    for copy in outgoing:
        copy.wait_send()
    for forward in forwards:
        forward.wait()


def row_gather(x, n_row):
    n_chip = n_row // 2
    return pl.pallas_call(
        functools.partial(_row_gather_kernel, n_row=n_row),
        out_shape=jax.ShapeDtypeStruct((n_row,) + x.shape, x.dtype),
        in_specs=[pl.BlockSpec(memory_space=pl.ANY)],
        out_specs=pl.BlockSpec(memory_space=pl.ANY),
        scratch_shapes=[
            pltpu.SemaphoreType.DMA((n_chip,)),
            pltpu.SemaphoreType.DMA((n_chip,)),
            pltpu.SemaphoreType.DMA,
            pltpu.SemaphoreType.DMA,
            pltpu.SemaphoreType.DMA((n_chip,)),
            pltpu.SemaphoreType.DMA((n_chip,)),
            pltpu.SemaphoreType.DMA,
        ],
        compiler_params=pltpu.CompilerParams(collective_id=0, has_side_effects=True),
    )(x)


def _col_gather_kernel(x_ref, o_ref, send_sems, recv_sems, local_sem, *, n_col):
    mesh_ids = pl.DeviceIdType.MESH
    me = lax.axis_index("col")
    row = lax.axis_index("row")
    barrier = pltpu.get_barrier_semaphore()
    for k in range(1, n_col):
        peer = lax.rem(me + k, n_col)
        pl.semaphore_signal(barrier, inc=1, device_id=(row, peer), device_id_type=mesh_ids)
    pl.semaphore_wait(barrier, n_col - 1)
    local = pltpu.make_async_copy(x_ref, o_ref.at[me], local_sem)
    local.start()
    copies = []
    for k in range(1, n_col):
        peer = lax.rem(me + k, n_col)
        copy = pltpu.make_async_remote_copy(
            src_ref=x_ref, dst_ref=o_ref.at[me], send_sem=send_sems.at[k], recv_sem=recv_sems.at[k],
            device_id=(row, peer), device_id_type=mesh_ids,
        )
        copy.start()
        copies.append(copy)
    local.wait()
    for copy in copies:
        copy.wait()


def col_gather(x, n_col):
    return pl.pallas_call(
        functools.partial(_col_gather_kernel, n_col=n_col),
        out_shape=jax.ShapeDtypeStruct((n_col,) + x.shape, x.dtype),
        in_specs=[pl.BlockSpec(memory_space=pl.ANY)],
        out_specs=pl.BlockSpec(memory_space=pl.ANY),
        scratch_shapes=[
            pltpu.SemaphoreType.DMA((n_col,)),
            pltpu.SemaphoreType.DMA((n_col,)),
            pltpu.SemaphoreType.DMA,
        ],
        compiler_params=pltpu.CompilerParams(collective_id=1, has_side_effects=True),
    )(x)


def block_tables(q_seg, k_seg, q_start):
    n_q = q_seg.shape[0] // Q_BLOCK
    n_k = k_seg.shape[0] // K_BLOCK
    values = jnp.arange(-1, 2, dtype=jnp.int32)
    q_has = jnp.any(q_seg.reshape(n_q, Q_BLOCK, 1) == values, axis=1).astype(jnp.float32)
    k_has = jnp.any(k_seg.reshape(n_k, K_BLOCK, 1) == values, axis=1).astype(jnp.float32)
    shared = jnp.dot(q_has, k_has.T) > 0
    single = (jnp.sum(q_has, axis=1)[:, None] == 1) & (jnp.sum(k_has, axis=1)[None, :] == 1)
    diag = (q_start + jnp.arange(n_q, dtype=jnp.int32) * Q_BLOCK) // K_BLOCK
    order = (diag[:, None] + jnp.arange(n_k, dtype=jnp.int32)[None, :]) % n_k
    need = jnp.take_along_axis(shared, order, axis=1)
    full = jnp.take_along_axis(single, order, axis=1)
    rank = jnp.cumsum(need.astype(jnp.int32), axis=1) - 1
    count = jnp.sum(need.astype(jnp.int32), axis=1)
    pos = jnp.where(need, rank, n_k + jnp.arange(n_k)[None, :])
    perm = jnp.argsort(pos, axis=1)
    kb_sorted = jnp.take_along_axis(order, perm, axis=1)
    full_sorted = jnp.take_along_axis(full, perm, axis=1)
    step = jnp.arange(n_k, dtype=jnp.int32)[None, :]
    live = step < count[:, None]
    last = jnp.take_along_axis(kb_sorted, (count - 1)[:, None], axis=1)
    kb_map = jnp.where(live, kb_sorted, last).astype(jnp.int32)
    flags = jnp.where(live, jnp.where(full_sorted, 2, 1), 0).astype(jnp.int32)
    return kb_map, flags


def attention(q_t, q_seg_f, kv, kb_map, flags, scale, interpret=False):
    n_tok = q_t.shape[0]
    per_peer = kv.shape[3] // K_BLOCK
    n_keys = kv.shape[0] * kv.shape[3]
    n_q = n_tok // Q_BLOCK
    n_k = n_keys // K_BLOCK
    kernel = functools.partial(_attn_kernel, scale=scale, n_steps=n_k)
    grid_spec = pltpu.PrefetchScalarGridSpec(
        num_scalar_prefetch=2,
        grid=(n_q, n_k),
        in_specs=[
            pl.BlockSpec((Q_BLOCK, PADW), lambda i, j, km, fl: (i, 0)),
            pl.BlockSpec((Q_BLOCK, 1), lambda i, j, km, fl: (i, 0)),
            pl.BlockSpec((None, None, PADW, K_BLOCK), lambda i, j, km, fl: (km[i, j] // per_peer, 0, 0, km[i, j] % per_peer)),
            pl.BlockSpec((None, None, PADW, K_BLOCK), lambda i, j, km, fl: (km[i, j] // per_peer, 1, 0, km[i, j] % per_peer)),
        ],
        out_specs=pl.BlockSpec((Q_BLOCK, PADW), lambda i, j, km, fl: (i, 0)),
        scratch_shapes=[
            pltpu.VMEM((Q_BLOCK, 1), jnp.float32),
            pltpu.VMEM((Q_BLOCK, 1), jnp.float32),
            pltpu.VMEM((Q_BLOCK, PADW), jnp.float32),
        ],
    )
    return pl.pallas_call(
        kernel,
        grid_spec=grid_spec,
        out_shape=jax.ShapeDtypeStruct((n_tok, PADW), jnp.bfloat16),
        compiler_params=pltpu.CompilerParams(dimension_semantics=("arbitrary", "arbitrary")),
        interpret=interpret,
    )(kb_map, flags, q_t, q_seg_f, kv, kv)


def on_device(
    n_row,
    hidden,
    gain_in,
    w_query,
    w_pair,
    kv_cache,
    recompute_rows,
    segment_ids,
    w_out,
    gain_merge,
    w_merge,
    requests,
):
    local_width, tok_rows = hidden.shape
    model_width = w_query.shape[1]
    n_col = model_width // local_width
    heads_here = local_width // HD
    score_scale = HD ** (-0.5)
    col_index = lax.axis_index("col")
    gathered_rows = lax.all_gather(hidden, "col", axis=0, tiled=True)
    picked_rows = recompute_rows[0]
    hidden_picked = jnp.take(hidden, picked_rows, axis=1)
    picked_copies = jnp.broadcast_to(hidden_picked[None], (n_col,) + hidden_picked.shape)
    picked_full = lax.all_to_all(picked_copies, "col", 0, 0, tiled=True)
    picked_float = picked_full.reshape(model_width, -1).astype(jnp.float32)
    picked_mean = jnp.sum(picked_float, axis=0, keepdims=True) / model_width
    picked_square = jnp.sum(picked_float * picked_float, axis=0, keepdims=True) / model_width
    normed_picked = (
        (picked_float - picked_mean)
        * lax.rsqrt(picked_square - picked_mean * picked_mean + EPSILON)
        * gain_in.astype(jnp.float32)[:, None]
    ).astype(jnp.bfloat16)
    fresh_pairs = jnp.dot(
        w_pair.reshape(2 * local_width, model_width),
        normed_picked,
        preferred_element_type=jnp.float32,
    )
    fresh_pairs = fresh_pairs.astype(jnp.bfloat16).reshape(2, local_width, -1)
    keys_values = kv_cache.at[:, :, picked_rows].set(fresh_pairs)

    pair_local = jnp.pad(keys_values, ((0, 0), (0, PADW - HD), (0, 0)))
    pair_local = pair_local.at[0, HD].set(segment_ids.astype(jnp.bfloat16))
    pair_all = row_gather(pair_local, n_row)
    full_rows, pair_all = lax.optimization_barrier((gathered_rows, pair_all))
    full_float = full_rows.astype(jnp.float32)
    in_mean = jnp.sum(full_float, axis=0, keepdims=True) / model_width
    in_square = jnp.sum(full_float * full_float, axis=0, keepdims=True) / model_width
    normed = (
        (full_float - in_mean)
        * lax.rsqrt(in_square - in_mean * in_mean + EPSILON)
        * gain_in.astype(jnp.float32)[:, None]
    ).astype(jnp.bfloat16)
    query_rows = lax.dot_general(
        normed, w_query, (((0,), (1,)), ((), ())), preferred_element_type=jnp.float32
    ).astype(jnp.bfloat16)
    query_rows = jnp.pad(query_rows, ((0, 0), (0, PADW - HD)))
    segment_line = pair_all[:, 0, HD].reshape(-1).astype(jnp.int32)
    weight_stack = jnp.concatenate([w_out[None], w_merge], axis=0)
    weight_stack, _ = lax.optimization_barrier((weight_stack, full_rows))
    weights_full = lax.all_gather(weight_stack, "col", axis=1, tiled=True)
    out_weight = weights_full[0]
    merge_full = weights_full[1:]
    kb_map, flags = block_tables(segment_ids, segment_line, lax.axis_index("row") * tok_rows)
    attended_rows = attention(
        query_rows, segment_ids.astype(jnp.float32)[:, None], pair_all, kb_map, flags, score_scale
    )
    attended = attended_rows[:, :HD].T
    chunk = tok_rows // n_col
    attended_chunk = lax.all_to_all(attended, "col", 1, 0, tiled=True)
    x_chunk = lax.dynamic_slice_in_dim(full_rows, col_index * chunk, chunk, 1).astype(jnp.float32)
    projected = lax.dot_general(
        out_weight, attended_chunk, (((0,), (0,)), ((), ())), preferred_element_type=jnp.float32
    )
    updated = x_chunk + projected
    row_mean = jnp.sum(updated, axis=0, keepdims=True) / model_width
    row_square = jnp.sum(updated * updated, axis=0, keepdims=True) / model_width
    merger_chunk = (
        (updated - row_mean)
        * lax.rsqrt(row_square - row_mean * row_mean + EPSILON)
        * gain_merge.astype(jnp.float32)[:, None]
    ).astype(jnp.bfloat16)
    grouped = merger_chunk.reshape(model_width, chunk // 4, 4)
    merged_here = jnp.einsum("fgi,ifd->gd", grouped, merge_full, preferred_element_type=jnp.float32)
    merged_all = col_gather(merged_here.astype(jnp.bfloat16), n_col).reshape(-1, model_width)
    wanted_rows = lax.dynamic_index_in_dim(requests[0], col_index, 0, keepdims=False)
    is_valid = wanted_rows >= 0
    safe_index = jnp.where(is_valid, wanted_rows, 0)
    picked = jnp.where(is_valid[:, None], merged_all[safe_index], jnp.zeros((), jnp.bfloat16))
    return picked.reshape(1, 1, picked.shape[0], model_width)


def solution(mesh):
    placed = (
        P("col", "row"),
        P(),
        P("col", None),
        P(None, "col", None),
        P(None, "col", "row"),
        P("row", None),
        P("row"),
        P("col", None),
        P(),
        P(None, "col", None),
        P("row", None, None),
    )
    return jax.shard_map(
        functools.partial(on_device, mesh.shape["row"]),
        mesh=mesh,
        in_specs=placed,
        out_specs=P("row", "col", None, None),
        check_vma=False,
    )
```

```python
import jax
import jax.numpy as jnp
from jax import lax
import functools
from jax.experimental import pallas as pl
from jax.experimental.pallas import tpu as pltpu
from jax.sharding import PartitionSpec as P

HD = 88


EPSILON = 1e-06
MASKED = -1e30
PADW = 96
Q_BLOCK = 1024
K_BLOCK = 2048


def _attn_kernel(kb_map, flags, q_ref, qs_ref, k_ref, v_ref, o_ref, m_ref, l_ref, acc_ref, *, scale, n_steps):
    qb = pl.program_id(0)
    j = pl.program_id(1)
    flag = flags[qb, j]

    @pl.when(j == 0)
    def _():
        m_ref[...] = jnp.full(m_ref.shape, MASKED, jnp.float32)
        l_ref[...] = jnp.zeros(l_ref.shape, jnp.float32)
        acc_ref[...] = jnp.zeros(acc_ref.shape, jnp.float32)

    def step(masked):
        q = q_ref[...]
        k = k_ref[...]
        s = jnp.dot(q, k, preferred_element_type=jnp.float32) * scale
        if masked:
            key_seg = k[HD:HD + 1, :].astype(jnp.float32)
            s = jnp.where(qs_ref[...] == key_seg, s, MASKED)
        m_prev = m_ref[...]
        m_new = jnp.maximum(m_prev, jnp.max(s, axis=1, keepdims=True))
        p = jnp.exp(s - m_new)
        alpha = jnp.exp(m_prev - m_new)
        l_ref[...] = alpha * l_ref[...] + jnp.sum(p, axis=1, keepdims=True)
        pv = lax.dot_general(
            p.astype(jnp.bfloat16), v_ref[...], (((1,), (1,)), ((), ())),
            preferred_element_type=jnp.float32,
        )
        acc_ref[...] = alpha * acc_ref[...] + pv
        m_ref[...] = m_new

    @pl.when(flag == 1)
    def _():
        step(True)

    @pl.when(flag == 2)
    def _():
        step(False)

    @pl.when(j == n_steps - 1)
    def _():
        o_ref[...] = (acc_ref[...] / l_ref[...]).astype(o_ref.dtype)


def _row_gather_kernel(x_ref, o_ref, send_far, recv_far, send_pair, recv_pair, send_fwd, recv_fwd, local_sem, *, n_row):
    mesh_ids = pl.DeviceIdType.MESH
    n_chip = n_row // 2
    me = lax.axis_index("row")
    col = lax.axis_index("col")
    chip = me // 2
    core = me % 2
    sibling = chip * 2 + 1 - core
    far = [lax.rem(chip + k, n_chip) * 2 + core for k in range(1, n_chip)]
    barrier = pltpu.get_barrier_semaphore()
    for peer in far + [sibling]:
        pl.semaphore_signal(barrier, inc=1, device_id=(peer, col), device_id_type=mesh_ids)
    pl.semaphore_wait(barrier, n_chip)
    local = pltpu.make_async_copy(x_ref, o_ref.at[me], local_sem)
    local.start()
    pair = pltpu.make_async_remote_copy(
        src_ref=x_ref, dst_ref=o_ref.at[me], send_sem=send_pair, recv_sem=recv_pair,
        device_id=(sibling, col), device_id_type=mesh_ids,
    )
    pair.start()
    outgoing = []
    for k in range(1, n_chip):
        copy = pltpu.make_async_remote_copy(
            src_ref=x_ref, dst_ref=o_ref.at[me], send_sem=send_far.at[k], recv_sem=recv_far.at[k],
            device_id=(far[k - 1], col), device_id_type=mesh_ids,
        )
        copy.start()
        outgoing.append(copy)
    forwards = []
    for k in range(1, n_chip):
        outgoing[k - 1].wait_recv()
        source = lax.rem(chip + n_chip - k, n_chip) * 2 + core
        forward = pltpu.make_async_remote_copy(
            src_ref=o_ref.at[source], dst_ref=o_ref.at[source], send_sem=send_fwd.at[k],
            recv_sem=recv_fwd.at[k], device_id=(sibling, col), device_id_type=mesh_ids,
        )
        forward.start()
        forwards.append(forward)
    local.wait()
    pair.wait()
    for copy in outgoing:
        copy.wait_send()
    for forward in forwards:
        forward.wait()


def row_gather(x, n_row):
    n_chip = n_row // 2
    return pl.pallas_call(
        functools.partial(_row_gather_kernel, n_row=n_row),
        out_shape=jax.ShapeDtypeStruct((n_row,) + x.shape, x.dtype),
        in_specs=[pl.BlockSpec(memory_space=pl.ANY)],
        out_specs=pl.BlockSpec(memory_space=pl.ANY),
        scratch_shapes=[
            pltpu.SemaphoreType.DMA((n_chip,)),
            pltpu.SemaphoreType.DMA((n_chip,)),
            pltpu.SemaphoreType.DMA,
            pltpu.SemaphoreType.DMA,
            pltpu.SemaphoreType.DMA((n_chip,)),
            pltpu.SemaphoreType.DMA((n_chip,)),
            pltpu.SemaphoreType.DMA,
        ],
        compiler_params=pltpu.CompilerParams(collective_id=0, has_side_effects=True),
    )(x)


def _col_gather_kernel(x_ref, o_ref, send_sems, recv_sems, local_sem, *, n_col):
    mesh_ids = pl.DeviceIdType.MESH
    me = lax.axis_index("col")
    row = lax.axis_index("row")
    barrier = pltpu.get_barrier_semaphore()
    for k in range(1, n_col):
        peer = lax.rem(me + k, n_col)
        pl.semaphore_signal(barrier, inc=1, device_id=(row, peer), device_id_type=mesh_ids)
    pl.semaphore_wait(barrier, n_col - 1)
    local = pltpu.make_async_copy(x_ref, o_ref.at[me], local_sem)
    local.start()
    copies = []
    for k in range(1, n_col):
        peer = lax.rem(me + k, n_col)
        copy = pltpu.make_async_remote_copy(
            src_ref=x_ref, dst_ref=o_ref.at[me], send_sem=send_sems.at[k], recv_sem=recv_sems.at[k],
            device_id=(row, peer), device_id_type=mesh_ids,
        )
        copy.start()
        copies.append(copy)
    local.wait()
    for copy in copies:
        copy.wait()


def col_gather(x, n_col):
    return pl.pallas_call(
        functools.partial(_col_gather_kernel, n_col=n_col),
        out_shape=jax.ShapeDtypeStruct((n_col,) + x.shape, x.dtype),
        in_specs=[pl.BlockSpec(memory_space=pl.ANY)],
        out_specs=pl.BlockSpec(memory_space=pl.ANY),
        scratch_shapes=[
            pltpu.SemaphoreType.DMA((n_col,)),
            pltpu.SemaphoreType.DMA((n_col,)),
            pltpu.SemaphoreType.DMA,
        ],
        compiler_params=pltpu.CompilerParams(collective_id=1, has_side_effects=True),
    )(x)


def block_tables(q_seg, k_seg, q_start):
    n_q = q_seg.shape[0] // Q_BLOCK
    n_k = k_seg.shape[0] // K_BLOCK
    values = jnp.arange(-1, 2, dtype=jnp.int32)
    q_has = jnp.any(q_seg.reshape(n_q, Q_BLOCK, 1) == values, axis=1).astype(jnp.float32)
    k_has = jnp.any(k_seg.reshape(n_k, K_BLOCK, 1) == values, axis=1).astype(jnp.float32)
    shared = jnp.dot(q_has, k_has.T) > 0
    single = (jnp.sum(q_has, axis=1)[:, None] == 1) & (jnp.sum(k_has, axis=1)[None, :] == 1)
    diag = (q_start + jnp.arange(n_q, dtype=jnp.int32) * Q_BLOCK) // K_BLOCK
    order = (diag[:, None] + jnp.arange(n_k, dtype=jnp.int32)[None, :]) % n_k
    need = jnp.take_along_axis(shared, order, axis=1)
    full = jnp.take_along_axis(single, order, axis=1)
    rank = jnp.cumsum(need.astype(jnp.int32), axis=1) - 1
    count = jnp.sum(need.astype(jnp.int32), axis=1)
    pos = jnp.where(need, rank, n_k + jnp.arange(n_k)[None, :])
    perm = jnp.argsort(pos, axis=1)
    kb_sorted = jnp.take_along_axis(order, perm, axis=1)
    full_sorted = jnp.take_along_axis(full, perm, axis=1)
    step = jnp.arange(n_k, dtype=jnp.int32)[None, :]
    live = step < count[:, None]
    last = jnp.take_along_axis(kb_sorted, (count - 1)[:, None], axis=1)
    kb_map = jnp.where(live, kb_sorted, last).astype(jnp.int32)
    flags = jnp.where(live, jnp.where(full_sorted, 2, 1), 0).astype(jnp.int32)
    return kb_map, flags


def attention(q_t, q_seg_f, kv, kb_map, flags, scale, interpret=False):
    n_tok = q_t.shape[0]
    per_peer = kv.shape[3] // K_BLOCK
    n_keys = kv.shape[0] * kv.shape[3]
    n_q = n_tok // Q_BLOCK
    n_k = n_keys // K_BLOCK
    kernel = functools.partial(_attn_kernel, scale=scale, n_steps=n_k)
    grid_spec = pltpu.PrefetchScalarGridSpec(
        num_scalar_prefetch=2,
        grid=(n_q, n_k),
        in_specs=[
            pl.BlockSpec((Q_BLOCK, PADW), lambda i, j, km, fl: (i, 0)),
            pl.BlockSpec((Q_BLOCK, 1), lambda i, j, km, fl: (i, 0)),
            pl.BlockSpec((None, None, PADW, K_BLOCK), lambda i, j, km, fl: (km[i, j] // per_peer, 0, 0, km[i, j] % per_peer)),
            pl.BlockSpec((None, None, PADW, K_BLOCK), lambda i, j, km, fl: (km[i, j] // per_peer, 1, 0, km[i, j] % per_peer)),
        ],
        out_specs=pl.BlockSpec((Q_BLOCK, PADW), lambda i, j, km, fl: (i, 0)),
        scratch_shapes=[
            pltpu.VMEM((Q_BLOCK, 1), jnp.float32),
            pltpu.VMEM((Q_BLOCK, 1), jnp.float32),
            pltpu.VMEM((Q_BLOCK, PADW), jnp.float32),
        ],
    )
    return pl.pallas_call(
        kernel,
        grid_spec=grid_spec,
        out_shape=jax.ShapeDtypeStruct((n_tok, PADW), jnp.bfloat16),
        compiler_params=pltpu.CompilerParams(dimension_semantics=("arbitrary", "arbitrary")),
        interpret=interpret,
    )(kb_map, flags, q_t, q_seg_f, kv, kv)


def on_device(
    n_row,
    hidden,
    gain_in,
    w_query,
    w_pair,
    kv_cache,
    recompute_rows,
    segment_ids,
    w_out,
    gain_merge,
    w_merge,
    requests,
):
    local_width, tok_rows = hidden.shape
    model_width = w_query.shape[1]
    n_col = model_width // local_width
    heads_here = local_width // HD
    score_scale = HD ** (-0.5)
    col_index = lax.axis_index("col")
    gathered_rows = lax.all_gather(hidden, "col", axis=0, tiled=True)
    picked_rows = recompute_rows[0]
    hidden_picked = jnp.take(hidden, picked_rows, axis=1)
    picked_copies = jnp.broadcast_to(hidden_picked[None], (n_col,) + hidden_picked.shape)
    picked_full = lax.all_to_all(picked_copies, "col", 0, 0, tiled=True)
    picked_float = picked_full.reshape(model_width, -1).astype(jnp.float32)
    picked_mean = jnp.sum(picked_float, axis=0, keepdims=True) / model_width
    picked_square = jnp.sum(picked_float * picked_float, axis=0, keepdims=True) / model_width
    normed_picked = (
        (picked_float - picked_mean)
        * lax.rsqrt(picked_square - picked_mean * picked_mean + EPSILON)
        * gain_in.astype(jnp.float32)[:, None]
    ).astype(jnp.bfloat16)
    fresh_pairs = jnp.dot(
        w_pair.reshape(2 * local_width, model_width),
        normed_picked,
        preferred_element_type=jnp.float32,
    )
    fresh_pairs = fresh_pairs.astype(jnp.bfloat16).reshape(2, local_width, -1)
    keys_values = kv_cache.at[:, :, picked_rows].set(fresh_pairs)

    pair_local = jnp.pad(keys_values, ((0, 0), (0, PADW - HD), (0, 0)))
    pair_local = pair_local.at[0, HD].set(segment_ids.astype(jnp.bfloat16))
    pair_all = row_gather(pair_local, n_row)
    full_rows, pair_all = lax.optimization_barrier((gathered_rows, pair_all))
    full_float = full_rows.astype(jnp.float32)
    in_mean = jnp.sum(full_float, axis=0, keepdims=True) / model_width
    in_square = jnp.sum(full_float * full_float, axis=0, keepdims=True) / model_width
    normed = (
        (full_float - in_mean)
        * lax.rsqrt(in_square - in_mean * in_mean + EPSILON)
        * gain_in.astype(jnp.float32)[:, None]
    ).astype(jnp.bfloat16)
    query_rows = lax.dot_general(
        normed, w_query, (((0,), (1,)), ((), ())), preferred_element_type=jnp.float32
    ).astype(jnp.bfloat16)
    query_rows = jnp.pad(query_rows, ((0, 0), (0, PADW - HD)))
    segment_line = pair_all[:, 0, HD].reshape(-1).astype(jnp.int32)
    weight_stack = jnp.concatenate([w_out[None], w_merge], axis=0)
    weight_stack, _ = lax.optimization_barrier((weight_stack, picked_full))
    weights_full = lax.all_gather(weight_stack, "col", axis=1, tiled=True)
    out_weight = weights_full[0]
    merge_full = weights_full[1:]
    kb_map, flags = block_tables(segment_ids, segment_line, lax.axis_index("row") * tok_rows)
    attended_rows = attention(
        query_rows, segment_ids.astype(jnp.float32)[:, None], pair_all, kb_map, flags, score_scale
    )
    attended = attended_rows[:, :HD].T
    chunk = tok_rows // n_col
    attended_chunk = lax.all_to_all(attended, "col", 1, 0, tiled=True)
    x_chunk = lax.dynamic_slice_in_dim(full_rows, col_index * chunk, chunk, 1).astype(jnp.float32)
    projected = lax.dot_general(
        out_weight, attended_chunk, (((0,), (0,)), ((), ())), preferred_element_type=jnp.float32
    )
    updated = x_chunk + projected
    row_mean = jnp.sum(updated, axis=0, keepdims=True) / model_width
    row_square = jnp.sum(updated * updated, axis=0, keepdims=True) / model_width
    merger_chunk = (
        (updated - row_mean)
        * lax.rsqrt(row_square - row_mean * row_mean + EPSILON)
        * gain_merge.astype(jnp.float32)[:, None]
    ).astype(jnp.bfloat16)
    grouped = merger_chunk.reshape(model_width, chunk // 4, 4)
    merged_here = jnp.einsum("fgi,ifd->gd", grouped, merge_full, preferred_element_type=jnp.float32)
    merged_all = col_gather(merged_here.astype(jnp.bfloat16), n_col).reshape(-1, model_width)
    wanted_rows = lax.dynamic_index_in_dim(requests[0], col_index, 0, keepdims=False)
    is_valid = wanted_rows >= 0
    safe_index = jnp.where(is_valid, wanted_rows, 0)
    picked = jnp.where(is_valid[:, None], merged_all[safe_index], jnp.zeros((), jnp.bfloat16))
    return picked.reshape(1, 1, picked.shape[0], model_width)


def solution(mesh):
    placed = (
        P("col", "row"),
        P(),
        P("col", None),
        P(None, "col", None),
        P(None, "col", "row"),
        P("row", None),
        P("row"),
        P("col", None),
        P(),
        P(None, "col", None),
        P("row", None, None),
    )
    return jax.shard_map(
        functools.partial(on_device, mesh.shape["row"]),
        mesh=mesh,
        in_specs=placed,
        out_specs=P("row", "col", None, None),
        check_vma=False,
    )
```

```python
import jax
import jax.numpy as jnp
from jax import lax
import functools
from jax.experimental import pallas as pl
from jax.experimental.pallas import tpu as pltpu
from jax.sharding import PartitionSpec as P

HD = 88


EPSILON = 1e-06
MASKED = -1e30
PADW = 96
Q_BLOCK = 1024
K_BLOCK = 2048


def _attn_kernel(kb_map, flags, q_ref, qs_ref, k_ref, v_ref, o_ref, m_ref, l_ref, acc_ref, *, scale, n_steps):
    qb = pl.program_id(0)
    j = pl.program_id(1)
    flag = flags[qb, j]

    @pl.when(j == 0)
    def _():
        m_ref[...] = jnp.full(m_ref.shape, MASKED, jnp.float32)
        l_ref[...] = jnp.zeros(l_ref.shape, jnp.float32)
        acc_ref[...] = jnp.zeros(acc_ref.shape, jnp.float32)

    def step(masked):
        q = q_ref[...]
        k = k_ref[...]
        s = jnp.dot(q, k, preferred_element_type=jnp.float32) * scale
        if masked:
            key_seg = k[HD:HD + 1, :].astype(jnp.float32)
            s = jnp.where(qs_ref[...] == key_seg, s, MASKED)
        m_prev = m_ref[...]
        m_new = jnp.maximum(m_prev, jnp.max(s, axis=1, keepdims=True))
        p = jnp.exp(s - m_new)
        alpha = jnp.exp(m_prev - m_new)
        l_ref[...] = alpha * l_ref[...] + jnp.sum(p, axis=1, keepdims=True)
        pv = lax.dot_general(
            p.astype(jnp.bfloat16), v_ref[...], (((1,), (1,)), ((), ())),
            preferred_element_type=jnp.float32,
        )
        acc_ref[...] = alpha * acc_ref[...] + pv
        m_ref[...] = m_new

    @pl.when(flag == 1)
    def _():
        step(True)

    @pl.when(flag == 2)
    def _():
        step(False)

    @pl.when(j == n_steps - 1)
    def _():
        o_ref[...] = (acc_ref[...] / l_ref[...]).astype(o_ref.dtype)


def _row_gather_kernel(x_ref, o_ref, send_far, recv_far, send_pair, recv_pair, send_fwd, recv_fwd, local_sem, *, n_row):
    mesh_ids = pl.DeviceIdType.MESH
    n_chip = n_row // 2
    me = lax.axis_index("row")
    col = lax.axis_index("col")
    chip = me // 2
    core = me % 2
    sibling = chip * 2 + 1 - core
    far = [lax.rem(chip + k, n_chip) * 2 + core for k in range(1, n_chip)]
    barrier = pltpu.get_barrier_semaphore()
    for peer in far + [sibling]:
        pl.semaphore_signal(barrier, inc=1, device_id=(peer, col), device_id_type=mesh_ids)
    pl.semaphore_wait(barrier, n_chip)
    local = pltpu.make_async_copy(x_ref, o_ref.at[me], local_sem)
    local.start()
    pair = pltpu.make_async_remote_copy(
        src_ref=x_ref, dst_ref=o_ref.at[me], send_sem=send_pair, recv_sem=recv_pair,
        device_id=(sibling, col), device_id_type=mesh_ids,
    )
    pair.start()
    outgoing = []
    for k in range(1, n_chip):
        copy = pltpu.make_async_remote_copy(
            src_ref=x_ref, dst_ref=o_ref.at[me], send_sem=send_far.at[k], recv_sem=recv_far.at[k],
            device_id=(far[k - 1], col), device_id_type=mesh_ids,
        )
        copy.start()
        outgoing.append(copy)
    forwards = []
    for k in range(1, n_chip):
        outgoing[k - 1].wait_recv()
        source = lax.rem(chip + n_chip - k, n_chip) * 2 + core
        forward = pltpu.make_async_remote_copy(
            src_ref=o_ref.at[source], dst_ref=o_ref.at[source], send_sem=send_fwd.at[k],
            recv_sem=recv_fwd.at[k], device_id=(sibling, col), device_id_type=mesh_ids,
        )
        forward.start()
        forwards.append(forward)
    local.wait()
    pair.wait()
    for copy in outgoing:
        copy.wait_send()
    for forward in forwards:
        forward.wait()


def row_gather(x, n_row):
    n_chip = n_row // 2
    return pl.pallas_call(
        functools.partial(_row_gather_kernel, n_row=n_row),
        out_shape=jax.ShapeDtypeStruct((n_row,) + x.shape, x.dtype),
        in_specs=[pl.BlockSpec(memory_space=pl.ANY)],
        out_specs=pl.BlockSpec(memory_space=pl.ANY),
        scratch_shapes=[
            pltpu.SemaphoreType.DMA((n_chip,)),
            pltpu.SemaphoreType.DMA((n_chip,)),
            pltpu.SemaphoreType.DMA,
            pltpu.SemaphoreType.DMA,
            pltpu.SemaphoreType.DMA((n_chip,)),
            pltpu.SemaphoreType.DMA((n_chip,)),
            pltpu.SemaphoreType.DMA,
        ],
        compiler_params=pltpu.CompilerParams(collective_id=0, has_side_effects=True),
    )(x)


def _col_gather_kernel(x_ref, o_ref, send_sems, recv_sems, local_sem, *, n_col):
    mesh_ids = pl.DeviceIdType.MESH
    me = lax.axis_index("col")
    row = lax.axis_index("row")
    barrier = pltpu.get_barrier_semaphore()
    for k in range(1, n_col):
        peer = lax.rem(me + k, n_col)
        pl.semaphore_signal(barrier, inc=1, device_id=(row, peer), device_id_type=mesh_ids)
    pl.semaphore_wait(barrier, n_col - 1)
    local = pltpu.make_async_copy(x_ref, o_ref.at[me], local_sem)
    local.start()
    copies = []
    for k in range(1, n_col):
        peer = lax.rem(me + k, n_col)
        copy = pltpu.make_async_remote_copy(
            src_ref=x_ref, dst_ref=o_ref.at[me], send_sem=send_sems.at[k], recv_sem=recv_sems.at[k],
            device_id=(row, peer), device_id_type=mesh_ids,
        )
        copy.start()
        copies.append(copy)
    local.wait()
    for copy in copies:
        copy.wait()


def col_gather(x, n_col, kernel_id):
    return pl.pallas_call(
        functools.partial(_col_gather_kernel, n_col=n_col),
        out_shape=jax.ShapeDtypeStruct((n_col,) + x.shape, x.dtype),
        in_specs=[pl.BlockSpec(memory_space=pl.ANY)],
        out_specs=pl.BlockSpec(memory_space=pl.ANY),
        scratch_shapes=[
            pltpu.SemaphoreType.DMA((n_col,)),
            pltpu.SemaphoreType.DMA((n_col,)),
            pltpu.SemaphoreType.DMA,
        ],
        compiler_params=pltpu.CompilerParams(collective_id=kernel_id, has_side_effects=True),
    )(x)


def block_tables(q_seg, k_seg, q_start):
    n_q = q_seg.shape[0] // Q_BLOCK
    n_k = k_seg.shape[0] // K_BLOCK
    values = jnp.arange(-1, 2, dtype=jnp.int32)
    q_has = jnp.any(q_seg.reshape(n_q, Q_BLOCK, 1) == values, axis=1).astype(jnp.float32)
    k_has = jnp.any(k_seg.reshape(n_k, K_BLOCK, 1) == values, axis=1).astype(jnp.float32)
    shared = jnp.dot(q_has, k_has.T) > 0
    single = (jnp.sum(q_has, axis=1)[:, None] == 1) & (jnp.sum(k_has, axis=1)[None, :] == 1)
    diag = (q_start + jnp.arange(n_q, dtype=jnp.int32) * Q_BLOCK) // K_BLOCK
    order = (diag[:, None] + jnp.arange(n_k, dtype=jnp.int32)[None, :]) % n_k
    need = jnp.take_along_axis(shared, order, axis=1)
    full = jnp.take_along_axis(single, order, axis=1)
    rank = jnp.cumsum(need.astype(jnp.int32), axis=1) - 1
    count = jnp.sum(need.astype(jnp.int32), axis=1)
    pos = jnp.where(need, rank, n_k + jnp.arange(n_k)[None, :])
    perm = jnp.argsort(pos, axis=1)
    kb_sorted = jnp.take_along_axis(order, perm, axis=1)
    full_sorted = jnp.take_along_axis(full, perm, axis=1)
    step = jnp.arange(n_k, dtype=jnp.int32)[None, :]
    live = step < count[:, None]
    last = jnp.take_along_axis(kb_sorted, (count - 1)[:, None], axis=1)
    kb_map = jnp.where(live, kb_sorted, last).astype(jnp.int32)
    flags = jnp.where(live, jnp.where(full_sorted, 2, 1), 0).astype(jnp.int32)
    return kb_map, flags


def attention(q_t, q_seg_f, kv, kb_map, flags, scale, interpret=False):
    n_tok = q_t.shape[0]
    per_peer = kv.shape[3] // K_BLOCK
    n_keys = kv.shape[0] * kv.shape[3]
    n_q = n_tok // Q_BLOCK
    n_k = n_keys // K_BLOCK
    kernel = functools.partial(_attn_kernel, scale=scale, n_steps=n_k)
    grid_spec = pltpu.PrefetchScalarGridSpec(
        num_scalar_prefetch=2,
        grid=(n_q, n_k),
        in_specs=[
            pl.BlockSpec((Q_BLOCK, PADW), lambda i, j, km, fl: (i, 0)),
            pl.BlockSpec((Q_BLOCK, 1), lambda i, j, km, fl: (i, 0)),
            pl.BlockSpec((None, None, PADW, K_BLOCK), lambda i, j, km, fl: (km[i, j] // per_peer, 0, 0, km[i, j] % per_peer)),
            pl.BlockSpec((None, None, PADW, K_BLOCK), lambda i, j, km, fl: (km[i, j] // per_peer, 1, 0, km[i, j] % per_peer)),
        ],
        out_specs=pl.BlockSpec((Q_BLOCK, PADW), lambda i, j, km, fl: (i, 0)),
        scratch_shapes=[
            pltpu.VMEM((Q_BLOCK, 1), jnp.float32),
            pltpu.VMEM((Q_BLOCK, 1), jnp.float32),
            pltpu.VMEM((Q_BLOCK, PADW), jnp.float32),
        ],
    )
    return pl.pallas_call(
        kernel,
        grid_spec=grid_spec,
        out_shape=jax.ShapeDtypeStruct((n_tok, PADW), jnp.bfloat16),
        compiler_params=pltpu.CompilerParams(dimension_semantics=("arbitrary", "arbitrary")),
        interpret=interpret,
    )(kb_map, flags, q_t, q_seg_f, kv, kv)


def on_device(
    n_row,
    hidden,
    gain_in,
    w_query,
    w_pair,
    kv_cache,
    recompute_rows,
    segment_ids,
    w_out,
    gain_merge,
    w_merge,
    requests,
):
    local_width, tok_rows = hidden.shape
    model_width = w_query.shape[1]
    n_col = model_width // local_width
    heads_here = local_width // HD
    score_scale = HD ** (-0.5)
    col_index = lax.axis_index("col")
    full_rows = col_gather(hidden, n_col, 2).reshape(model_width, tok_rows)
    full_float = full_rows.astype(jnp.float32)
    in_mean = jnp.sum(full_float, axis=0, keepdims=True) / model_width
    in_square = jnp.sum(full_float * full_float, axis=0, keepdims=True) / model_width
    normed = (
        (full_float - in_mean)
        * lax.rsqrt(in_square - in_mean * in_mean + EPSILON)
        * gain_in.astype(jnp.float32)[:, None]
    ).astype(jnp.bfloat16)
    query_rows = lax.dot_general(
        normed, w_query, (((0,), (1,)), ((), ())), preferred_element_type=jnp.float32
    ).astype(jnp.bfloat16)
    query_rows = jnp.pad(query_rows, ((0, 0), (0, PADW - HD)))
    picked_rows = recompute_rows[0]
    normed_picked = jnp.take(normed, picked_rows, axis=1)
    fresh_pairs = jnp.dot(
        w_pair.reshape(2 * local_width, model_width),
        normed_picked,
        preferred_element_type=jnp.float32,
    )
    fresh_pairs = fresh_pairs.astype(jnp.bfloat16).reshape(2, local_width, -1)
    keys_values = kv_cache.at[:, :, picked_rows].set(fresh_pairs)

    pair_local = jnp.pad(keys_values, ((0, 0), (0, PADW - HD), (0, 0)))
    pair_local = pair_local.at[0, HD].set(segment_ids.astype(jnp.bfloat16))
    pair_all = row_gather(pair_local, n_row)
    segment_line = pair_all[:, 0, HD].reshape(-1).astype(jnp.int32)
    weight_stack = jnp.concatenate([w_out[None], w_merge], axis=0)
    weights_full = lax.all_gather(weight_stack, "col", axis=1, tiled=True)
    out_weight = weights_full[0]
    merge_full = weights_full[1:]
    kb_map, flags = block_tables(segment_ids, segment_line, lax.axis_index("row") * tok_rows)
    attended_rows = attention(
        query_rows, segment_ids.astype(jnp.float32)[:, None], pair_all, kb_map, flags, score_scale
    )
    attended = attended_rows[:, :HD].T
    chunk = tok_rows // n_col
    attended_chunk = lax.all_to_all(attended, "col", 1, 0, tiled=True)
    x_chunk = lax.dynamic_slice_in_dim(full_rows, col_index * chunk, chunk, 1).astype(jnp.float32)
    projected = lax.dot_general(
        out_weight, attended_chunk, (((0,), (0,)), ((), ())), preferred_element_type=jnp.float32
    )
    updated = x_chunk + projected
    row_mean = jnp.sum(updated, axis=0, keepdims=True) / model_width
    row_square = jnp.sum(updated * updated, axis=0, keepdims=True) / model_width
    merger_chunk = (
        (updated - row_mean)
        * lax.rsqrt(row_square - row_mean * row_mean + EPSILON)
        * gain_merge.astype(jnp.float32)[:, None]
    ).astype(jnp.bfloat16)
    grouped = merger_chunk.reshape(model_width, chunk // 4, 4)
    merged_here = jnp.einsum("fgi,ifd->gd", grouped, merge_full, preferred_element_type=jnp.float32)
    merged_all = col_gather(merged_here.astype(jnp.bfloat16), n_col, 1).reshape(-1, model_width)
    wanted_rows = lax.dynamic_index_in_dim(requests[0], col_index, 0, keepdims=False)
    is_valid = wanted_rows >= 0
    safe_index = jnp.where(is_valid, wanted_rows, 0)
    picked = jnp.where(is_valid[:, None], merged_all[safe_index], jnp.zeros((), jnp.bfloat16))
    return picked.reshape(1, 1, picked.shape[0], model_width)


def solution(mesh):
    placed = (
        P("col", "row"),
        P(),
        P("col", None),
        P(None, "col", None),
        P(None, "col", "row"),
        P("row", None),
        P("row"),
        P("col", None),
        P(),
        P(None, "col", None),
        P("row", None, None),
    )
    return jax.shard_map(
        functools.partial(on_device, mesh.shape["row"]),
        mesh=mesh,
        in_specs=placed,
        out_specs=P("row", "col", None, None),
        check_vma=False,
    )
```

```python
import jax
import jax.numpy as jnp
from jax import lax
import functools
from jax.experimental import pallas as pl
from jax.experimental.pallas import tpu as pltpu
from jax.sharding import PartitionSpec as P

HD = 88


EPSILON = 1e-06
MASKED = -1e30
PADW = 96
Q_BLOCK = 1024
K_BLOCK = 2048


def _attn_kernel(kb_map, flags, q_ref, qs_ref, k_ref, v_ref, o_ref, m_ref, l_ref, acc_ref, *, scale, n_steps):
    qb = pl.program_id(0)
    j = pl.program_id(1)
    flag = flags[qb, j]

    @pl.when(j == 0)
    def _():
        m_ref[...] = jnp.full(m_ref.shape, MASKED, jnp.float32)
        l_ref[...] = jnp.zeros(l_ref.shape, jnp.float32)
        acc_ref[...] = jnp.zeros(acc_ref.shape, jnp.float32)

    def step(masked):
        q = q_ref[...]
        k = k_ref[...]
        s = jnp.dot(q, k, preferred_element_type=jnp.float32) * scale
        if masked:
            key_seg = k[HD:HD + 1, :].astype(jnp.float32)
            s = jnp.where(qs_ref[...] == key_seg, s, MASKED)
        m_prev = m_ref[...]
        m_new = jnp.maximum(m_prev, jnp.max(s, axis=1, keepdims=True))
        p = jnp.exp(s - m_new)
        alpha = jnp.exp(m_prev - m_new)
        l_ref[...] = alpha * l_ref[...] + jnp.sum(p, axis=1, keepdims=True)
        pv = lax.dot_general(
            p.astype(jnp.bfloat16), v_ref[...], (((1,), (1,)), ((), ())),
            preferred_element_type=jnp.float32,
        )
        acc_ref[...] = alpha * acc_ref[...] + pv
        m_ref[...] = m_new

    @pl.when(flag == 1)
    def _():
        step(True)

    @pl.when(flag == 2)
    def _():
        step(False)

    @pl.when(j == n_steps - 1)
    def _():
        o_ref[...] = (acc_ref[...] / l_ref[...]).astype(o_ref.dtype)


def _row_gather_kernel(x_ref, o_ref, send_far, recv_far, send_pair, recv_pair, send_fwd, recv_fwd, local_sem, *, n_row):
    mesh_ids = pl.DeviceIdType.MESH
    n_chip = n_row // 2
    me = lax.axis_index("row")
    col = lax.axis_index("col")
    chip = me // 2
    core = me % 2
    sibling = chip * 2 + 1 - core
    far = [lax.rem(chip + k, n_chip) * 2 + core for k in range(1, n_chip)]
    barrier = pltpu.get_barrier_semaphore()
    for peer in far + [sibling]:
        pl.semaphore_signal(barrier, inc=1, device_id=(peer, col), device_id_type=mesh_ids)
    pl.semaphore_wait(barrier, n_chip)
    local = pltpu.make_async_copy(x_ref, o_ref.at[me], local_sem)
    local.start()
    pair = pltpu.make_async_remote_copy(
        src_ref=x_ref, dst_ref=o_ref.at[me], send_sem=send_pair, recv_sem=recv_pair,
        device_id=(sibling, col), device_id_type=mesh_ids,
    )
    pair.start()
    outgoing = []
    for k in range(1, n_chip):
        copy = pltpu.make_async_remote_copy(
            src_ref=x_ref, dst_ref=o_ref.at[me], send_sem=send_far.at[k], recv_sem=recv_far.at[k],
            device_id=(far[k - 1], col), device_id_type=mesh_ids,
        )
        copy.start()
        outgoing.append(copy)
    forwards = []
    for k in range(1, n_chip):
        outgoing[k - 1].wait_recv()
        source = lax.rem(chip + n_chip - k, n_chip) * 2 + core
        forward = pltpu.make_async_remote_copy(
            src_ref=o_ref.at[source], dst_ref=o_ref.at[source], send_sem=send_fwd.at[k],
            recv_sem=recv_fwd.at[k], device_id=(sibling, col), device_id_type=mesh_ids,
        )
        forward.start()
        forwards.append(forward)
    local.wait()
    pair.wait()
    for copy in outgoing:
        copy.wait_send()
    for forward in forwards:
        forward.wait()


def row_gather(x, n_row):
    n_chip = n_row // 2
    return pl.pallas_call(
        functools.partial(_row_gather_kernel, n_row=n_row),
        out_shape=jax.ShapeDtypeStruct((n_row,) + x.shape, x.dtype),
        in_specs=[pl.BlockSpec(memory_space=pl.ANY)],
        out_specs=pl.BlockSpec(memory_space=pl.ANY),
        scratch_shapes=[
            pltpu.SemaphoreType.DMA((n_chip,)),
            pltpu.SemaphoreType.DMA((n_chip,)),
            pltpu.SemaphoreType.DMA,
            pltpu.SemaphoreType.DMA,
            pltpu.SemaphoreType.DMA((n_chip,)),
            pltpu.SemaphoreType.DMA((n_chip,)),
            pltpu.SemaphoreType.DMA,
        ],
        compiler_params=pltpu.CompilerParams(collective_id=0, has_side_effects=True),
    )(x)


def _col_gather_kernel(x_ref, o_ref, send_sems, recv_sems, local_sem, *, n_col):
    mesh_ids = pl.DeviceIdType.MESH
    me = lax.axis_index("col")
    row = lax.axis_index("row")
    barrier = pltpu.get_barrier_semaphore()
    for k in range(1, n_col):
        peer = lax.rem(me + k, n_col)
        pl.semaphore_signal(barrier, inc=1, device_id=(row, peer), device_id_type=mesh_ids)
    pl.semaphore_wait(barrier, n_col - 1)
    local = pltpu.make_async_copy(x_ref, o_ref.at[me], local_sem)
    local.start()
    copies = []
    for k in range(1, n_col):
        peer = lax.rem(me + k, n_col)
        copy = pltpu.make_async_remote_copy(
            src_ref=x_ref, dst_ref=o_ref.at[me], send_sem=send_sems.at[k], recv_sem=recv_sems.at[k],
            device_id=(row, peer), device_id_type=mesh_ids,
        )
        copy.start()
        copies.append(copy)
    local.wait()
    for copy in copies:
        copy.wait()


def col_gather(x, n_col):
    return pl.pallas_call(
        functools.partial(_col_gather_kernel, n_col=n_col),
        out_shape=jax.ShapeDtypeStruct((n_col,) + x.shape, x.dtype),
        in_specs=[pl.BlockSpec(memory_space=pl.ANY)],
        out_specs=pl.BlockSpec(memory_space=pl.ANY),
        scratch_shapes=[
            pltpu.SemaphoreType.DMA((n_col,)),
            pltpu.SemaphoreType.DMA((n_col,)),
            pltpu.SemaphoreType.DMA,
        ],
        compiler_params=pltpu.CompilerParams(collective_id=1, has_side_effects=True),
    )(x)


def block_tables(q_seg, k_seg, q_start):
    n_q = q_seg.shape[0] // Q_BLOCK
    n_k = k_seg.shape[0] // K_BLOCK
    values = jnp.arange(-1, 2, dtype=jnp.int32)
    q_has = jnp.any(q_seg.reshape(n_q, Q_BLOCK, 1) == values, axis=1).astype(jnp.float32)
    k_has = jnp.any(k_seg.reshape(n_k, K_BLOCK, 1) == values, axis=1).astype(jnp.float32)
    shared = jnp.dot(q_has, k_has.T) > 0
    single = (jnp.sum(q_has, axis=1)[:, None] == 1) & (jnp.sum(k_has, axis=1)[None, :] == 1)
    diag = (q_start + jnp.arange(n_q, dtype=jnp.int32) * Q_BLOCK) // K_BLOCK
    order = (diag[:, None] + jnp.arange(n_k, dtype=jnp.int32)[None, :]) % n_k
    need = jnp.take_along_axis(shared, order, axis=1)
    full = jnp.take_along_axis(single, order, axis=1)
    rank = jnp.cumsum(need.astype(jnp.int32), axis=1) - 1
    count = jnp.sum(need.astype(jnp.int32), axis=1)
    pos = jnp.where(need, rank, n_k + jnp.arange(n_k)[None, :])
    perm = jnp.argsort(pos, axis=1)
    kb_sorted = jnp.take_along_axis(order, perm, axis=1)
    full_sorted = jnp.take_along_axis(full, perm, axis=1)
    step = jnp.arange(n_k, dtype=jnp.int32)[None, :]
    live = step < count[:, None]
    last = jnp.take_along_axis(kb_sorted, (count - 1)[:, None], axis=1)
    kb_map = jnp.where(live, kb_sorted, last).astype(jnp.int32)
    flags = jnp.where(live, jnp.where(full_sorted, 2, 1), 0).astype(jnp.int32)
    return kb_map, flags


def attention(q_t, q_seg_f, kv, kb_map, flags, scale, interpret=False):
    n_tok = q_t.shape[0]
    per_peer = kv.shape[3] // K_BLOCK
    n_keys = kv.shape[0] * kv.shape[3]
    n_q = n_tok // Q_BLOCK
    n_k = n_keys // K_BLOCK
    kernel = functools.partial(_attn_kernel, scale=scale, n_steps=n_k)
    grid_spec = pltpu.PrefetchScalarGridSpec(
        num_scalar_prefetch=2,
        grid=(n_q, n_k),
        in_specs=[
            pl.BlockSpec((Q_BLOCK, PADW), lambda i, j, km, fl: (i, 0)),
            pl.BlockSpec((Q_BLOCK, 1), lambda i, j, km, fl: (i, 0)),
            pl.BlockSpec((None, None, PADW, K_BLOCK), lambda i, j, km, fl: (km[i, j] // per_peer, 0, 0, km[i, j] % per_peer)),
            pl.BlockSpec((None, None, PADW, K_BLOCK), lambda i, j, km, fl: (km[i, j] // per_peer, 1, 0, km[i, j] % per_peer)),
        ],
        out_specs=pl.BlockSpec((Q_BLOCK, PADW), lambda i, j, km, fl: (i, 0)),
        scratch_shapes=[
            pltpu.VMEM((Q_BLOCK, 1), jnp.float32),
            pltpu.VMEM((Q_BLOCK, 1), jnp.float32),
            pltpu.VMEM((Q_BLOCK, PADW), jnp.float32),
        ],
    )
    return pl.pallas_call(
        kernel,
        grid_spec=grid_spec,
        out_shape=jax.ShapeDtypeStruct((n_tok, PADW), jnp.bfloat16),
        compiler_params=pltpu.CompilerParams(dimension_semantics=("arbitrary", "arbitrary")),
        interpret=interpret,
    )(kb_map, flags, q_t, q_seg_f, kv, kv)


def on_device(
    n_row,
    hidden,
    gain_in,
    w_query,
    w_pair,
    kv_cache,
    recompute_rows,
    segment_ids,
    w_out,
    gain_merge,
    w_merge,
    requests,
):
    local_width, tok_rows = hidden.shape
    model_width = w_query.shape[1]
    n_col = model_width // local_width
    heads_here = local_width // HD
    score_scale = HD ** (-0.5)
    col_index = lax.axis_index("col")
    gathered_rows = lax.all_gather(hidden, "col", axis=0, tiled=True)
    picked_rows = recompute_rows[0]
    hidden_picked = jnp.take(hidden, picked_rows, axis=1)
    picked_copies = jnp.broadcast_to(hidden_picked[None], (n_col,) + hidden_picked.shape)
    picked_full = lax.all_to_all(picked_copies, "col", 0, 0, tiled=True)
    picked_float = picked_full.reshape(model_width, -1).astype(jnp.float32)
    picked_mean = jnp.sum(picked_float, axis=0, keepdims=True) / model_width
    picked_square = jnp.sum(picked_float * picked_float, axis=0, keepdims=True) / model_width
    normed_picked = (
        (picked_float - picked_mean)
        * lax.rsqrt(picked_square - picked_mean * picked_mean + EPSILON)
        * gain_in.astype(jnp.float32)[:, None]
    ).astype(jnp.bfloat16)
    fresh_pairs = jnp.dot(
        w_pair.reshape(2 * local_width, model_width),
        normed_picked,
        preferred_element_type=jnp.float32,
    )
    fresh_pairs = fresh_pairs.astype(jnp.bfloat16).reshape(2, local_width, -1)
    keys_values = kv_cache.at[:, :, picked_rows].set(fresh_pairs)

    pair_local = jnp.pad(keys_values, ((0, 0), (0, PADW - HD), (0, 0)))
    pair_local = pair_local.at[0, HD].set(segment_ids.astype(jnp.bfloat16))
    pair_all = row_gather(pair_local, n_row)
    full_rows, pair_all = lax.optimization_barrier((gathered_rows, pair_all))
    full_float = full_rows.astype(jnp.float32)
    in_mean = jnp.sum(full_float, axis=0, keepdims=True) / model_width
    in_square = jnp.sum(full_float * full_float, axis=0, keepdims=True) / model_width
    normed = (
        (full_float - in_mean)
        * lax.rsqrt(in_square - in_mean * in_mean + EPSILON)
        * gain_in.astype(jnp.float32)[:, None]
    ).astype(jnp.bfloat16)
    query_rows = lax.dot_general(
        normed, w_query, (((0,), (1,)), ((), ())), preferred_element_type=jnp.float32
    ).astype(jnp.bfloat16)
    query_rows = jnp.pad(query_rows, ((0, 0), (0, PADW - HD)))
    segment_line = pair_all[:, 0, HD].reshape(-1).astype(jnp.int32)
    weight_stack = jnp.concatenate([w_out[None], w_merge], axis=0)
    weight_copies = jnp.broadcast_to(weight_stack[None], (n_col,) + weight_stack.shape)
    weights_full = lax.all_to_all(weight_copies, "col", 0, 0, tiled=True)
    out_weight = weights_full[:, 0].reshape(model_width, model_width)
    merge_parts = weights_full[:, 1:]
    kb_map, flags = block_tables(segment_ids, segment_line, lax.axis_index("row") * tok_rows)
    attended_rows = attention(
        query_rows, segment_ids.astype(jnp.float32)[:, None], pair_all, kb_map, flags, score_scale
    )
    attended = attended_rows[:, :HD].T
    chunk = tok_rows // n_col
    attended_chunk = lax.all_to_all(attended, "col", 1, 0, tiled=True)
    x_chunk = lax.dynamic_slice_in_dim(full_rows, col_index * chunk, chunk, 1).astype(jnp.float32)
    projected = lax.dot_general(
        out_weight, attended_chunk, (((0,), (0,)), ((), ())), preferred_element_type=jnp.float32
    )
    updated = x_chunk + projected
    row_mean = jnp.sum(updated, axis=0, keepdims=True) / model_width
    row_square = jnp.sum(updated * updated, axis=0, keepdims=True) / model_width
    merger_chunk = (
        (updated - row_mean)
        * lax.rsqrt(row_square - row_mean * row_mean + EPSILON)
        * gain_merge.astype(jnp.float32)[:, None]
    ).astype(jnp.bfloat16)
    grouped = merger_chunk.reshape(n_col, local_width, chunk // 4, 4)
    merged_here = jnp.einsum("cfgi,cifd->gd", grouped, merge_parts, preferred_element_type=jnp.float32)
    merged_all = col_gather(merged_here.astype(jnp.bfloat16), n_col).reshape(-1, model_width)
    wanted_rows = lax.dynamic_index_in_dim(requests[0], col_index, 0, keepdims=False)
    is_valid = wanted_rows >= 0
    safe_index = jnp.where(is_valid, wanted_rows, 0)
    picked = jnp.where(is_valid[:, None], merged_all[safe_index], jnp.zeros((), jnp.bfloat16))
    return picked.reshape(1, 1, picked.shape[0], model_width)


def solution(mesh):
    placed = (
        P("col", "row"),
        P(),
        P("col", None),
        P(None, "col", None),
        P(None, "col", "row"),
        P("row", None),
        P("row"),
        P("col", None),
        P(),
        P(None, "col", None),
        P("row", None, None),
    )
    return jax.shard_map(
        functools.partial(on_device, mesh.shape["row"]),
        mesh=mesh,
        in_specs=placed,
        out_specs=P("row", "col", None, None),
        check_vma=False,
    )
```

```python
import jax
import jax.numpy as jnp
from jax import lax
import functools
from jax.experimental import pallas as pl
from jax.experimental.pallas import tpu as pltpu
from jax.sharding import PartitionSpec as P

HD = 88


EPSILON = 1e-06
MASKED = -1e30
PADW = 96
Q_BLOCK = 1024
K_BLOCK = 2048


def _attn_kernel(kb_map, flags, q_ref, qs_ref, k_ref, v_ref, o_ref, m_ref, l_ref, acc_ref, *, scale, n_steps):
    qb = pl.program_id(0)
    j = pl.program_id(1)
    flag = flags[qb, j]

    @pl.when(j == 0)
    def _():
        m_ref[...] = jnp.full(m_ref.shape, MASKED, jnp.float32)
        l_ref[...] = jnp.zeros(l_ref.shape, jnp.float32)
        acc_ref[...] = jnp.zeros(acc_ref.shape, jnp.float32)

    def step(masked):
        q = q_ref[...]
        k = k_ref[...]
        s = jnp.dot(q, k, preferred_element_type=jnp.float32) * scale
        if masked:
            key_seg = k[HD:HD + 1, :].astype(jnp.float32)
            s = jnp.where(qs_ref[...] == key_seg, s, MASKED)
        m_prev = m_ref[...]
        m_new = jnp.maximum(m_prev, jnp.max(s, axis=1, keepdims=True))
        p = jnp.exp(s - m_new)
        alpha = jnp.exp(m_prev - m_new)
        l_ref[...] = alpha * l_ref[...] + jnp.sum(p, axis=1, keepdims=True)
        pv = lax.dot_general(
            p.astype(jnp.bfloat16), v_ref[...], (((1,), (1,)), ((), ())),
            preferred_element_type=jnp.float32,
        )
        acc_ref[...] = alpha * acc_ref[...] + pv
        m_ref[...] = m_new

    @pl.when(flag == 1)
    def _():
        step(True)

    @pl.when(flag == 2)
    def _():
        step(False)

    @pl.when(j == n_steps - 1)
    def _():
        o_ref[...] = (acc_ref[...] / l_ref[...]).astype(o_ref.dtype)


def _row_gather_kernel(x_ref, o_ref, send_far, recv_far, send_pair, recv_pair, send_fwd, recv_fwd, local_sem, *, n_row):
    mesh_ids = pl.DeviceIdType.MESH
    n_chip = n_row // 2
    me = lax.axis_index("row")
    col = lax.axis_index("col")
    chip = me // 2
    core = me % 2
    sibling = chip * 2 + 1 - core
    far = [lax.rem(chip + k, n_chip) * 2 + core for k in range(1, n_chip)]
    barrier = pltpu.get_barrier_semaphore()
    for peer in far + [sibling]:
        pl.semaphore_signal(barrier, inc=1, device_id=(peer, col), device_id_type=mesh_ids)
    pl.semaphore_wait(barrier, n_chip)
    local = pltpu.make_async_copy(x_ref, o_ref.at[me], local_sem)
    local.start()
    pair = pltpu.make_async_remote_copy(
        src_ref=x_ref, dst_ref=o_ref.at[me], send_sem=send_pair, recv_sem=recv_pair,
        device_id=(sibling, col), device_id_type=mesh_ids,
    )
    pair.start()
    outgoing = []
    for k in range(1, n_chip):
        copy = pltpu.make_async_remote_copy(
            src_ref=x_ref, dst_ref=o_ref.at[me], send_sem=send_far.at[k], recv_sem=recv_far.at[k],
            device_id=(far[k - 1], col), device_id_type=mesh_ids,
        )
        copy.start()
        outgoing.append(copy)
    forwards = []
    for k in range(1, n_chip):
        outgoing[k - 1].wait_recv()
        source = lax.rem(chip + n_chip - k, n_chip) * 2 + core
        forward = pltpu.make_async_remote_copy(
            src_ref=o_ref.at[source], dst_ref=o_ref.at[source], send_sem=send_fwd.at[k],
            recv_sem=recv_fwd.at[k], device_id=(sibling, col), device_id_type=mesh_ids,
        )
        forward.start()
        forwards.append(forward)
    local.wait()
    pair.wait()
    for copy in outgoing:
        copy.wait_send()
    for forward in forwards:
        forward.wait()


def row_gather(x, n_row):
    n_chip = n_row // 2
    return pl.pallas_call(
        functools.partial(_row_gather_kernel, n_row=n_row),
        out_shape=jax.ShapeDtypeStruct((n_row,) + x.shape, x.dtype),
        in_specs=[pl.BlockSpec(memory_space=pl.ANY)],
        out_specs=pl.BlockSpec(memory_space=pl.ANY),
        scratch_shapes=[
            pltpu.SemaphoreType.DMA((n_chip,)),
            pltpu.SemaphoreType.DMA((n_chip,)),
            pltpu.SemaphoreType.DMA,
            pltpu.SemaphoreType.DMA,
            pltpu.SemaphoreType.DMA((n_chip,)),
            pltpu.SemaphoreType.DMA((n_chip,)),
            pltpu.SemaphoreType.DMA,
        ],
        compiler_params=pltpu.CompilerParams(collective_id=0, has_side_effects=True),
    )(x)


def _col_gather_kernel(x_ref, o_ref, send_sems, recv_sems, local_sem, *, n_col):
    mesh_ids = pl.DeviceIdType.MESH
    me = lax.axis_index("col")
    row = lax.axis_index("row")
    barrier = pltpu.get_barrier_semaphore()
    for k in range(1, n_col):
        peer = lax.rem(me + k, n_col)
        pl.semaphore_signal(barrier, inc=1, device_id=(row, peer), device_id_type=mesh_ids)
    pl.semaphore_wait(barrier, n_col - 1)
    local = pltpu.make_async_copy(x_ref, o_ref.at[me], local_sem)
    local.start()
    copies = []
    for k in range(1, n_col):
        peer = lax.rem(me + k, n_col)
        copy = pltpu.make_async_remote_copy(
            src_ref=x_ref, dst_ref=o_ref.at[me], send_sem=send_sems.at[k], recv_sem=recv_sems.at[k],
            device_id=(row, peer), device_id_type=mesh_ids,
        )
        copy.start()
        copies.append(copy)
    local.wait()
    for copy in copies:
        copy.wait()


def col_gather(x, n_col):
    return pl.pallas_call(
        functools.partial(_col_gather_kernel, n_col=n_col),
        out_shape=jax.ShapeDtypeStruct((n_col,) + x.shape, x.dtype),
        in_specs=[pl.BlockSpec(memory_space=pl.ANY)],
        out_specs=pl.BlockSpec(memory_space=pl.ANY),
        scratch_shapes=[
            pltpu.SemaphoreType.DMA((n_col,)),
            pltpu.SemaphoreType.DMA((n_col,)),
            pltpu.SemaphoreType.DMA,
        ],
        compiler_params=pltpu.CompilerParams(collective_id=1, has_side_effects=True),
    )(x)


def block_tables(q_seg, k_seg, q_start):
    n_q = q_seg.shape[0] // Q_BLOCK
    n_k = k_seg.shape[0] // K_BLOCK
    values = jnp.arange(-1, 2, dtype=jnp.int32)
    q_has = jnp.any(q_seg.reshape(n_q, Q_BLOCK, 1) == values, axis=1).astype(jnp.float32)
    k_has = jnp.any(k_seg.reshape(n_k, K_BLOCK, 1) == values, axis=1).astype(jnp.float32)
    shared = jnp.dot(q_has, k_has.T) > 0
    single = (jnp.sum(q_has, axis=1)[:, None] == 1) & (jnp.sum(k_has, axis=1)[None, :] == 1)
    diag = (q_start + jnp.arange(n_q, dtype=jnp.int32) * Q_BLOCK) // K_BLOCK
    order = (diag[:, None] + jnp.arange(n_k, dtype=jnp.int32)[None, :]) % n_k
    need = jnp.take_along_axis(shared, order, axis=1)
    full = jnp.take_along_axis(single, order, axis=1)
    rank = jnp.cumsum(need.astype(jnp.int32), axis=1) - 1
    count = jnp.sum(need.astype(jnp.int32), axis=1)
    pos = jnp.where(need, rank, n_k + jnp.arange(n_k)[None, :])
    perm = jnp.argsort(pos, axis=1)
    kb_sorted = jnp.take_along_axis(order, perm, axis=1)
    full_sorted = jnp.take_along_axis(full, perm, axis=1)
    step = jnp.arange(n_k, dtype=jnp.int32)[None, :]
    live = step < count[:, None]
    last = jnp.take_along_axis(kb_sorted, (count - 1)[:, None], axis=1)
    kb_map = jnp.where(live, kb_sorted, last).astype(jnp.int32)
    flags = jnp.where(live, jnp.where(full_sorted, 2, 1), 0).astype(jnp.int32)
    return kb_map, flags


def attention(q_t, q_seg_f, kv, kb_map, flags, scale, interpret=False):
    n_tok = q_t.shape[0]
    per_peer = kv.shape[3] // K_BLOCK
    n_keys = kv.shape[0] * kv.shape[3]
    n_q = n_tok // Q_BLOCK
    n_k = n_keys // K_BLOCK
    kernel = functools.partial(_attn_kernel, scale=scale, n_steps=n_k)
    grid_spec = pltpu.PrefetchScalarGridSpec(
        num_scalar_prefetch=2,
        grid=(n_q, n_k),
        in_specs=[
            pl.BlockSpec((Q_BLOCK, PADW), lambda i, j, km, fl: (i, 0)),
            pl.BlockSpec((Q_BLOCK, 1), lambda i, j, km, fl: (i, 0)),
            pl.BlockSpec((None, None, PADW, K_BLOCK), lambda i, j, km, fl: (km[i, j] // per_peer, 0, 0, km[i, j] % per_peer)),
            pl.BlockSpec((None, None, PADW, K_BLOCK), lambda i, j, km, fl: (km[i, j] // per_peer, 1, 0, km[i, j] % per_peer)),
        ],
        out_specs=pl.BlockSpec((Q_BLOCK, PADW), lambda i, j, km, fl: (i, 0)),
        scratch_shapes=[
            pltpu.VMEM((Q_BLOCK, 1), jnp.float32),
            pltpu.VMEM((Q_BLOCK, 1), jnp.float32),
            pltpu.VMEM((Q_BLOCK, PADW), jnp.float32),
        ],
    )
    return pl.pallas_call(
        kernel,
        grid_spec=grid_spec,
        out_shape=jax.ShapeDtypeStruct((n_tok, PADW), jnp.bfloat16),
        compiler_params=pltpu.CompilerParams(dimension_semantics=("arbitrary", "arbitrary")),
        interpret=interpret,
    )(kb_map, flags, q_t, q_seg_f, kv, kv)


def on_device(
    n_row,
    hidden,
    gain_in,
    w_query,
    w_pair,
    kv_cache,
    recompute_rows,
    segment_ids,
    w_out,
    gain_merge,
    w_merge,
    requests,
):
    local_width, tok_rows = hidden.shape
    model_width = w_query.shape[1]
    n_col = model_width // local_width
    heads_here = local_width // HD
    score_scale = HD ** (-0.5)
    col_index = lax.axis_index("col")
    gathered_rows = lax.all_gather(hidden, "col", axis=0, tiled=True)
    picked_rows = recompute_rows[0]
    hidden_picked = jnp.take(hidden, picked_rows, axis=1)
    picked_copies = jnp.broadcast_to(hidden_picked[None], (n_col,) + hidden_picked.shape)
    picked_full = lax.all_to_all(picked_copies, "col", 0, 0, tiled=True)
    picked_float = picked_full.reshape(model_width, -1).astype(jnp.float32)
    picked_mean = jnp.sum(picked_float, axis=0, keepdims=True) / model_width
    picked_square = jnp.sum(picked_float * picked_float, axis=0, keepdims=True) / model_width
    normed_picked = (
        (picked_float - picked_mean)
        * lax.rsqrt(picked_square - picked_mean * picked_mean + EPSILON)
        * gain_in.astype(jnp.float32)[:, None]
    ).astype(jnp.bfloat16)
    fresh_pairs = jnp.dot(
        w_pair.reshape(2 * local_width, model_width),
        normed_picked,
        preferred_element_type=jnp.float32,
    )
    fresh_pairs = fresh_pairs.astype(jnp.bfloat16).reshape(2, local_width, -1)
    keys_values = kv_cache.at[:, :, picked_rows].set(fresh_pairs)

    pair_local = jnp.pad(keys_values, ((0, 0), (0, PADW - HD), (0, 0)))
    pair_local = pair_local.at[0, HD].set(segment_ids.astype(jnp.bfloat16))
    pair_all = row_gather(pair_local, n_row)
    full_rows, pair_all = lax.optimization_barrier((gathered_rows, pair_all))
    full_float = full_rows.astype(jnp.float32)
    in_mean = jnp.sum(full_float, axis=0, keepdims=True) / model_width
    in_square = jnp.sum(full_float * full_float, axis=0, keepdims=True) / model_width
    normed = (
        (full_float - in_mean)
        * lax.rsqrt(in_square - in_mean * in_mean + EPSILON)
        * gain_in.astype(jnp.float32)[:, None]
    ).astype(jnp.bfloat16)
    query_rows = lax.dot_general(
        normed, w_query, (((0,), (1,)), ((), ())), preferred_element_type=jnp.float32
    ).astype(jnp.bfloat16)
    query_rows = jnp.pad(query_rows, ((0, 0), (0, PADW - HD)))
    segment_line = pair_all[:, 0, HD].reshape(-1).astype(jnp.int32)
    half = model_width // 2
    core = lax.axis_index("row") % 2
    weight_stack = jnp.concatenate([w_out[None], w_merge], axis=0)
    weight_half = lax.dynamic_slice_in_dim(weight_stack, core * half, half, 2)
    weight_half, _ = lax.optimization_barrier((weight_half, full_rows))
    weights_mine = lax.all_gather(weight_half, "col", axis=1, tiled=True)

    def in_order(mine, other, axis):
        return jnp.where(
            core == 0,
            jnp.concatenate([mine, other], axis=axis),
            jnp.concatenate([other, mine], axis=axis),
        )
    kb_map, flags = block_tables(segment_ids, segment_line, lax.axis_index("row") * tok_rows)
    attended_rows = attention(
        query_rows, segment_ids.astype(jnp.float32)[:, None], pair_all, kb_map, flags, score_scale
    )
    attended = attended_rows[:, :HD].T
    weights_mine, _ = lax.optimization_barrier((weights_mine, attended_rows))
    weights_other = lax.ppermute(weights_mine, "row", [(i, i ^ 1) for i in range(n_row)])
    chunk = tok_rows // n_col
    attended_chunk = lax.all_to_all(attended, "col", 1, 0, tiled=True)
    x_chunk = lax.dynamic_slice_in_dim(full_rows, col_index * chunk, chunk, 1).astype(jnp.float32)
    projected = in_order(
        *[
            lax.dot_general(
                part[0], attended_chunk, (((0,), (0,)), ((), ())), preferred_element_type=jnp.float32
            )
            for part in (weights_mine, weights_other)
        ],
        0,
    )
    updated = x_chunk + projected
    row_mean = jnp.sum(updated, axis=0, keepdims=True) / model_width
    row_square = jnp.sum(updated * updated, axis=0, keepdims=True) / model_width
    merger_chunk = (
        (updated - row_mean)
        * lax.rsqrt(row_square - row_mean * row_mean + EPSILON)
        * gain_merge.astype(jnp.float32)[:, None]
    ).astype(jnp.bfloat16)
    grouped = merger_chunk.reshape(model_width, chunk // 4, 4)
    merged_here = in_order(
        *[
            jnp.einsum("fgi,ifd->gd", grouped, part[1:], preferred_element_type=jnp.float32)
            for part in (weights_mine, weights_other)
        ],
        1,
    )
    merged_all = col_gather(merged_here.astype(jnp.bfloat16), n_col).reshape(-1, model_width)
    wanted_rows = lax.dynamic_index_in_dim(requests[0], col_index, 0, keepdims=False)
    is_valid = wanted_rows >= 0
    safe_index = jnp.where(is_valid, wanted_rows, 0)
    picked = jnp.where(is_valid[:, None], merged_all[safe_index], jnp.zeros((), jnp.bfloat16))
    return picked.reshape(1, 1, picked.shape[0], model_width)


def solution(mesh):
    placed = (
        P("col", "row"),
        P(),
        P("col", None),
        P(None, "col", None),
        P(None, "col", "row"),
        P("row", None),
        P("row"),
        P("col", None),
        P(),
        P(None, "col", None),
        P("row", None, None),
    )
    return jax.shard_map(
        functools.partial(on_device, mesh.shape["row"]),
        mesh=mesh,
        in_specs=placed,
        out_specs=P("row", "col", None, None),
        check_vma=False,
    )
```

```python
import jax
import jax.numpy as jnp
from jax import lax
import functools
from jax.experimental import pallas as pl
from jax.experimental.pallas import tpu as pltpu
from jax.sharding import PartitionSpec as P

HD = 88


EPSILON = 1e-06
MASKED = -1e30
PADW = 96
Q_BLOCK = 1024
K_BLOCK = 2048


def _attn_kernel(kb_map, flags, q_ref, qs_ref, k_ref, v_ref, o_ref, m_ref, l_ref, acc_ref, *, scale, n_steps):
    qb = pl.program_id(0)
    j = pl.program_id(1)
    flag = flags[qb, j]

    @pl.when(j == 0)
    def _():
        m_ref[...] = jnp.full(m_ref.shape, MASKED, jnp.float32)
        l_ref[...] = jnp.zeros(l_ref.shape, jnp.float32)
        acc_ref[...] = jnp.zeros(acc_ref.shape, jnp.float32)

    def step(masked):
        q = q_ref[...]
        k = k_ref[...]
        s = jnp.dot(q, k, preferred_element_type=jnp.float32) * scale
        if masked:
            key_seg = k[HD:HD + 1, :].astype(jnp.float32)
            s = jnp.where(qs_ref[...] == key_seg, s, MASKED)
        m_prev = m_ref[...]
        m_new = jnp.maximum(m_prev, jnp.max(s, axis=1, keepdims=True))
        p = jnp.exp(s - m_new)
        alpha = jnp.exp(m_prev - m_new)
        l_ref[...] = alpha * l_ref[...] + jnp.sum(p, axis=1, keepdims=True)
        pv = lax.dot_general(
            p.astype(jnp.bfloat16), v_ref[...], (((1,), (1,)), ((), ())),
            preferred_element_type=jnp.float32,
        )
        acc_ref[...] = alpha * acc_ref[...] + pv
        m_ref[...] = m_new

    @pl.when(flag == 1)
    def _():
        step(True)

    @pl.when(flag == 2)
    def _():
        step(False)

    @pl.when(j == n_steps - 1)
    def _():
        o_ref[...] = (acc_ref[...] / l_ref[...]).astype(o_ref.dtype)


def _row_gather_kernel(x_ref, o_ref, send_far, recv_far, send_pair, recv_pair, send_fwd, recv_fwd, local_sem, *, n_row):
    mesh_ids = pl.DeviceIdType.MESH
    n_chip = n_row // 2
    me = lax.axis_index("row")
    col = lax.axis_index("col")
    chip = me // 2
    core = me % 2
    sibling = chip * 2 + 1 - core
    far = [lax.rem(chip + k, n_chip) * 2 + core for k in range(1, n_chip)]
    barrier = pltpu.get_barrier_semaphore()
    for peer in far + [sibling]:
        pl.semaphore_signal(barrier, inc=1, device_id=(peer, col), device_id_type=mesh_ids)
    pl.semaphore_wait(barrier, n_chip)
    local = pltpu.make_async_copy(x_ref, o_ref.at[me], local_sem)
    local.start()
    pair = pltpu.make_async_remote_copy(
        src_ref=x_ref, dst_ref=o_ref.at[me], send_sem=send_pair, recv_sem=recv_pair,
        device_id=(sibling, col), device_id_type=mesh_ids,
    )
    pair.start()
    outgoing = []
    for k in range(1, n_chip):
        copy = pltpu.make_async_remote_copy(
            src_ref=x_ref, dst_ref=o_ref.at[me], send_sem=send_far.at[k], recv_sem=recv_far.at[k],
            device_id=(far[k - 1], col), device_id_type=mesh_ids,
        )
        copy.start()
        outgoing.append(copy)
    forwards = []
    for k in range(1, n_chip):
        outgoing[k - 1].wait_recv()
        source = lax.rem(chip + n_chip - k, n_chip) * 2 + core
        forward = pltpu.make_async_remote_copy(
            src_ref=o_ref.at[source], dst_ref=o_ref.at[source], send_sem=send_fwd.at[k],
            recv_sem=recv_fwd.at[k], device_id=(sibling, col), device_id_type=mesh_ids,
        )
        forward.start()
        forwards.append(forward)
    local.wait()
    pair.wait()
    for copy in outgoing:
        copy.wait_send()
    for forward in forwards:
        forward.wait()


def row_gather(x, n_row):
    n_chip = n_row // 2
    return pl.pallas_call(
        functools.partial(_row_gather_kernel, n_row=n_row),
        out_shape=jax.ShapeDtypeStruct((n_row,) + x.shape, x.dtype),
        in_specs=[pl.BlockSpec(memory_space=pl.ANY)],
        out_specs=pl.BlockSpec(memory_space=pl.ANY),
        scratch_shapes=[
            pltpu.SemaphoreType.DMA((n_chip,)),
            pltpu.SemaphoreType.DMA((n_chip,)),
            pltpu.SemaphoreType.DMA,
            pltpu.SemaphoreType.DMA,
            pltpu.SemaphoreType.DMA((n_chip,)),
            pltpu.SemaphoreType.DMA((n_chip,)),
            pltpu.SemaphoreType.DMA,
        ],
        compiler_params=pltpu.CompilerParams(collective_id=0, has_side_effects=True),
    )(x)


def _col_gather_kernel(x_ref, o_ref, send_sems, recv_sems, local_sem, *, n_col):
    mesh_ids = pl.DeviceIdType.MESH
    me = lax.axis_index("col")
    row = lax.axis_index("row")
    barrier = pltpu.get_barrier_semaphore()
    for k in range(1, n_col):
        peer = lax.rem(me + k, n_col)
        pl.semaphore_signal(barrier, inc=1, device_id=(row, peer), device_id_type=mesh_ids)
    pl.semaphore_wait(barrier, n_col - 1)
    local = pltpu.make_async_copy(x_ref, o_ref.at[me], local_sem)
    local.start()
    copies = []
    for k in range(1, n_col):
        peer = lax.rem(me + k, n_col)
        copy = pltpu.make_async_remote_copy(
            src_ref=x_ref, dst_ref=o_ref.at[me], send_sem=send_sems.at[k], recv_sem=recv_sems.at[k],
            device_id=(row, peer), device_id_type=mesh_ids,
        )
        copy.start()
        copies.append(copy)
    local.wait()
    for copy in copies:
        copy.wait()


def col_gather(x, n_col):
    return pl.pallas_call(
        functools.partial(_col_gather_kernel, n_col=n_col),
        out_shape=jax.ShapeDtypeStruct((n_col,) + x.shape, x.dtype),
        in_specs=[pl.BlockSpec(memory_space=pl.ANY)],
        out_specs=pl.BlockSpec(memory_space=pl.ANY),
        scratch_shapes=[
            pltpu.SemaphoreType.DMA((n_col,)),
            pltpu.SemaphoreType.DMA((n_col,)),
            pltpu.SemaphoreType.DMA,
        ],
        compiler_params=pltpu.CompilerParams(collective_id=1, has_side_effects=True),
    )(x)


def block_tables(q_seg, k_seg, q_start):
    n_q = q_seg.shape[0] // Q_BLOCK
    n_k = k_seg.shape[0] // K_BLOCK
    values = jnp.arange(-1, 2, dtype=jnp.int32)
    q_has = jnp.any(q_seg.reshape(n_q, Q_BLOCK, 1) == values, axis=1).astype(jnp.float32)
    k_has = jnp.any(k_seg.reshape(n_k, K_BLOCK, 1) == values, axis=1).astype(jnp.float32)
    shared = jnp.dot(q_has, k_has.T) > 0
    single = (jnp.sum(q_has, axis=1)[:, None] == 1) & (jnp.sum(k_has, axis=1)[None, :] == 1)
    diag = (q_start + jnp.arange(n_q, dtype=jnp.int32) * Q_BLOCK) // K_BLOCK
    order = (diag[:, None] + jnp.arange(n_k, dtype=jnp.int32)[None, :]) % n_k
    need = jnp.take_along_axis(shared, order, axis=1)
    full = jnp.take_along_axis(single, order, axis=1)
    rank = jnp.cumsum(need.astype(jnp.int32), axis=1) - 1
    count = jnp.sum(need.astype(jnp.int32), axis=1)
    pos = jnp.where(need, rank, n_k + jnp.arange(n_k)[None, :])
    perm = jnp.argsort(pos, axis=1)
    kb_sorted = jnp.take_along_axis(order, perm, axis=1)
    full_sorted = jnp.take_along_axis(full, perm, axis=1)
    step = jnp.arange(n_k, dtype=jnp.int32)[None, :]
    live = step < count[:, None]
    last = jnp.take_along_axis(kb_sorted, (count - 1)[:, None], axis=1)
    kb_map = jnp.where(live, kb_sorted, last).astype(jnp.int32)
    flags = jnp.where(live, jnp.where(full_sorted, 2, 1), 0).astype(jnp.int32)
    return kb_map, flags


def attention(q_t, q_seg_f, kv, kb_map, flags, scale, interpret=False):
    n_tok = q_t.shape[0]
    per_peer = kv.shape[3] // K_BLOCK
    n_keys = kv.shape[0] * kv.shape[3]
    n_q = n_tok // Q_BLOCK
    n_k = n_keys // K_BLOCK
    kernel = functools.partial(_attn_kernel, scale=scale, n_steps=n_k)
    grid_spec = pltpu.PrefetchScalarGridSpec(
        num_scalar_prefetch=2,
        grid=(n_q, n_k),
        in_specs=[
            pl.BlockSpec((Q_BLOCK, PADW), lambda i, j, km, fl: (i, 0)),
            pl.BlockSpec((Q_BLOCK, 1), lambda i, j, km, fl: (i, 0)),
            pl.BlockSpec((None, None, PADW, K_BLOCK), lambda i, j, km, fl: (km[i, j] // per_peer, 0, 0, km[i, j] % per_peer)),
            pl.BlockSpec((None, None, PADW, K_BLOCK), lambda i, j, km, fl: (km[i, j] // per_peer, 1, 0, km[i, j] % per_peer)),
        ],
        out_specs=pl.BlockSpec((Q_BLOCK, PADW), lambda i, j, km, fl: (i, 0)),
        scratch_shapes=[
            pltpu.VMEM((Q_BLOCK, 1), jnp.float32),
            pltpu.VMEM((Q_BLOCK, 1), jnp.float32),
            pltpu.VMEM((Q_BLOCK, PADW), jnp.float32),
        ],
    )
    return pl.pallas_call(
        kernel,
        grid_spec=grid_spec,
        out_shape=jax.ShapeDtypeStruct((n_tok, PADW), jnp.bfloat16),
        compiler_params=pltpu.CompilerParams(dimension_semantics=("arbitrary", "arbitrary")),
        interpret=interpret,
    )(kb_map, flags, q_t, q_seg_f, kv, kv)


def on_device(
    n_row,
    hidden,
    gain_in,
    w_query,
    w_pair,
    kv_cache,
    recompute_rows,
    segment_ids,
    w_out,
    gain_merge,
    w_merge,
    requests,
):
    local_width, tok_rows = hidden.shape
    model_width = w_query.shape[1]
    n_col = model_width // local_width
    heads_here = local_width // HD
    score_scale = HD ** (-0.5)
    col_index = lax.axis_index("col")
    gathered_rows = lax.all_gather(hidden, "col", axis=0, tiled=True)
    picked_rows = recompute_rows[0]
    hidden_picked = jnp.take(hidden, picked_rows, axis=1)
    picked_copies = jnp.broadcast_to(hidden_picked[None], (n_col,) + hidden_picked.shape)
    picked_full = lax.all_to_all(picked_copies, "col", 0, 0, tiled=True)
    picked_float = picked_full.reshape(model_width, -1).astype(jnp.float32)
    picked_mean = jnp.sum(picked_float, axis=0, keepdims=True) / model_width
    picked_square = jnp.sum(picked_float * picked_float, axis=0, keepdims=True) / model_width
    normed_picked = (
        (picked_float - picked_mean)
        * lax.rsqrt(picked_square - picked_mean * picked_mean + EPSILON)
        * gain_in.astype(jnp.float32)[:, None]
    ).astype(jnp.bfloat16)
    fresh_pairs = jnp.dot(
        w_pair.reshape(2 * local_width, model_width),
        normed_picked,
        preferred_element_type=jnp.float32,
    )
    fresh_pairs = fresh_pairs.astype(jnp.bfloat16).reshape(2, local_width, -1)
    keys_values = kv_cache.at[:, :, picked_rows].set(fresh_pairs)

    pair_local = jnp.pad(keys_values, ((0, 0), (0, PADW - HD), (0, 0)))
    pair_local = pair_local.at[0, HD].set(segment_ids.astype(jnp.bfloat16))
    pair_all = row_gather(pair_local, n_row)
    full_rows, pair_all = lax.optimization_barrier((gathered_rows, pair_all))
    full_float = full_rows.astype(jnp.float32)
    in_mean = jnp.sum(full_float, axis=0, keepdims=True) / model_width
    in_square = jnp.sum(full_float * full_float, axis=0, keepdims=True) / model_width
    normed = (
        (full_float - in_mean)
        * lax.rsqrt(in_square - in_mean * in_mean + EPSILON)
        * gain_in.astype(jnp.float32)[:, None]
    ).astype(jnp.bfloat16)
    query_rows = lax.dot_general(
        normed, w_query, (((0,), (1,)), ((), ())), preferred_element_type=jnp.float32
    ).astype(jnp.bfloat16)
    query_rows = jnp.pad(query_rows, ((0, 0), (0, PADW - HD)))
    segment_line = pair_all[:, 0, HD].reshape(-1).astype(jnp.int32)
    half = model_width // 2
    core = lax.axis_index("row") % 2
    weight_stack = jnp.concatenate([w_out[None], w_merge], axis=0)
    weight_half = lax.dynamic_slice_in_dim(weight_stack, core * half, half, 2)
    weight_half, _ = lax.optimization_barrier((weight_half, picked_full))
    weights_mine = lax.all_gather(weight_half, "col", axis=1, tiled=True)

    def in_order(mine, other, axis):
        return jnp.where(
            core == 0,
            jnp.concatenate([mine, other], axis=axis),
            jnp.concatenate([other, mine], axis=axis),
        )
    kb_map, flags = block_tables(segment_ids, segment_line, lax.axis_index("row") * tok_rows)
    attended_rows = attention(
        query_rows, segment_ids.astype(jnp.float32)[:, None], pair_all, kb_map, flags, score_scale
    )
    attended = attended_rows[:, :HD].T
    weights_mine, _ = lax.optimization_barrier((weights_mine, attended_rows))
    weights_other = lax.ppermute(weights_mine, "row", [(i, i ^ 1) for i in range(n_row)])
    chunk = tok_rows // n_col
    attended_chunk = lax.all_to_all(attended, "col", 1, 0, tiled=True)
    x_chunk = lax.dynamic_slice_in_dim(full_rows, col_index * chunk, chunk, 1).astype(jnp.float32)
    projected = in_order(
        *[
            lax.dot_general(
                part[0], attended_chunk, (((0,), (0,)), ((), ())), preferred_element_type=jnp.float32
            )
            for part in (weights_mine, weights_other)
        ],
        0,
    )
    updated = x_chunk + projected
    row_mean = jnp.sum(updated, axis=0, keepdims=True) / model_width
    row_square = jnp.sum(updated * updated, axis=0, keepdims=True) / model_width
    merger_chunk = (
        (updated - row_mean)
        * lax.rsqrt(row_square - row_mean * row_mean + EPSILON)
        * gain_merge.astype(jnp.float32)[:, None]
    ).astype(jnp.bfloat16)
    grouped = merger_chunk.reshape(model_width, chunk // 4, 4)
    merged_here = in_order(
        *[
            jnp.einsum("fgi,ifd->gd", grouped, part[1:], preferred_element_type=jnp.float32)
            for part in (weights_mine, weights_other)
        ],
        1,
    )
    merged_all = col_gather(merged_here.astype(jnp.bfloat16), n_col).reshape(-1, model_width)
    wanted_rows = lax.dynamic_index_in_dim(requests[0], col_index, 0, keepdims=False)
    is_valid = wanted_rows >= 0
    safe_index = jnp.where(is_valid, wanted_rows, 0)
    picked = jnp.where(is_valid[:, None], merged_all[safe_index], jnp.zeros((), jnp.bfloat16))
    return picked.reshape(1, 1, picked.shape[0], model_width)


def solution(mesh):
    placed = (
        P("col", "row"),
        P(),
        P("col", None),
        P(None, "col", None),
        P(None, "col", "row"),
        P("row", None),
        P("row"),
        P("col", None),
        P(),
        P(None, "col", None),
        P("row", None, None),
    )
    return jax.shard_map(
        functools.partial(on_device, mesh.shape["row"]),
        mesh=mesh,
        in_specs=placed,
        out_specs=P("row", "col", None, None),
        check_vma=False,
    )
```

```python
import jax
import jax.numpy as jnp
from jax import lax
import functools
from jax.experimental import pallas as pl
from jax.experimental.pallas import tpu as pltpu
from jax.sharding import PartitionSpec as P

HD = 88


EPSILON = 1e-06
MASKED = -1e30
PADW = 96
Q_BLOCK = 1024
K_BLOCK = 2048


def _attn_kernel(kb_map, flags, q_ref, qs_ref, k_ref, v_ref, o_ref, m_ref, l_ref, acc_ref, *, scale, n_steps):
    qb = pl.program_id(0)
    j = pl.program_id(1)
    flag = flags[qb, j]

    @pl.when(j == 0)
    def _():
        m_ref[...] = jnp.full(m_ref.shape, MASKED, jnp.float32)
        l_ref[...] = jnp.zeros(l_ref.shape, jnp.float32)
        acc_ref[...] = jnp.zeros(acc_ref.shape, jnp.float32)

    def step(masked):
        q = q_ref[...]
        k = k_ref[...]
        s = jnp.dot(q, k, preferred_element_type=jnp.float32) * scale
        if masked:
            key_seg = k[HD:HD + 1, :].astype(jnp.float32)
            s = jnp.where(qs_ref[...] == key_seg, s, MASKED)
        m_prev = m_ref[...]
        m_new = jnp.maximum(m_prev, jnp.max(s, axis=1, keepdims=True))
        p = jnp.exp(s - m_new)
        alpha = jnp.exp(m_prev - m_new)
        l_ref[...] = alpha * l_ref[...] + jnp.sum(p, axis=1, keepdims=True)
        pv = lax.dot_general(
            p.astype(jnp.bfloat16), v_ref[...], (((1,), (1,)), ((), ())),
            preferred_element_type=jnp.float32,
        )
        acc_ref[...] = alpha * acc_ref[...] + pv
        m_ref[...] = m_new

    @pl.when(flag == 1)
    def _():
        step(True)

    @pl.when(flag == 2)
    def _():
        step(False)

    @pl.when(j == n_steps - 1)
    def _():
        o_ref[...] = (acc_ref[...] / l_ref[...]).astype(o_ref.dtype)


def _row_gather_kernel(x_ref, o_ref, send_far, recv_far, send_pair, recv_pair, send_fwd, recv_fwd, local_sem, *, n_row):
    mesh_ids = pl.DeviceIdType.MESH
    n_chip = n_row // 2
    me = lax.axis_index("row")
    col = lax.axis_index("col")
    chip = me // 2
    core = me % 2
    sibling = chip * 2 + 1 - core
    far = [lax.rem(chip + k, n_chip) * 2 + core for k in range(1, n_chip)]
    barrier = pltpu.get_barrier_semaphore()
    for peer in far + [sibling]:
        pl.semaphore_signal(barrier, inc=1, device_id=(peer, col), device_id_type=mesh_ids)
    pl.semaphore_wait(barrier, n_chip)
    local = pltpu.make_async_copy(x_ref, o_ref.at[me], local_sem)
    local.start()
    pair = pltpu.make_async_remote_copy(
        src_ref=x_ref, dst_ref=o_ref.at[me], send_sem=send_pair, recv_sem=recv_pair,
        device_id=(sibling, col), device_id_type=mesh_ids,
    )
    pair.start()
    outgoing = []
    for k in range(1, n_chip):
        copy = pltpu.make_async_remote_copy(
            src_ref=x_ref, dst_ref=o_ref.at[me], send_sem=send_far.at[k], recv_sem=recv_far.at[k],
            device_id=(far[k - 1], col), device_id_type=mesh_ids,
        )
        copy.start()
        outgoing.append(copy)
    forwards = []
    for k in range(1, n_chip):
        outgoing[k - 1].wait_recv()
        source = lax.rem(chip + n_chip - k, n_chip) * 2 + core
        forward = pltpu.make_async_remote_copy(
            src_ref=o_ref.at[source], dst_ref=o_ref.at[source], send_sem=send_fwd.at[k],
            recv_sem=recv_fwd.at[k], device_id=(sibling, col), device_id_type=mesh_ids,
        )
        forward.start()
        forwards.append(forward)
    local.wait()
    pair.wait()
    for copy in outgoing:
        copy.wait_send()
    for forward in forwards:
        forward.wait()


def row_gather(x, n_row):
    n_chip = n_row // 2
    return pl.pallas_call(
        functools.partial(_row_gather_kernel, n_row=n_row),
        out_shape=jax.ShapeDtypeStruct((n_row,) + x.shape, x.dtype),
        in_specs=[pl.BlockSpec(memory_space=pl.ANY)],
        out_specs=pl.BlockSpec(memory_space=pl.ANY),
        scratch_shapes=[
            pltpu.SemaphoreType.DMA((n_chip,)),
            pltpu.SemaphoreType.DMA((n_chip,)),
            pltpu.SemaphoreType.DMA,
            pltpu.SemaphoreType.DMA,
            pltpu.SemaphoreType.DMA((n_chip,)),
            pltpu.SemaphoreType.DMA((n_chip,)),
            pltpu.SemaphoreType.DMA,
        ],
        compiler_params=pltpu.CompilerParams(collective_id=0, has_side_effects=True),
    )(x)


def _col_gather_kernel(x_ref, o_ref, send_sems, recv_sems, local_sem, *, n_col):
    mesh_ids = pl.DeviceIdType.MESH
    me = lax.axis_index("col")
    row = lax.axis_index("row")
    barrier = pltpu.get_barrier_semaphore()
    for k in range(1, n_col):
        peer = lax.rem(me + k, n_col)
        pl.semaphore_signal(barrier, inc=1, device_id=(row, peer), device_id_type=mesh_ids)
    pl.semaphore_wait(barrier, n_col - 1)
    local = pltpu.make_async_copy(x_ref, o_ref.at[me], local_sem)
    local.start()
    copies = []
    for k in range(1, n_col):
        peer = lax.rem(me + k, n_col)
        copy = pltpu.make_async_remote_copy(
            src_ref=x_ref, dst_ref=o_ref.at[me], send_sem=send_sems.at[k], recv_sem=recv_sems.at[k],
            device_id=(row, peer), device_id_type=mesh_ids,
        )
        copy.start()
        copies.append(copy)
    local.wait()
    for copy in copies:
        copy.wait()


def col_gather(x, n_col):
    return pl.pallas_call(
        functools.partial(_col_gather_kernel, n_col=n_col),
        out_shape=jax.ShapeDtypeStruct((n_col,) + x.shape, x.dtype),
        in_specs=[pl.BlockSpec(memory_space=pl.ANY)],
        out_specs=pl.BlockSpec(memory_space=pl.ANY),
        scratch_shapes=[
            pltpu.SemaphoreType.DMA((n_col,)),
            pltpu.SemaphoreType.DMA((n_col,)),
            pltpu.SemaphoreType.DMA,
        ],
        compiler_params=pltpu.CompilerParams(collective_id=1, has_side_effects=True),
    )(x)


def block_tables(q_seg, k_seg, q_start):
    n_q = q_seg.shape[0] // Q_BLOCK
    n_k = k_seg.shape[0] // K_BLOCK
    values = jnp.arange(-1, 2, dtype=jnp.int32)
    q_has = jnp.any(q_seg.reshape(n_q, Q_BLOCK, 1) == values, axis=1).astype(jnp.float32)
    k_has = jnp.any(k_seg.reshape(n_k, K_BLOCK, 1) == values, axis=1).astype(jnp.float32)
    shared = jnp.dot(q_has, k_has.T) > 0
    single = (jnp.sum(q_has, axis=1)[:, None] == 1) & (jnp.sum(k_has, axis=1)[None, :] == 1)
    diag = (q_start + jnp.arange(n_q, dtype=jnp.int32) * Q_BLOCK) // K_BLOCK
    order = (diag[:, None] + jnp.arange(n_k, dtype=jnp.int32)[None, :]) % n_k
    need = jnp.take_along_axis(shared, order, axis=1)
    full = jnp.take_along_axis(single, order, axis=1)
    rank = jnp.cumsum(need.astype(jnp.int32), axis=1) - 1
    count = jnp.sum(need.astype(jnp.int32), axis=1)
    pos = jnp.where(need, rank, n_k + jnp.arange(n_k)[None, :])
    perm = jnp.argsort(pos, axis=1)
    kb_sorted = jnp.take_along_axis(order, perm, axis=1)
    full_sorted = jnp.take_along_axis(full, perm, axis=1)
    step = jnp.arange(n_k, dtype=jnp.int32)[None, :]
    live = step < count[:, None]
    last = jnp.take_along_axis(kb_sorted, (count - 1)[:, None], axis=1)
    kb_map = jnp.where(live, kb_sorted, last).astype(jnp.int32)
    flags = jnp.where(live, jnp.where(full_sorted, 2, 1), 0).astype(jnp.int32)
    return kb_map, flags


def attention(q_t, q_seg_f, kv, kb_map, flags, scale, interpret=False):
    n_tok = q_t.shape[0]
    per_peer = kv.shape[3] // K_BLOCK
    n_keys = kv.shape[0] * kv.shape[3]
    n_q = n_tok // Q_BLOCK
    n_k = n_keys // K_BLOCK
    kernel = functools.partial(_attn_kernel, scale=scale, n_steps=n_k)
    grid_spec = pltpu.PrefetchScalarGridSpec(
        num_scalar_prefetch=2,
        grid=(n_q, n_k),
        in_specs=[
            pl.BlockSpec((Q_BLOCK, PADW), lambda i, j, km, fl: (i, 0)),
            pl.BlockSpec((Q_BLOCK, 1), lambda i, j, km, fl: (i, 0)),
            pl.BlockSpec((None, None, PADW, K_BLOCK), lambda i, j, km, fl: (km[i, j] // per_peer, 0, 0, km[i, j] % per_peer)),
            pl.BlockSpec((None, None, PADW, K_BLOCK), lambda i, j, km, fl: (km[i, j] // per_peer, 1, 0, km[i, j] % per_peer)),
        ],
        out_specs=pl.BlockSpec((Q_BLOCK, PADW), lambda i, j, km, fl: (i, 0)),
        scratch_shapes=[
            pltpu.VMEM((Q_BLOCK, 1), jnp.float32),
            pltpu.VMEM((Q_BLOCK, 1), jnp.float32),
            pltpu.VMEM((Q_BLOCK, PADW), jnp.float32),
        ],
    )
    return pl.pallas_call(
        kernel,
        grid_spec=grid_spec,
        out_shape=jax.ShapeDtypeStruct((n_tok, PADW), jnp.bfloat16),
        compiler_params=pltpu.CompilerParams(dimension_semantics=("arbitrary", "arbitrary")),
        interpret=interpret,
    )(kb_map, flags, q_t, q_seg_f, kv, kv)


def on_device(
    n_row,
    hidden,
    gain_in,
    w_query,
    w_pair,
    kv_cache,
    recompute_rows,
    segment_ids,
    w_out,
    gain_merge,
    w_merge,
    requests,
):
    local_width, tok_rows = hidden.shape
    model_width = w_query.shape[1]
    n_col = model_width // local_width
    heads_here = local_width // HD
    score_scale = HD ** (-0.5)
    col_index = lax.axis_index("col")
    gathered_rows = lax.all_gather(hidden, "col", axis=0, tiled=True)
    picked_rows = recompute_rows[0]
    hidden_picked = jnp.take(hidden, picked_rows, axis=1)
    picked_copies = jnp.broadcast_to(hidden_picked[None], (n_col,) + hidden_picked.shape)
    picked_full = lax.all_to_all(picked_copies, "col", 0, 0, tiled=True)
    picked_float = picked_full.reshape(model_width, -1).astype(jnp.float32)
    picked_mean = jnp.sum(picked_float, axis=0, keepdims=True) / model_width
    picked_square = jnp.sum(picked_float * picked_float, axis=0, keepdims=True) / model_width
    normed_picked = (
        (picked_float - picked_mean)
        * lax.rsqrt(picked_square - picked_mean * picked_mean + EPSILON)
        * gain_in.astype(jnp.float32)[:, None]
    ).astype(jnp.bfloat16)
    fresh_pairs = jnp.dot(
        w_pair.reshape(2 * local_width, model_width),
        normed_picked,
        preferred_element_type=jnp.float32,
    )
    fresh_pairs = fresh_pairs.astype(jnp.bfloat16).reshape(2, local_width, -1)
    keys_values = kv_cache.at[:, :, picked_rows].set(fresh_pairs)

    pair_local = jnp.pad(keys_values, ((0, 0), (0, PADW - HD), (0, 0)))
    pair_local = pair_local.at[0, HD].set(segment_ids.astype(jnp.bfloat16))
    pair_all = row_gather(pair_local, n_row)
    full_rows, pair_all = lax.optimization_barrier((gathered_rows, pair_all))
    full_float = full_rows.astype(jnp.float32)
    in_mean = jnp.sum(full_float, axis=0, keepdims=True) / model_width
    in_square = jnp.sum(full_float * full_float, axis=0, keepdims=True) / model_width
    normed = (
        (full_float - in_mean)
        * lax.rsqrt(in_square - in_mean * in_mean + EPSILON)
        * gain_in.astype(jnp.float32)[:, None]
    ).astype(jnp.bfloat16)
    query_rows = lax.dot_general(
        normed, w_query, (((0,), (1,)), ((), ())), preferred_element_type=jnp.float32
    ).astype(jnp.bfloat16)
    query_rows = jnp.pad(query_rows, ((0, 0), (0, PADW - HD)))
    segment_line = pair_all[:, 0, HD].reshape(-1).astype(jnp.int32)
    half = -(-model_width // 256) * 128
    core = lax.axis_index("row") % 2
    weight_stack = jnp.concatenate([w_out[None], w_merge], axis=0)
    weight_stack = jnp.pad(weight_stack, ((0, 0), (0, 0), (0, 2 * half - model_width)))
    weight_half = lax.dynamic_slice_in_dim(weight_stack, core * half, half, 2)
    weight_half, _ = lax.optimization_barrier((weight_half, picked_full))
    weights_mine = lax.all_gather(weight_half, "col", axis=1, tiled=True)

    def in_order(mine, other, axis):
        return jnp.where(
            core == 0,
            jnp.concatenate([mine, other], axis=axis),
            jnp.concatenate([other, mine], axis=axis),
        )
    kb_map, flags = block_tables(segment_ids, segment_line, lax.axis_index("row") * tok_rows)
    attended_rows = attention(
        query_rows, segment_ids.astype(jnp.float32)[:, None], pair_all, kb_map, flags, score_scale
    )
    attended = attended_rows[:, :HD].T
    weights_mine, _ = lax.optimization_barrier((weights_mine, attended_rows))
    weights_other = lax.ppermute(weights_mine, "row", [(i, i ^ 1) for i in range(n_row)])
    chunk = tok_rows // n_col
    attended_chunk = lax.all_to_all(attended, "col", 1, 0, tiled=True)
    x_chunk = lax.dynamic_slice_in_dim(full_rows, col_index * chunk, chunk, 1).astype(jnp.float32)
    projected = in_order(
        *[
            lax.dot_general(
                part[0], attended_chunk, (((0,), (0,)), ((), ())), preferred_element_type=jnp.float32
            )
            for part in (weights_mine, weights_other)
        ],
        0,
    )[:model_width]
    updated = x_chunk + projected
    row_mean = jnp.sum(updated, axis=0, keepdims=True) / model_width
    row_square = jnp.sum(updated * updated, axis=0, keepdims=True) / model_width
    merger_chunk = (
        (updated - row_mean)
        * lax.rsqrt(row_square - row_mean * row_mean + EPSILON)
        * gain_merge.astype(jnp.float32)[:, None]
    ).astype(jnp.bfloat16)
    grouped = merger_chunk.reshape(model_width, chunk // 4, 4)
    merged_here = in_order(
        *[
            jnp.einsum("fgi,ifd->gd", grouped, part[1:], preferred_element_type=jnp.float32)
            for part in (weights_mine, weights_other)
        ],
        1,
    )[:, :model_width]
    merged_all = col_gather(merged_here.astype(jnp.bfloat16), n_col).reshape(-1, model_width)
    wanted_rows = lax.dynamic_index_in_dim(requests[0], col_index, 0, keepdims=False)
    is_valid = wanted_rows >= 0
    safe_index = jnp.where(is_valid, wanted_rows, 0)
    picked = jnp.where(is_valid[:, None], merged_all[safe_index], jnp.zeros((), jnp.bfloat16))
    return picked.reshape(1, 1, picked.shape[0], model_width)


def solution(mesh):
    placed = (
        P("col", "row"),
        P(),
        P("col", None),
        P(None, "col", None),
        P(None, "col", "row"),
        P("row", None),
        P("row"),
        P("col", None),
        P(),
        P(None, "col", None),
        P("row", None, None),
    )
    return jax.shard_map(
        functools.partial(on_device, mesh.shape["row"]),
        mesh=mesh,
        in_specs=placed,
        out_specs=P("row", "col", None, None),
        check_vma=False,
    )
```

```python
import jax
import jax.numpy as jnp
from jax import lax
import functools
from jax.experimental import pallas as pl
from jax.experimental.pallas import tpu as pltpu
from jax.sharding import PartitionSpec as P

HD = 88


EPSILON = 1e-06
MASKED = -1e30
PADW = 96
Q_BLOCK = 1024
K_BLOCK = 2048


def _attn_kernel(kb_map, flags, q_ref, qs_ref, k_ref, v_ref, o_ref, m_ref, l_ref, acc_ref, *, scale, n_steps):
    qb = pl.program_id(0)
    j = pl.program_id(1)
    flag = flags[qb, j]

    @pl.when(j == 0)
    def _():
        m_ref[...] = jnp.full(m_ref.shape, MASKED, jnp.float32)
        l_ref[...] = jnp.zeros(l_ref.shape, jnp.float32)
        acc_ref[...] = jnp.zeros(acc_ref.shape, jnp.float32)

    def step(masked):
        q = q_ref[...]
        k = k_ref[...]
        s = jnp.dot(q, k, preferred_element_type=jnp.float32) * scale
        if masked:
            key_seg = k[HD:HD + 1, :].astype(jnp.float32)
            s = jnp.where(qs_ref[...] == key_seg, s, MASKED)
        m_prev = m_ref[...]
        m_new = jnp.maximum(m_prev, jnp.max(s, axis=1, keepdims=True))
        p = jnp.exp(s - m_new)
        alpha = jnp.exp(m_prev - m_new)
        l_ref[...] = alpha * l_ref[...] + jnp.sum(p, axis=1, keepdims=True)
        pv = lax.dot_general(
            p.astype(jnp.bfloat16), v_ref[...], (((1,), (1,)), ((), ())),
            preferred_element_type=jnp.float32,
        )
        acc_ref[...] = alpha * acc_ref[...] + pv
        m_ref[...] = m_new

    @pl.when(flag == 1)
    def _():
        step(True)

    @pl.when(flag == 2)
    def _():
        step(False)

    @pl.when(j == n_steps - 1)
    def _():
        o_ref[...] = (acc_ref[...] / l_ref[...]).astype(o_ref.dtype)


def _row_gather_kernel(x_ref, o_ref, send_far, recv_far, send_pair, recv_pair, send_fwd, recv_fwd, local_sem, *, n_row):
    mesh_ids = pl.DeviceIdType.MESH
    n_chip = n_row // 2
    me = lax.axis_index("row")
    col = lax.axis_index("col")
    chip = me // 2
    core = me % 2
    sibling = chip * 2 + 1 - core
    far = [lax.rem(chip + k, n_chip) * 2 + core for k in range(1, n_chip)]
    barrier = pltpu.get_barrier_semaphore()
    for peer in far + [sibling]:
        pl.semaphore_signal(barrier, inc=1, device_id=(peer, col), device_id_type=mesh_ids)
    pl.semaphore_wait(barrier, n_chip)
    local = pltpu.make_async_copy(x_ref, o_ref.at[me], local_sem)
    local.start()
    pair = pltpu.make_async_remote_copy(
        src_ref=x_ref, dst_ref=o_ref.at[me], send_sem=send_pair, recv_sem=recv_pair,
        device_id=(sibling, col), device_id_type=mesh_ids,
    )
    pair.start()
    outgoing = []
    for k in range(1, n_chip):
        copy = pltpu.make_async_remote_copy(
            src_ref=x_ref, dst_ref=o_ref.at[me], send_sem=send_far.at[k], recv_sem=recv_far.at[k],
            device_id=(far[k - 1], col), device_id_type=mesh_ids,
        )
        copy.start()
        outgoing.append(copy)
    forwards = []
    for k in range(1, n_chip):
        outgoing[k - 1].wait_recv()
        source = lax.rem(chip + n_chip - k, n_chip) * 2 + core
        forward = pltpu.make_async_remote_copy(
            src_ref=o_ref.at[source], dst_ref=o_ref.at[source], send_sem=send_fwd.at[k],
            recv_sem=recv_fwd.at[k], device_id=(sibling, col), device_id_type=mesh_ids,
        )
        forward.start()
        forwards.append(forward)
    local.wait()
    pair.wait()
    for copy in outgoing:
        copy.wait_send()
    for forward in forwards:
        forward.wait()


def row_gather(x, n_row):
    n_chip = n_row // 2
    return pl.pallas_call(
        functools.partial(_row_gather_kernel, n_row=n_row),
        out_shape=jax.ShapeDtypeStruct((n_row,) + x.shape, x.dtype),
        in_specs=[pl.BlockSpec(memory_space=pl.ANY)],
        out_specs=pl.BlockSpec(memory_space=pl.ANY),
        scratch_shapes=[
            pltpu.SemaphoreType.DMA((n_chip,)),
            pltpu.SemaphoreType.DMA((n_chip,)),
            pltpu.SemaphoreType.DMA,
            pltpu.SemaphoreType.DMA,
            pltpu.SemaphoreType.DMA((n_chip,)),
            pltpu.SemaphoreType.DMA((n_chip,)),
            pltpu.SemaphoreType.DMA,
        ],
        compiler_params=pltpu.CompilerParams(collective_id=0, has_side_effects=True),
    )(x)


def _col_gather_kernel(x_ref, o_ref, send_sems, recv_sems, local_sem, *, n_col):
    mesh_ids = pl.DeviceIdType.MESH
    me = lax.axis_index("col")
    row = lax.axis_index("row")
    barrier = pltpu.get_barrier_semaphore()
    for k in range(1, n_col):
        peer = lax.rem(me + k, n_col)
        pl.semaphore_signal(barrier, inc=1, device_id=(row, peer), device_id_type=mesh_ids)
    pl.semaphore_wait(barrier, n_col - 1)
    local = pltpu.make_async_copy(x_ref, o_ref.at[me], local_sem)
    local.start()
    copies = []
    for k in range(1, n_col):
        peer = lax.rem(me + k, n_col)
        copy = pltpu.make_async_remote_copy(
            src_ref=x_ref, dst_ref=o_ref.at[me], send_sem=send_sems.at[k], recv_sem=recv_sems.at[k],
            device_id=(row, peer), device_id_type=mesh_ids,
        )
        copy.start()
        copies.append(copy)
    local.wait()
    for copy in copies:
        copy.wait()


def col_gather(x, n_col):
    return pl.pallas_call(
        functools.partial(_col_gather_kernel, n_col=n_col),
        out_shape=jax.ShapeDtypeStruct((n_col,) + x.shape, x.dtype),
        in_specs=[pl.BlockSpec(memory_space=pl.ANY)],
        out_specs=pl.BlockSpec(memory_space=pl.ANY),
        scratch_shapes=[
            pltpu.SemaphoreType.DMA((n_col,)),
            pltpu.SemaphoreType.DMA((n_col,)),
            pltpu.SemaphoreType.DMA,
        ],
        compiler_params=pltpu.CompilerParams(collective_id=1, has_side_effects=True),
    )(x)


def block_tables(q_seg, k_seg, q_start):
    n_q = q_seg.shape[0] // Q_BLOCK
    n_k = k_seg.shape[0] // K_BLOCK
    values = jnp.arange(-1, 2, dtype=jnp.int32)
    q_has = jnp.any(q_seg.reshape(n_q, Q_BLOCK, 1) == values, axis=1).astype(jnp.float32)
    k_has = jnp.any(k_seg.reshape(n_k, K_BLOCK, 1) == values, axis=1).astype(jnp.float32)
    shared = jnp.dot(q_has, k_has.T) > 0
    single = (jnp.sum(q_has, axis=1)[:, None] == 1) & (jnp.sum(k_has, axis=1)[None, :] == 1)
    diag = (q_start + jnp.arange(n_q, dtype=jnp.int32) * Q_BLOCK) // K_BLOCK
    order = (diag[:, None] + jnp.arange(n_k, dtype=jnp.int32)[None, :]) % n_k
    need = jnp.take_along_axis(shared, order, axis=1)
    full = jnp.take_along_axis(single, order, axis=1)
    rank = jnp.cumsum(need.astype(jnp.int32), axis=1) - 1
    count = jnp.sum(need.astype(jnp.int32), axis=1)
    pos = jnp.where(need, rank, n_k + jnp.arange(n_k)[None, :])
    perm = jnp.argsort(pos, axis=1)
    kb_sorted = jnp.take_along_axis(order, perm, axis=1)
    full_sorted = jnp.take_along_axis(full, perm, axis=1)
    step = jnp.arange(n_k, dtype=jnp.int32)[None, :]
    live = step < count[:, None]
    last = jnp.take_along_axis(kb_sorted, (count - 1)[:, None], axis=1)
    kb_map = jnp.where(live, kb_sorted, last).astype(jnp.int32)
    flags = jnp.where(live, jnp.where(full_sorted, 2, 1), 0).astype(jnp.int32)
    return kb_map, flags


def attention(q_t, q_seg_f, kv, kb_map, flags, scale, interpret=False):
    n_tok = q_t.shape[0]
    per_peer = kv.shape[3] // K_BLOCK
    n_keys = kv.shape[0] * kv.shape[3]
    n_q = n_tok // Q_BLOCK
    n_k = n_keys // K_BLOCK
    kernel = functools.partial(_attn_kernel, scale=scale, n_steps=n_k)
    grid_spec = pltpu.PrefetchScalarGridSpec(
        num_scalar_prefetch=2,
        grid=(n_q, n_k),
        in_specs=[
            pl.BlockSpec((Q_BLOCK, PADW), lambda i, j, km, fl: (i, 0)),
            pl.BlockSpec((Q_BLOCK, 1), lambda i, j, km, fl: (i, 0)),
            pl.BlockSpec((None, None, PADW, K_BLOCK), lambda i, j, km, fl: (km[i, j] // per_peer, 0, 0, km[i, j] % per_peer)),
            pl.BlockSpec((None, None, PADW, K_BLOCK), lambda i, j, km, fl: (km[i, j] // per_peer, 1, 0, km[i, j] % per_peer)),
        ],
        out_specs=pl.BlockSpec((Q_BLOCK, PADW), lambda i, j, km, fl: (i, 0)),
        scratch_shapes=[
            pltpu.VMEM((Q_BLOCK, 1), jnp.float32),
            pltpu.VMEM((Q_BLOCK, 1), jnp.float32),
            pltpu.VMEM((Q_BLOCK, PADW), jnp.float32),
        ],
    )
    return pl.pallas_call(
        kernel,
        grid_spec=grid_spec,
        out_shape=jax.ShapeDtypeStruct((n_tok, PADW), jnp.bfloat16),
        compiler_params=pltpu.CompilerParams(dimension_semantics=("arbitrary", "arbitrary")),
        interpret=interpret,
    )(kb_map, flags, q_t, q_seg_f, kv, kv)


def on_device(
    n_row,
    hidden,
    gain_in,
    w_query,
    w_pair,
    kv_cache,
    recompute_rows,
    segment_ids,
    w_out,
    gain_merge,
    w_merge,
    requests,
):
    local_width, tok_rows = hidden.shape
    model_width = w_query.shape[1]
    n_col = model_width // local_width
    heads_here = local_width // HD
    score_scale = HD ** (-0.5)
    col_index = lax.axis_index("col")
    gathered_rows = lax.all_gather(hidden, "col", axis=0, tiled=True)
    picked_rows = recompute_rows[0]
    hidden_picked = jnp.take(hidden, picked_rows, axis=1)
    picked_copies = jnp.broadcast_to(hidden_picked[None], (n_col,) + hidden_picked.shape)
    picked_full = lax.all_to_all(picked_copies, "col", 0, 0, tiled=True)
    picked_float = picked_full.reshape(model_width, -1).astype(jnp.float32)
    picked_mean = jnp.sum(picked_float, axis=0, keepdims=True) / model_width
    picked_square = jnp.sum(picked_float * picked_float, axis=0, keepdims=True) / model_width
    normed_picked = (
        (picked_float - picked_mean)
        * lax.rsqrt(picked_square - picked_mean * picked_mean + EPSILON)
        * gain_in.astype(jnp.float32)[:, None]
    ).astype(jnp.bfloat16)
    fresh_pairs = jnp.dot(
        w_pair.reshape(2 * local_width, model_width),
        normed_picked,
        preferred_element_type=jnp.float32,
    )
    fresh_pairs = fresh_pairs.astype(jnp.bfloat16).reshape(2, local_width, -1)
    token_line = jnp.arange(tok_rows, dtype=jnp.int32)
    hit_grid = picked_rows[:, None] == token_line[None, :]
    placed = jnp.dot(
        fresh_pairs.reshape(2 * local_width, -1),
        hit_grid.astype(jnp.bfloat16),
        preferred_element_type=jnp.float32,
    ).astype(jnp.bfloat16)
    is_fresh = jnp.any(hit_grid, axis=0)
    keys_values = jnp.where(is_fresh[None, None, :], placed.reshape(2, local_width, tok_rows), kv_cache)

    pair_local = jnp.pad(keys_values, ((0, 0), (0, PADW - HD), (0, 0)))
    pair_local = pair_local.at[0, HD].set(segment_ids.astype(jnp.bfloat16))
    pair_all = row_gather(pair_local, n_row)
    full_rows, pair_all = lax.optimization_barrier((gathered_rows, pair_all))
    full_float = full_rows.astype(jnp.float32)
    in_mean = jnp.sum(full_float, axis=0, keepdims=True) / model_width
    in_square = jnp.sum(full_float * full_float, axis=0, keepdims=True) / model_width
    normed = (
        (full_float - in_mean)
        * lax.rsqrt(in_square - in_mean * in_mean + EPSILON)
        * gain_in.astype(jnp.float32)[:, None]
    ).astype(jnp.bfloat16)
    query_rows = lax.dot_general(
        normed, w_query, (((0,), (1,)), ((), ())), preferred_element_type=jnp.float32
    ).astype(jnp.bfloat16)
    query_rows = jnp.pad(query_rows, ((0, 0), (0, PADW - HD)))
    segment_line = pair_all[:, 0, HD].reshape(-1).astype(jnp.int32)
    half = -(-model_width // 256) * 128
    core = lax.axis_index("row") % 2
    weight_stack = jnp.concatenate([w_out[None], w_merge], axis=0)
    weight_stack = jnp.pad(weight_stack, ((0, 0), (0, 0), (0, 2 * half - model_width)))
    weight_half = lax.dynamic_slice_in_dim(weight_stack, core * half, half, 2)
    weight_half, _ = lax.optimization_barrier((weight_half, picked_full))
    weights_mine = lax.all_gather(weight_half, "col", axis=1, tiled=True)

    def in_order(mine, other, axis):
        return jnp.where(
            core == 0,
            jnp.concatenate([mine, other], axis=axis),
            jnp.concatenate([other, mine], axis=axis),
        )
    kb_map, flags = block_tables(segment_ids, segment_line, lax.axis_index("row") * tok_rows)
    attended_rows = attention(
        query_rows, segment_ids.astype(jnp.float32)[:, None], pair_all, kb_map, flags, score_scale
    )
    attended = attended_rows[:, :HD].T
    weights_mine, _ = lax.optimization_barrier((weights_mine, attended_rows))
    weights_other = lax.ppermute(weights_mine, "row", [(i, i ^ 1) for i in range(n_row)])
    chunk = tok_rows // n_col
    attended_chunk = lax.all_to_all(attended, "col", 1, 0, tiled=True)
    x_chunk = lax.dynamic_slice_in_dim(full_rows, col_index * chunk, chunk, 1).astype(jnp.float32)
    projected = in_order(
        *[
            lax.dot_general(
                part[0], attended_chunk, (((0,), (0,)), ((), ())), preferred_element_type=jnp.float32
            )
            for part in (weights_mine, weights_other)
        ],
        0,
    )[:model_width]
    updated = x_chunk + projected
    row_mean = jnp.sum(updated, axis=0, keepdims=True) / model_width
    row_square = jnp.sum(updated * updated, axis=0, keepdims=True) / model_width
    merger_chunk = (
        (updated - row_mean)
        * lax.rsqrt(row_square - row_mean * row_mean + EPSILON)
        * gain_merge.astype(jnp.float32)[:, None]
    ).astype(jnp.bfloat16)
    grouped = merger_chunk.reshape(model_width, chunk // 4, 4)
    merged_here = in_order(
        *[
            jnp.einsum("fgi,ifd->gd", grouped, part[1:], preferred_element_type=jnp.float32)
            for part in (weights_mine, weights_other)
        ],
        1,
    )[:, :model_width]
    merged_all = col_gather(merged_here.astype(jnp.bfloat16), n_col).reshape(-1, model_width)
    wanted_rows = lax.dynamic_index_in_dim(requests[0], col_index, 0, keepdims=False)
    is_valid = wanted_rows >= 0
    safe_index = jnp.where(is_valid, wanted_rows, 0)
    picked = jnp.where(is_valid[:, None], merged_all[safe_index], jnp.zeros((), jnp.bfloat16))
    return picked.reshape(1, 1, picked.shape[0], model_width)


def solution(mesh):
    placed = (
        P("col", "row"),
        P(),
        P("col", None),
        P(None, "col", None),
        P(None, "col", "row"),
        P("row", None),
        P("row"),
        P("col", None),
        P(),
        P(None, "col", None),
        P("row", None, None),
    )
    return jax.shard_map(
        functools.partial(on_device, mesh.shape["row"]),
        mesh=mesh,
        in_specs=placed,
        out_specs=P("row", "col", None, None),
        check_vma=False,
    )
```

```python
import jax
import jax.numpy as jnp
from jax import lax
import functools
from jax.experimental import pallas as pl
from jax.experimental.pallas import tpu as pltpu
from jax.sharding import PartitionSpec as P

HD = 88


EPSILON = 1e-06
MASKED = -1e30
PADW = 96
Q_BLOCK = 2048
K_BLOCK = 2048


def _attn_kernel(kb_map, flags, q_ref, qs_ref, k_ref, v_ref, o_ref, m_ref, l_ref, acc_ref, *, scale, n_steps):
    qb = pl.program_id(0)
    j = pl.program_id(1)
    flag = flags[qb, j]

    @pl.when(j == 0)
    def _():
        m_ref[...] = jnp.full(m_ref.shape, MASKED, jnp.float32)
        l_ref[...] = jnp.zeros(l_ref.shape, jnp.float32)
        acc_ref[...] = jnp.zeros(acc_ref.shape, jnp.float32)

    def step(masked):
        q = q_ref[...]
        k = k_ref[...]
        s = jnp.dot(q, k, preferred_element_type=jnp.float32) * scale
        if masked:
            key_seg = k[HD:HD + 1, :].astype(jnp.float32)
            s = jnp.where(qs_ref[...] == key_seg, s, MASKED)
        m_prev = m_ref[...]
        m_new = jnp.maximum(m_prev, jnp.max(s, axis=1, keepdims=True))
        p = jnp.exp(s - m_new)
        alpha = jnp.exp(m_prev - m_new)
        l_ref[...] = alpha * l_ref[...] + jnp.sum(p, axis=1, keepdims=True)
        pv = lax.dot_general(
            p.astype(jnp.bfloat16), v_ref[...], (((1,), (1,)), ((), ())),
            preferred_element_type=jnp.float32,
        )
        acc_ref[...] = alpha * acc_ref[...] + pv
        m_ref[...] = m_new

    @pl.when(flag == 1)
    def _():
        step(True)

    @pl.when(flag == 2)
    def _():
        step(False)

    @pl.when(j == n_steps - 1)
    def _():
        o_ref[...] = (acc_ref[...] / l_ref[...]).astype(o_ref.dtype)


def _row_gather_kernel(x_ref, o_ref, send_far, recv_far, send_pair, recv_pair, send_fwd, recv_fwd, local_sem, *, n_row):
    mesh_ids = pl.DeviceIdType.MESH
    n_chip = n_row // 2
    me = lax.axis_index("row")
    col = lax.axis_index("col")
    chip = me // 2
    core = me % 2
    sibling = chip * 2 + 1 - core
    far = [lax.rem(chip + k, n_chip) * 2 + core for k in range(1, n_chip)]
    barrier = pltpu.get_barrier_semaphore()
    for peer in far + [sibling]:
        pl.semaphore_signal(barrier, inc=1, device_id=(peer, col), device_id_type=mesh_ids)
    pl.semaphore_wait(barrier, n_chip)
    local = pltpu.make_async_copy(x_ref, o_ref.at[me], local_sem)
    local.start()
    pair = pltpu.make_async_remote_copy(
        src_ref=x_ref, dst_ref=o_ref.at[me], send_sem=send_pair, recv_sem=recv_pair,
        device_id=(sibling, col), device_id_type=mesh_ids,
    )
    pair.start()
    outgoing = []
    for k in range(1, n_chip):
        copy = pltpu.make_async_remote_copy(
            src_ref=x_ref, dst_ref=o_ref.at[me], send_sem=send_far.at[k], recv_sem=recv_far.at[k],
            device_id=(far[k - 1], col), device_id_type=mesh_ids,
        )
        copy.start()
        outgoing.append(copy)
    forwards = []
    for k in range(1, n_chip):
        outgoing[k - 1].wait_recv()
        source = lax.rem(chip + n_chip - k, n_chip) * 2 + core
        forward = pltpu.make_async_remote_copy(
            src_ref=o_ref.at[source], dst_ref=o_ref.at[source], send_sem=send_fwd.at[k],
            recv_sem=recv_fwd.at[k], device_id=(sibling, col), device_id_type=mesh_ids,
        )
        forward.start()
        forwards.append(forward)
    local.wait()
    pair.wait()
    for copy in outgoing:
        copy.wait_send()
    for forward in forwards:
        forward.wait()


def row_gather(x, n_row):
    n_chip = n_row // 2
    return pl.pallas_call(
        functools.partial(_row_gather_kernel, n_row=n_row),
        out_shape=jax.ShapeDtypeStruct((n_row,) + x.shape, x.dtype),
        in_specs=[pl.BlockSpec(memory_space=pl.ANY)],
        out_specs=pl.BlockSpec(memory_space=pl.ANY),
        scratch_shapes=[
            pltpu.SemaphoreType.DMA((n_chip,)),
            pltpu.SemaphoreType.DMA((n_chip,)),
            pltpu.SemaphoreType.DMA,
            pltpu.SemaphoreType.DMA,
            pltpu.SemaphoreType.DMA((n_chip,)),
            pltpu.SemaphoreType.DMA((n_chip,)),
            pltpu.SemaphoreType.DMA,
        ],
        compiler_params=pltpu.CompilerParams(collective_id=0, has_side_effects=True),
    )(x)


def _col_gather_kernel(x_ref, o_ref, send_sems, recv_sems, local_sem, *, n_col):
    mesh_ids = pl.DeviceIdType.MESH
    me = lax.axis_index("col")
    row = lax.axis_index("row")
    barrier = pltpu.get_barrier_semaphore()
    for k in range(1, n_col):
        peer = lax.rem(me + k, n_col)
        pl.semaphore_signal(barrier, inc=1, device_id=(row, peer), device_id_type=mesh_ids)
    pl.semaphore_wait(barrier, n_col - 1)
    local = pltpu.make_async_copy(x_ref, o_ref.at[me], local_sem)
    local.start()
    copies = []
    for k in range(1, n_col):
        peer = lax.rem(me + k, n_col)
        copy = pltpu.make_async_remote_copy(
            src_ref=x_ref, dst_ref=o_ref.at[me], send_sem=send_sems.at[k], recv_sem=recv_sems.at[k],
            device_id=(row, peer), device_id_type=mesh_ids,
        )
        copy.start()
        copies.append(copy)
    local.wait()
    for copy in copies:
        copy.wait()


def col_gather(x, n_col):
    return pl.pallas_call(
        functools.partial(_col_gather_kernel, n_col=n_col),
        out_shape=jax.ShapeDtypeStruct((n_col,) + x.shape, x.dtype),
        in_specs=[pl.BlockSpec(memory_space=pl.ANY)],
        out_specs=pl.BlockSpec(memory_space=pl.ANY),
        scratch_shapes=[
            pltpu.SemaphoreType.DMA((n_col,)),
            pltpu.SemaphoreType.DMA((n_col,)),
            pltpu.SemaphoreType.DMA,
        ],
        compiler_params=pltpu.CompilerParams(collective_id=1, has_side_effects=True),
    )(x)


def block_tables(q_seg, k_seg, q_start):
    n_q = q_seg.shape[0] // Q_BLOCK
    n_k = k_seg.shape[0] // K_BLOCK
    values = jnp.arange(-1, 2, dtype=jnp.int32)
    q_has = jnp.any(q_seg.reshape(n_q, Q_BLOCK, 1) == values, axis=1).astype(jnp.float32)
    k_has = jnp.any(k_seg.reshape(n_k, K_BLOCK, 1) == values, axis=1).astype(jnp.float32)
    shared = jnp.dot(q_has, k_has.T) > 0
    single = (jnp.sum(q_has, axis=1)[:, None] == 1) & (jnp.sum(k_has, axis=1)[None, :] == 1)
    diag = (q_start + jnp.arange(n_q, dtype=jnp.int32) * Q_BLOCK) // K_BLOCK
    order = (diag[:, None] + jnp.arange(n_k, dtype=jnp.int32)[None, :]) % n_k
    need = jnp.take_along_axis(shared, order, axis=1)
    full = jnp.take_along_axis(single, order, axis=1)
    rank = jnp.cumsum(need.astype(jnp.int32), axis=1) - 1
    count = jnp.sum(need.astype(jnp.int32), axis=1)
    pos = jnp.where(need, rank, n_k + jnp.arange(n_k)[None, :])
    perm = jnp.argsort(pos, axis=1)
    kb_sorted = jnp.take_along_axis(order, perm, axis=1)
    full_sorted = jnp.take_along_axis(full, perm, axis=1)
    step = jnp.arange(n_k, dtype=jnp.int32)[None, :]
    live = step < count[:, None]
    last = jnp.take_along_axis(kb_sorted, (count - 1)[:, None], axis=1)
    kb_map = jnp.where(live, kb_sorted, last).astype(jnp.int32)
    flags = jnp.where(live, jnp.where(full_sorted, 2, 1), 0).astype(jnp.int32)
    return kb_map, flags


def attention(q_t, q_seg_f, kv, kb_map, flags, scale, interpret=False):
    n_tok = q_t.shape[0]
    per_peer = kv.shape[3] // K_BLOCK
    n_keys = kv.shape[0] * kv.shape[3]
    n_q = n_tok // Q_BLOCK
    n_k = n_keys // K_BLOCK
    kernel = functools.partial(_attn_kernel, scale=scale, n_steps=n_k)
    grid_spec = pltpu.PrefetchScalarGridSpec(
        num_scalar_prefetch=2,
        grid=(n_q, n_k),
        in_specs=[
            pl.BlockSpec((Q_BLOCK, PADW), lambda i, j, km, fl: (i, 0)),
            pl.BlockSpec((Q_BLOCK, 1), lambda i, j, km, fl: (i, 0)),
            pl.BlockSpec((None, None, PADW, K_BLOCK), lambda i, j, km, fl: (km[i, j] // per_peer, 0, 0, km[i, j] % per_peer)),
            pl.BlockSpec((None, None, PADW, K_BLOCK), lambda i, j, km, fl: (km[i, j] // per_peer, 1, 0, km[i, j] % per_peer)),
        ],
        out_specs=pl.BlockSpec((Q_BLOCK, PADW), lambda i, j, km, fl: (i, 0)),
        scratch_shapes=[
            pltpu.VMEM((Q_BLOCK, 1), jnp.float32),
            pltpu.VMEM((Q_BLOCK, 1), jnp.float32),
            pltpu.VMEM((Q_BLOCK, PADW), jnp.float32),
        ],
    )
    return pl.pallas_call(
        kernel,
        grid_spec=grid_spec,
        out_shape=jax.ShapeDtypeStruct((n_tok, PADW), jnp.bfloat16),
        compiler_params=pltpu.CompilerParams(dimension_semantics=("arbitrary", "arbitrary")),
        interpret=interpret,
    )(kb_map, flags, q_t, q_seg_f, kv, kv)


def on_device(
    n_row,
    hidden,
    gain_in,
    w_query,
    w_pair,
    kv_cache,
    recompute_rows,
    segment_ids,
    w_out,
    gain_merge,
    w_merge,
    requests,
):
    local_width, tok_rows = hidden.shape
    model_width = w_query.shape[1]
    n_col = model_width // local_width
    heads_here = local_width // HD
    score_scale = HD ** (-0.5)
    col_index = lax.axis_index("col")
    gathered_rows = lax.all_gather(hidden, "col", axis=0, tiled=True)
    picked_rows = recompute_rows[0]
    hidden_picked = jnp.take(hidden, picked_rows, axis=1)
    picked_copies = jnp.broadcast_to(hidden_picked[None], (n_col,) + hidden_picked.shape)
    picked_full = lax.all_to_all(picked_copies, "col", 0, 0, tiled=True)
    picked_float = picked_full.reshape(model_width, -1).astype(jnp.float32)
    picked_mean = jnp.sum(picked_float, axis=0, keepdims=True) / model_width
    picked_square = jnp.sum(picked_float * picked_float, axis=0, keepdims=True) / model_width
    normed_picked = (
        (picked_float - picked_mean)
        * lax.rsqrt(picked_square - picked_mean * picked_mean + EPSILON)
        * gain_in.astype(jnp.float32)[:, None]
    ).astype(jnp.bfloat16)
    fresh_pairs = jnp.dot(
        w_pair.reshape(2 * local_width, model_width),
        normed_picked,
        preferred_element_type=jnp.float32,
    )
    fresh_pairs = fresh_pairs.astype(jnp.bfloat16).reshape(2, local_width, -1)
    keys_values = kv_cache.at[:, :, picked_rows].set(fresh_pairs)

    pair_local = jnp.pad(keys_values, ((0, 0), (0, PADW - HD), (0, 0)))
    pair_local = pair_local.at[0, HD].set(segment_ids.astype(jnp.bfloat16))
    pair_all = row_gather(pair_local, n_row)
    full_rows, pair_all = lax.optimization_barrier((gathered_rows, pair_all))
    full_float = full_rows.astype(jnp.float32)
    in_mean = jnp.sum(full_float, axis=0, keepdims=True) / model_width
    in_square = jnp.sum(full_float * full_float, axis=0, keepdims=True) / model_width
    normed = (
        (full_float - in_mean)
        * lax.rsqrt(in_square - in_mean * in_mean + EPSILON)
        * gain_in.astype(jnp.float32)[:, None]
    ).astype(jnp.bfloat16)
    query_rows = lax.dot_general(
        normed, w_query, (((0,), (1,)), ((), ())), preferred_element_type=jnp.float32
    ).astype(jnp.bfloat16)
    query_rows = jnp.pad(query_rows, ((0, 0), (0, PADW - HD)))
    segment_line = pair_all[:, 0, HD].reshape(-1).astype(jnp.int32)
    half = -(-model_width // 256) * 128
    core = lax.axis_index("row") % 2
    weight_stack = jnp.concatenate([w_out[None], w_merge], axis=0)
    weight_stack = jnp.pad(weight_stack, ((0, 0), (0, 0), (0, 2 * half - model_width)))
    weight_half = lax.dynamic_slice_in_dim(weight_stack, core * half, half, 2)
    weight_half, _ = lax.optimization_barrier((weight_half, picked_full))
    weights_mine = lax.all_gather(weight_half, "col", axis=1, tiled=True)

    def in_order(mine, other, axis):
        return jnp.where(
            core == 0,
            jnp.concatenate([mine, other], axis=axis),
            jnp.concatenate([other, mine], axis=axis),
        )
    kb_map, flags = block_tables(segment_ids, segment_line, lax.axis_index("row") * tok_rows)
    attended_rows = attention(
        query_rows, segment_ids.astype(jnp.float32)[:, None], pair_all, kb_map, flags, score_scale
    )
    attended = attended_rows[:, :HD].T
    weights_mine, _ = lax.optimization_barrier((weights_mine, attended_rows))
    weights_other = lax.ppermute(weights_mine, "row", [(i, i ^ 1) for i in range(n_row)])
    chunk = tok_rows // n_col
    attended_chunk = lax.all_to_all(attended, "col", 1, 0, tiled=True)
    x_chunk = lax.dynamic_slice_in_dim(full_rows, col_index * chunk, chunk, 1).astype(jnp.float32)
    projected = in_order(
        *[
            lax.dot_general(
                part[0], attended_chunk, (((0,), (0,)), ((), ())), preferred_element_type=jnp.float32
            )
            for part in (weights_mine, weights_other)
        ],
        0,
    )[:model_width]
    updated = x_chunk + projected
    row_mean = jnp.sum(updated, axis=0, keepdims=True) / model_width
    row_square = jnp.sum(updated * updated, axis=0, keepdims=True) / model_width
    merger_chunk = (
        (updated - row_mean)
        * lax.rsqrt(row_square - row_mean * row_mean + EPSILON)
        * gain_merge.astype(jnp.float32)[:, None]
    ).astype(jnp.bfloat16)
    grouped = merger_chunk.reshape(model_width, chunk // 4, 4)
    merged_here = in_order(
        *[
            jnp.einsum("fgi,ifd->gd", grouped, part[1:], preferred_element_type=jnp.float32)
            for part in (weights_mine, weights_other)
        ],
        1,
    )[:, :model_width]
    merged_all = col_gather(merged_here.astype(jnp.bfloat16), n_col).reshape(-1, model_width)
    wanted_rows = lax.dynamic_index_in_dim(requests[0], col_index, 0, keepdims=False)
    is_valid = wanted_rows >= 0
    safe_index = jnp.where(is_valid, wanted_rows, 0)
    picked = jnp.where(is_valid[:, None], merged_all[safe_index], jnp.zeros((), jnp.bfloat16))
    return picked.reshape(1, 1, picked.shape[0], model_width)


def solution(mesh):
    placed = (
        P("col", "row"),
        P(),
        P("col", None),
        P(None, "col", None),
        P(None, "col", "row"),
        P("row", None),
        P("row"),
        P("col", None),
        P(),
        P(None, "col", None),
        P("row", None, None),
    )
    return jax.shard_map(
        functools.partial(on_device, mesh.shape["row"]),
        mesh=mesh,
        in_specs=placed,
        out_specs=P("row", "col", None, None),
        check_vma=False,
    )
```

```python
import jax
import jax.numpy as jnp
from jax import lax
import functools
from jax.experimental import pallas as pl
from jax.experimental.pallas import tpu as pltpu
from jax.sharding import PartitionSpec as P

HD = 88


EPSILON = 1e-06
MASKED = -1e30
PADW = 96
Q_BLOCK = 512
K_BLOCK = 2048


def _attn_kernel(kb_map, flags, q_ref, qs_ref, k_ref, v_ref, o_ref, m_ref, l_ref, acc_ref, *, scale, n_steps):
    qb = pl.program_id(0)
    j = pl.program_id(1)
    flag = flags[qb, j]

    @pl.when(j == 0)
    def _():
        m_ref[...] = jnp.full(m_ref.shape, MASKED, jnp.float32)
        l_ref[...] = jnp.zeros(l_ref.shape, jnp.float32)
        acc_ref[...] = jnp.zeros(acc_ref.shape, jnp.float32)

    def step(masked):
        q = q_ref[...]
        k = k_ref[...]
        s = jnp.dot(q, k, preferred_element_type=jnp.float32) * scale
        if masked:
            key_seg = k[HD:HD + 1, :].astype(jnp.float32)
            s = jnp.where(qs_ref[...] == key_seg, s, MASKED)
        m_prev = m_ref[...]
        m_new = jnp.maximum(m_prev, jnp.max(s, axis=1, keepdims=True))
        p = jnp.exp(s - m_new)
        alpha = jnp.exp(m_prev - m_new)
        l_ref[...] = alpha * l_ref[...] + jnp.sum(p, axis=1, keepdims=True)
        pv = lax.dot_general(
            p.astype(jnp.bfloat16), v_ref[...], (((1,), (1,)), ((), ())),
            preferred_element_type=jnp.float32,
        )
        acc_ref[...] = alpha * acc_ref[...] + pv
        m_ref[...] = m_new

    @pl.when(flag == 1)
    def _():
        step(True)

    @pl.when(flag == 2)
    def _():
        step(False)

    @pl.when(j == n_steps - 1)
    def _():
        o_ref[...] = (acc_ref[...] / l_ref[...]).astype(o_ref.dtype)


def _row_gather_kernel(x_ref, o_ref, send_far, recv_far, send_pair, recv_pair, send_fwd, recv_fwd, local_sem, *, n_row):
    mesh_ids = pl.DeviceIdType.MESH
    n_chip = n_row // 2
    me = lax.axis_index("row")
    col = lax.axis_index("col")
    chip = me // 2
    core = me % 2
    sibling = chip * 2 + 1 - core
    far = [lax.rem(chip + k, n_chip) * 2 + core for k in range(1, n_chip)]
    barrier = pltpu.get_barrier_semaphore()
    for peer in far + [sibling]:
        pl.semaphore_signal(barrier, inc=1, device_id=(peer, col), device_id_type=mesh_ids)
    pl.semaphore_wait(barrier, n_chip)
    local = pltpu.make_async_copy(x_ref, o_ref.at[me], local_sem)
    local.start()
    pair = pltpu.make_async_remote_copy(
        src_ref=x_ref, dst_ref=o_ref.at[me], send_sem=send_pair, recv_sem=recv_pair,
        device_id=(sibling, col), device_id_type=mesh_ids,
    )
    pair.start()
    outgoing = []
    for k in range(1, n_chip):
        copy = pltpu.make_async_remote_copy(
            src_ref=x_ref, dst_ref=o_ref.at[me], send_sem=send_far.at[k], recv_sem=recv_far.at[k],
            device_id=(far[k - 1], col), device_id_type=mesh_ids,
        )
        copy.start()
        outgoing.append(copy)
    forwards = []
    for k in range(1, n_chip):
        outgoing[k - 1].wait_recv()
        source = lax.rem(chip + n_chip - k, n_chip) * 2 + core
        forward = pltpu.make_async_remote_copy(
            src_ref=o_ref.at[source], dst_ref=o_ref.at[source], send_sem=send_fwd.at[k],
            recv_sem=recv_fwd.at[k], device_id=(sibling, col), device_id_type=mesh_ids,
        )
        forward.start()
        forwards.append(forward)
    local.wait()
    pair.wait()
    for copy in outgoing:
        copy.wait_send()
    for forward in forwards:
        forward.wait()


def row_gather(x, n_row):
    n_chip = n_row // 2
    return pl.pallas_call(
        functools.partial(_row_gather_kernel, n_row=n_row),
        out_shape=jax.ShapeDtypeStruct((n_row,) + x.shape, x.dtype),
        in_specs=[pl.BlockSpec(memory_space=pl.ANY)],
        out_specs=pl.BlockSpec(memory_space=pl.ANY),
        scratch_shapes=[
            pltpu.SemaphoreType.DMA((n_chip,)),
            pltpu.SemaphoreType.DMA((n_chip,)),
            pltpu.SemaphoreType.DMA,
            pltpu.SemaphoreType.DMA,
            pltpu.SemaphoreType.DMA((n_chip,)),
            pltpu.SemaphoreType.DMA((n_chip,)),
            pltpu.SemaphoreType.DMA,
        ],
        compiler_params=pltpu.CompilerParams(collective_id=0, has_side_effects=True),
    )(x)


def _col_gather_kernel(x_ref, o_ref, send_sems, recv_sems, local_sem, *, n_col):
    mesh_ids = pl.DeviceIdType.MESH
    me = lax.axis_index("col")
    row = lax.axis_index("row")
    barrier = pltpu.get_barrier_semaphore()
    for k in range(1, n_col):
        peer = lax.rem(me + k, n_col)
        pl.semaphore_signal(barrier, inc=1, device_id=(row, peer), device_id_type=mesh_ids)
    pl.semaphore_wait(barrier, n_col - 1)
    local = pltpu.make_async_copy(x_ref, o_ref.at[me], local_sem)
    local.start()
    copies = []
    for k in range(1, n_col):
        peer = lax.rem(me + k, n_col)
        copy = pltpu.make_async_remote_copy(
            src_ref=x_ref, dst_ref=o_ref.at[me], send_sem=send_sems.at[k], recv_sem=recv_sems.at[k],
            device_id=(row, peer), device_id_type=mesh_ids,
        )
        copy.start()
        copies.append(copy)
    local.wait()
    for copy in copies:
        copy.wait()


def col_gather(x, n_col):
    return pl.pallas_call(
        functools.partial(_col_gather_kernel, n_col=n_col),
        out_shape=jax.ShapeDtypeStruct((n_col,) + x.shape, x.dtype),
        in_specs=[pl.BlockSpec(memory_space=pl.ANY)],
        out_specs=pl.BlockSpec(memory_space=pl.ANY),
        scratch_shapes=[
            pltpu.SemaphoreType.DMA((n_col,)),
            pltpu.SemaphoreType.DMA((n_col,)),
            pltpu.SemaphoreType.DMA,
        ],
        compiler_params=pltpu.CompilerParams(collective_id=1, has_side_effects=True),
    )(x)


def block_tables(q_seg, k_seg, q_start):
    n_q = q_seg.shape[0] // Q_BLOCK
    n_k = k_seg.shape[0] // K_BLOCK
    values = jnp.arange(-1, 2, dtype=jnp.int32)
    q_has = jnp.any(q_seg.reshape(n_q, Q_BLOCK, 1) == values, axis=1).astype(jnp.float32)
    k_has = jnp.any(k_seg.reshape(n_k, K_BLOCK, 1) == values, axis=1).astype(jnp.float32)
    shared = jnp.dot(q_has, k_has.T) > 0
    single = (jnp.sum(q_has, axis=1)[:, None] == 1) & (jnp.sum(k_has, axis=1)[None, :] == 1)
    diag = (q_start + jnp.arange(n_q, dtype=jnp.int32) * Q_BLOCK) // K_BLOCK
    order = (diag[:, None] + jnp.arange(n_k, dtype=jnp.int32)[None, :]) % n_k
    need = jnp.take_along_axis(shared, order, axis=1)
    full = jnp.take_along_axis(single, order, axis=1)
    rank = jnp.cumsum(need.astype(jnp.int32), axis=1) - 1
    count = jnp.sum(need.astype(jnp.int32), axis=1)
    pos = jnp.where(need, rank, n_k + jnp.arange(n_k)[None, :])
    perm = jnp.argsort(pos, axis=1)
    kb_sorted = jnp.take_along_axis(order, perm, axis=1)
    full_sorted = jnp.take_along_axis(full, perm, axis=1)
    step = jnp.arange(n_k, dtype=jnp.int32)[None, :]
    live = step < count[:, None]
    last = jnp.take_along_axis(kb_sorted, (count - 1)[:, None], axis=1)
    kb_map = jnp.where(live, kb_sorted, last).astype(jnp.int32)
    flags = jnp.where(live, jnp.where(full_sorted, 2, 1), 0).astype(jnp.int32)
    return kb_map, flags


def attention(q_t, q_seg_f, kv, kb_map, flags, scale, interpret=False):
    n_tok = q_t.shape[0]
    per_peer = kv.shape[3] // K_BLOCK
    n_keys = kv.shape[0] * kv.shape[3]
    n_q = n_tok // Q_BLOCK
    n_k = n_keys // K_BLOCK
    kernel = functools.partial(_attn_kernel, scale=scale, n_steps=n_k)
    grid_spec = pltpu.PrefetchScalarGridSpec(
        num_scalar_prefetch=2,
        grid=(n_q, n_k),
        in_specs=[
            pl.BlockSpec((Q_BLOCK, PADW), lambda i, j, km, fl: (i, 0)),
            pl.BlockSpec((Q_BLOCK, 1), lambda i, j, km, fl: (i, 0)),
            pl.BlockSpec((None, None, PADW, K_BLOCK), lambda i, j, km, fl: (km[i, j] // per_peer, 0, 0, km[i, j] % per_peer)),
            pl.BlockSpec((None, None, PADW, K_BLOCK), lambda i, j, km, fl: (km[i, j] // per_peer, 1, 0, km[i, j] % per_peer)),
        ],
        out_specs=pl.BlockSpec((Q_BLOCK, PADW), lambda i, j, km, fl: (i, 0)),
        scratch_shapes=[
            pltpu.VMEM((Q_BLOCK, 1), jnp.float32),
            pltpu.VMEM((Q_BLOCK, 1), jnp.float32),
            pltpu.VMEM((Q_BLOCK, PADW), jnp.float32),
        ],
    )
    return pl.pallas_call(
        kernel,
        grid_spec=grid_spec,
        out_shape=jax.ShapeDtypeStruct((n_tok, PADW), jnp.bfloat16),
        compiler_params=pltpu.CompilerParams(dimension_semantics=("arbitrary", "arbitrary")),
        interpret=interpret,
    )(kb_map, flags, q_t, q_seg_f, kv, kv)


def on_device(
    n_row,
    hidden,
    gain_in,
    w_query,
    w_pair,
    kv_cache,
    recompute_rows,
    segment_ids,
    w_out,
    gain_merge,
    w_merge,
    requests,
):
    local_width, tok_rows = hidden.shape
    model_width = w_query.shape[1]
    n_col = model_width // local_width
    heads_here = local_width // HD
    score_scale = HD ** (-0.5)
    col_index = lax.axis_index("col")
    gathered_rows = lax.all_gather(hidden, "col", axis=0, tiled=True)
    picked_rows = recompute_rows[0]
    hidden_picked = jnp.take(hidden, picked_rows, axis=1)
    picked_copies = jnp.broadcast_to(hidden_picked[None], (n_col,) + hidden_picked.shape)
    picked_full = lax.all_to_all(picked_copies, "col", 0, 0, tiled=True)
    picked_float = picked_full.reshape(model_width, -1).astype(jnp.float32)
    picked_mean = jnp.sum(picked_float, axis=0, keepdims=True) / model_width
    picked_square = jnp.sum(picked_float * picked_float, axis=0, keepdims=True) / model_width
    normed_picked = (
        (picked_float - picked_mean)
        * lax.rsqrt(picked_square - picked_mean * picked_mean + EPSILON)
        * gain_in.astype(jnp.float32)[:, None]
    ).astype(jnp.bfloat16)
    fresh_pairs = jnp.dot(
        w_pair.reshape(2 * local_width, model_width),
        normed_picked,
        preferred_element_type=jnp.float32,
    )
    fresh_pairs = fresh_pairs.astype(jnp.bfloat16).reshape(2, local_width, -1)
    keys_values = kv_cache.at[:, :, picked_rows].set(fresh_pairs)

    pair_local = jnp.pad(keys_values, ((0, 0), (0, PADW - HD), (0, 0)))
    pair_local = pair_local.at[0, HD].set(segment_ids.astype(jnp.bfloat16))
    pair_all = row_gather(pair_local, n_row)
    full_rows, pair_all = lax.optimization_barrier((gathered_rows, pair_all))
    full_float = full_rows.astype(jnp.float32)
    in_mean = jnp.sum(full_float, axis=0, keepdims=True) / model_width
    in_square = jnp.sum(full_float * full_float, axis=0, keepdims=True) / model_width
    normed = (
        (full_float - in_mean)
        * lax.rsqrt(in_square - in_mean * in_mean + EPSILON)
        * gain_in.astype(jnp.float32)[:, None]
    ).astype(jnp.bfloat16)
    query_rows = lax.dot_general(
        normed, w_query, (((0,), (1,)), ((), ())), preferred_element_type=jnp.float32
    ).astype(jnp.bfloat16)
    query_rows = jnp.pad(query_rows, ((0, 0), (0, PADW - HD)))
    segment_line = pair_all[:, 0, HD].reshape(-1).astype(jnp.int32)
    half = -(-model_width // 256) * 128
    core = lax.axis_index("row") % 2
    weight_stack = jnp.concatenate([w_out[None], w_merge], axis=0)
    weight_stack = jnp.pad(weight_stack, ((0, 0), (0, 0), (0, 2 * half - model_width)))
    weight_half = lax.dynamic_slice_in_dim(weight_stack, core * half, half, 2)
    weight_half, _ = lax.optimization_barrier((weight_half, picked_full))
    weights_mine = lax.all_gather(weight_half, "col", axis=1, tiled=True)

    def in_order(mine, other, axis):
        return jnp.where(
            core == 0,
            jnp.concatenate([mine, other], axis=axis),
            jnp.concatenate([other, mine], axis=axis),
        )
    kb_map, flags = block_tables(segment_ids, segment_line, lax.axis_index("row") * tok_rows)
    attended_rows = attention(
        query_rows, segment_ids.astype(jnp.float32)[:, None], pair_all, kb_map, flags, score_scale
    )
    attended = attended_rows[:, :HD].T
    weights_mine, _ = lax.optimization_barrier((weights_mine, attended_rows))
    weights_other = lax.ppermute(weights_mine, "row", [(i, i ^ 1) for i in range(n_row)])
    chunk = tok_rows // n_col
    attended_chunk = lax.all_to_all(attended, "col", 1, 0, tiled=True)
    x_chunk = lax.dynamic_slice_in_dim(full_rows, col_index * chunk, chunk, 1).astype(jnp.float32)
    projected = in_order(
        *[
            lax.dot_general(
                part[0], attended_chunk, (((0,), (0,)), ((), ())), preferred_element_type=jnp.float32
            )
            for part in (weights_mine, weights_other)
        ],
        0,
    )[:model_width]
    updated = x_chunk + projected
    row_mean = jnp.sum(updated, axis=0, keepdims=True) / model_width
    row_square = jnp.sum(updated * updated, axis=0, keepdims=True) / model_width
    merger_chunk = (
        (updated - row_mean)
        * lax.rsqrt(row_square - row_mean * row_mean + EPSILON)
        * gain_merge.astype(jnp.float32)[:, None]
    ).astype(jnp.bfloat16)
    grouped = merger_chunk.reshape(model_width, chunk // 4, 4)
    merged_here = in_order(
        *[
            jnp.einsum("fgi,ifd->gd", grouped, part[1:], preferred_element_type=jnp.float32)
            for part in (weights_mine, weights_other)
        ],
        1,
    )[:, :model_width]
    merged_all = col_gather(merged_here.astype(jnp.bfloat16), n_col).reshape(-1, model_width)
    wanted_rows = lax.dynamic_index_in_dim(requests[0], col_index, 0, keepdims=False)
    is_valid = wanted_rows >= 0
    safe_index = jnp.where(is_valid, wanted_rows, 0)
    picked = jnp.where(is_valid[:, None], merged_all[safe_index], jnp.zeros((), jnp.bfloat16))
    return picked.reshape(1, 1, picked.shape[0], model_width)


def solution(mesh):
    placed = (
        P("col", "row"),
        P(),
        P("col", None),
        P(None, "col", None),
        P(None, "col", "row"),
        P("row", None),
        P("row"),
        P("col", None),
        P(),
        P(None, "col", None),
        P("row", None, None),
    )
    return jax.shard_map(
        functools.partial(on_device, mesh.shape["row"]),
        mesh=mesh,
        in_specs=placed,
        out_specs=P("row", "col", None, None),
        check_vma=False,
    )
```
